256 devices in a mesh: gx: 2 (over z_hi), gy: 16 (over x, y), grp: 8 (over z_lo, core).
Axes of the slice: x: 4, y: 4, z: 8 (z_hi: 2, z_lo: 4; z = z_hi * 4 + z_lo), core: 2. Of those that a mesh axis runs over, the one named last changes fastest.
Arguments:
- field_in: bfloat16 [8, 16, 256, 1024], P('grp', 'gx', 'gy'), may hold values from -6 to 6
- first_weight: bfloat16 [3, 3, 3, 64, 64], replicated, may hold values from -0.15625 to 0.15625
- second_weight: bfloat16 [3, 3, 3, 64, 64], replicated, may hold values from -0.15625 to 0.15625
- cotangent: bfloat16 [8, 16, 256, 1024], P('grp', 'gx', 'gy'), may hold values from -6 to 6
Outputs:
- field_out: bfloat16 [8, 16, 256, 1024], P('grp', 'gx', 'gy')
- first_grad: float32 [3, 3, 3, 64, 64], replicated
- second_grad: float32 [3, 3, 3, 64, 64], replicated
The draws below stay inside these ranges and needn't reach their ends.
All inputs are finite; a program needn't handle non-finite values.
Results may differ from the reference program's by a relative error of at most 0.0095.
Values may be sent and summed in bfloat16 or wider, within the bound.
A program may use at most 64 MiB of HBM per device.

```python
import math
import jax
import jax.numpy as jnp
from jax import lax

C = 64
NZ = 16
S = 8
NX = 16
NY = 256


def level_of(own_key, extent, cuts, smallest, high):
    level, own = 1.0, jax.random.fold_in(own_key, 6)
    for position, shards_of in cuts:
        heights = jnp.exp(jax.random.uniform(jax.random.fold_in(own, position), (shards_of,), jnp.float32, smallest / len(cuts), high / len(cuts)))
        level = level * jnp.repeat(heights, extent[position] // shards_of).reshape([-1 if axis == position else 1 for axis in range(len(extent))])
    return level


def gaussian(own_key, shape, deviation, most, shards=(), dtype=jnp.bfloat16):
    level = level_of(own_key, shape, shards, -0.22, 0.18) if shards else 1.0
    array = jax.random.normal(own_key, shape, jnp.float32) * deviation * level
    return jnp.minimum(jnp.maximum(array, -most), most).astype(dtype)


def setup_inputs(seed: int = 0) -> dict:
    streams_of = jax.random.split(jax.random.key(seed), 5)
    field_in = gaussian(streams_of[0], (S, NX, NY, NZ * C), 1.0, 6.0, ((0, 8), (1, 2), (2, 16)))
    first_weight = gaussian(streams_of[1], (3, 3, 3, C, C), (27 * C) ** -0.5, 0.15625)
    second_weight = gaussian(streams_of[2], (3, 3, 3, C, C), (27 * C) ** -0.5, 0.15625)
    cotangent = gaussian(streams_of[3], (S, NX, NY, NZ * C), 1.0, 6.0, ((0, 8), (1, 2), (2, 16)))
    return {"field_in": field_in, "first_weight": first_weight, "second_weight": second_weight, "cotangent": cotangent}


def conv_full(field, weight):
    return lax.conv_general_dilated(field, weight, (1, 1, 1), ((1, 1), (1, 1), (1, 1)), dimension_numbers=('NHWDC', 'HWDIO', 'NHWDC'), precision=lax.Precision.HIGHEST, preferred_element_type=jnp.float32)

def kernel_grad(field, grad_out):
    result = lax.conv_general_dilated(field, grad_out, (1, 1, 1), ((1, 1), (1, 1), (1, 1)), dimension_numbers=('CHWDN', 'IHWDO', 'NHWDC'), precision=lax.Precision.HIGHEST, preferred_element_type=jnp.float32)
    return jnp.transpose(result, (1, 2, 3, 0, 4))

def reference(field_in, first_weight, second_weight, cotangent):
    first_w = first_weight.astype(jnp.float32)
    second_w = second_weight.astype(jnp.float32)
    flipped = jnp.swapaxes(second_w[::-1, ::-1, ::-1], 3, 4)

    def one_sample(items):
        source, grad_out = items
        source = source.reshape(1, NX, NY, NZ, C).astype(jnp.float32)
        grad_out = grad_out.reshape(1, NX, NY, NZ, C).astype(jnp.float32)
        pre_first = conv_full(source, first_w)
        hidden = jax.nn.silu(pre_first).astype(jnp.bfloat16)
        hidden = lax.optimization_barrier(hidden).astype(jnp.float32)
        output = conv_full(hidden, second_w).astype(jnp.bfloat16)
        second_part = kernel_grad(hidden, grad_out)
        hidden_grad = conv_full(grad_out, flipped)
        sigma = jax.nn.sigmoid(pre_first)
        pre_grad = (hidden_grad * sigma * (1.0 + pre_first * (1.0 - sigma))).astype(jnp.bfloat16)
        pre_grad = lax.optimization_barrier(pre_grad).astype(jnp.float32)
        first_part = kernel_grad(source, pre_grad)
        return (output.reshape(NX, NY, NZ * C), first_part, second_part)
    outputs, first_parts, second_parts = lax.map(one_sample, (field_in, cotangent))
    factor = 1.0 / math.sqrt(S * NX * NY * NZ)
    return (outputs, lax.optimization_barrier(jnp.sum(first_parts, axis=0)) * factor, lax.optimization_barrier(jnp.sum(second_parts, axis=0)) * factor)
```

```python
import functools
import math

import jax
import jax.numpy as jnp
from jax import lax
from jax.experimental import pallas as pl
from jax.experimental.pallas import tpu as pltpu
from jax.sharding import PartitionSpec as P

C = 64
NZ = 16
X = 8
Y = 16
Q = 8
XE = X + 2
YE = Y + 2
ROWS_E = XE * Y
PAIRS = 5
PACKED = PAIRS * 192
CELLS = 2 * X + Y + 2
F32 = jnp.float32
BF16 = jnp.bfloat16
MESH = pl.DeviceIdType.MESH


def low_lanes(rows):
    return lax.broadcasted_iota(jnp.int32, (rows, 128), 1) < 64


def fill_own(ext, x, q, value):
    ext[pl.ds(((x + 1) * YE + 1) * Q + q, Y, stride=Q), :] = value


def edge_cells(ext, sends, gx):
    near = X - (X - 1) * gx
    for y in range(Y):
        start = pl.multiple_of((near * YE + 1 + y) * Q, Q)
        sends[y] = ext[pl.ds(start, Q), :].astype(BF16)
    for x in range(X):
        sends[Y + x] = ext[pl.ds(((x + 1) * YE + 1) * Q, Q), :].astype(BF16)
        sends[Y + X + x] = ext[pl.ds(((x + 1) * YE + Y) * Q, Q), :].astype(BF16)


def halo_copies(sends, lands, send_sems, recv_sem, gx, gy, grp, count):
    up = lax.rem(gy + 1, count)
    down = lax.rem(gy + count - 1, count)
    other = 1 - gx
    moves = (
        (0, Y, 0, other, gy),
        (Y, X, Y + X, gx, down),
        (Y + X, X, Y, gx, up),
        (0, 1, 2 * X + Y + 1, other, down),
        (Y - 1, 1, 2 * X + Y, other, up),
    )
    for number, (source, size, target, to_x, to_y) in enumerate(moves):
        pltpu.make_async_remote_copy(
            src_ref=sends.at[pl.ds(source, size)],
            dst_ref=lands.at[pl.ds(target, size)],
            send_sem=send_sems.at[number],
            recv_sem=recv_sem,
            device_id=(to_x, to_y, grp),
            device_id_type=MESH,
        ).start()


def halo_arrived(lands, send_sems, recv_sem, me):
    pltpu.make_async_remote_copy(
        src_ref=lands, dst_ref=lands, send_sem=send_sems.at[0], recv_sem=recv_sem,
        device_id=me, device_id_type=MESH,
    ).wait_recv()


def halo_sent(sends, send_sems, me):
    for number, (source, size) in enumerate(((0, Y), (Y, X), (Y + X, X), (0, 1), (Y - 1, 1))):
        part = sends.at[pl.ds(source, size)]
        pltpu.make_async_remote_copy(
            src_ref=part, dst_ref=part, send_sem=send_sems.at[number], recv_sem=send_sems.at[number],
            device_id=me, device_id_type=MESH,
        ).wait_send()


def insert_halo(ext, lands, gx, gy, count):
    front = gx == 1
    back = gx == 0
    below = gy > 0
    above = gy < count - 1

    def put(x, y, cell, valid):
        value = lands[cell].astype(F32)
        ext[pl.ds((x * YE + y) * Q, Q), :] = jnp.where(valid, value, jnp.zeros_like(value))

    for y in range(Y):
        put(0, 1 + y, y, front)
        put(XE - 1, 1 + y, y, back)
    for x in range(X):
        put(1 + x, 0, Y + x, below)
        put(1 + x, YE - 1, Y + X + x, above)
    put(0, 0, 2 * X + Y, front & below)
    put(XE - 1, 0, 2 * X + Y, back & below)
    put(0, YE - 1, 2 * X + Y + 1, front & above)
    put(XE - 1, YE - 1, 2 * X + Y + 1, back & above)


def spread(ext, wide):
    low = low_lanes(Y)
    zero = jnp.zeros((Y, 128), F32)

    @pl.loop(0, XE)
    def _(x):
        rows = pl.ds(pl.multiple_of(x * Y, Y), Y)
        for dy in range(3):
            base = (x * YE + dy) * Q
            pairs = [zero] + [ext[pl.ds(base + q, Y, stride=Q), :] for q in range(Q)] + [zero]
            for q in range(Q):
                mixed = jnp.where(low, pairs[q + 2], pairs[q])
                wide[q, rows, dy * 256 : dy * 256 + 128] = pairs[q + 1].astype(BF16)
                wide[q, rows, dy * 256 + 128 : dy * 256 + 256] = mixed.astype(BF16)


TAPS = ((1, 0), (2, 1), (None, 2), (0, None))


def piece(weight, tap):
    return jnp.zeros((C, C), BF16) if tap is None else weight[tap]


def forward_weight(weight, banded):
    for dy in range(3):
        for slot in range(4):
            rows = slice(dy * 256 + slot * C, dy * 256 + slot * C + C)
            for dx in range(3):
                pieces = [
                    piece(weight, None if t is None else (dx * 3 + dy) * 3 + t) for t in TAPS[slot]
                ]
                banded[rows, dx * 128 : dx * 128 + 128] = jnp.concatenate(pieces, axis=1)


def backward_weight(weight, banded):
    for dx in range(3):
        for b in range(2):
            rows = slice(dx * 128 + b * C, dx * 128 + b * C + C)
            for dy in range(3):
                for half in range(2):
                    pieces = []
                    for slot in (2 * half, 2 * half + 1):
                        t = TAPS[slot][b]
                        tap = None if t is None else ((2 - dx) * 3 + 2 - dy) * 3 + 2 - t
                        pieces.append(piece(weight, tap))
                    start = dy * 256 + half * 128
                    banded[rows, start : start + 128] = jnp.concatenate(pieces, axis=1)


def conv_pair(wide, banded, p, flipped):
    dims = (((1,), (1 if flipped else 0,)), ((), ()))
    result = lax.dot_general(wide[p], banded[...], dims, preferred_element_type=F32)
    n = X * Y
    return result[0:n, 0:128] + result[Y : Y + n, 128:256] + result[2 * Y : 2 * Y + n, 256:384]


def kernel_grad(wide, turned, packed, g):
    low = low_lanes(192)
    turned_value = turned[...]

    def moving(tap):
        dx, dy = tap // 3, tap % 3
        block = wide[:, dx * Y : dx * Y + X * Y, dy * 256 : dy * 256 + 128]
        return block.reshape(Q * X * Y, 128)

    for pair in range(PAIRS):
        first = 2 * pair
        if first + 1 < 9:
            rhs = jnp.concatenate([moving(first), moving(first + 1)], axis=1)
        else:
            rhs = moving(first)
        result = jnp.dot(turned_value, rhs, preferred_element_type=F32)
        one = result[:, 0:128]
        two = result[:, 128:256] if first + 1 < 9 else jnp.zeros_like(one)
        straight = jnp.where(low, one[0:192], two[64:256])
        crossed = jnp.where(low, two[0:192], one[64:256])
        total = straight + pltpu.roll(crossed, 64, 1)
        packed[g, pair * 192 : pair * 192 + 192, :] = total.astype(BF16)


def turn(turned, q, block):
    flat = block.astype(F32).T.astype(BF16)
    columns = lambda w: slice(w * 128, w * 128 + 128)
    turned[64:192, columns(q)] = flat
    if q + 1 < Q:
        turned[0:64, columns(q + 1)] = flat[64:128]
    else:
        turned[192:256, columns(q)] = jnp.zeros((64, 128), BF16)
    if q > 0:
        turned[192:256, columns(q - 1)] = flat[0:64]
    else:
        turned[0:64, columns(q)] = jnp.zeros((64, 128), BF16)


def step(
    sizes, factor,
    field, first, second, cotangent,
    output, first_out, second_out,
    ext_f, ext_c, ext_h, wide_f, wide_c, wide_h,
    banded_1, banded_2, banded_t, turned_c, turned_p, pre,
    sends, lands, packed, mate, part, gathered_xy, summed, gathered_z, final, spread_z, full,
    halo_send, halo_recv, mate_send, mate_recv, xy_send, xy_recv, z_send, z_recv,
    back_z_send, back_z_recv, back_xy_send, back_xy_recv, share_send, share_recv,
):
    nx, ny, ng = sizes
    zl = ng // 2
    nz = nx * zl
    chunk = packed.shape[1] // ny
    tile = chunk // nz
    gx, gy, grp = lax.axis_index("gx"), lax.axis_index("gy"), lax.axis_index("grp")
    core = lax.rem(grp, 2)
    z = gx * zl + grp // 2
    me = (gx, gy, grp)
    sibling = (gx, gy, grp + 1 - 2 * core)

    def along_xy(k):
        return lax.rem(gy + k, ny)

    def along_z(k):
        return lax.rem(z + k, nz)

    def z_device(target):
        return (target // zl, gy, 2 * lax.rem(target, zl) + core)

    barrier = pltpu.get_barrier_semaphore()

    def greet(device):
        pl.semaphore_signal(barrier, inc=1, device_id=device, device_id_type=MESH)

    greet((1 - gx, along_xy(1), grp))
    greet((1 - gx, along_xy(ny - 1), grp))
    greet(sibling)

    @pl.loop(1, nz)
    def _(k):
        greet(z_device(along_z(k)))

    @pl.loop(1, ny)
    def _(k):
        greet((gx, along_xy(k), grp))

    fields = ((field, ext_f, 0), (cotangent, ext_c, 1))
    for source, ext, number in fields:
        for x in range(X):
            for q in range(Q):
                fill_own(ext, x, q, source[0, x, :, q * 128 : q * 128 + 128].astype(F32))
        edge_cells(ext, sends.at[number], gx)
    pl.semaphore_wait(barrier, nz - 1 + ny - 1 + 3)
    for number in range(2):
        halo_copies(
            sends.at[number], lands.at[number], halo_send.at[number], halo_recv.at[number], gx, gy, grp, ny
        )

    forward_weight(first, banded_1)
    forward_weight(second, banded_2)
    backward_weight(second, banded_t)
    for q in range(Q):
        turn(turned_c, q, cotangent[0, :, :, q * 128 : q * 128 + 128].reshape(X * Y, 128))

    halo_arrived(lands.at[0], halo_send.at[0], halo_recv.at[0], me)
    insert_halo(ext_f, lands.at[0], gx, gy, ny)
    spread(ext_f, wide_f)

    @pl.loop(0, Q)
    def _(p):
        value = conv_pair(wide_f, banded_1, p, False)
        pre[p] = value
        hidden = (value * jax.nn.sigmoid(value)).astype(BF16).astype(F32)
        for x in range(X):
            fill_own(ext_h, x, p, hidden[x * Y : x * Y + Y])

    edge_cells(ext_h, sends.at[2], gx)
    halo_copies(sends.at[2], lands.at[2], halo_send.at[2], halo_recv.at[2], gx, gy, grp, ny)

    halo_arrived(lands.at[1], halo_send.at[1], halo_recv.at[1], me)
    insert_halo(ext_c, lands.at[1], gx, gy, ny)
    spread(ext_c, wide_c)
    for p in range(Q):
        hidden_grad = conv_pair(wide_c, banded_t, p, True)
        value = pre[p]
        sigma = jax.nn.sigmoid(value)
        turn(turned_p, p, (hidden_grad * sigma * (1.0 + value * (1.0 - sigma))).astype(BF16))
    if packed.shape[1] > PACKED:
        rest = packed.shape[1] - PACKED
        for g in range(2):
            packed[g, PACKED:, :] = jnp.zeros((rest, 128), BF16)
    kernel_grad(wide_f, turned_p, packed, 0)

    halo_arrived(lands.at[2], halo_send.at[2], halo_recv.at[2], me)
    insert_halo(ext_h, lands.at[2], gx, gy, ny)
    spread(ext_h, wide_h)
    kernel_grad(wide_h, turned_c, packed, 1)

    pair_copy = pltpu.make_async_remote_copy(
        src_ref=packed.at[1 - core], dst_ref=mate, send_sem=mate_send, recv_sem=mate_recv,
        device_id=sibling, device_id_type=MESH,
    )
    pair_copy.start()
    pair_copy.wait_recv()
    part[...] = (packed[core].astype(F32) + mate[...].astype(F32)).astype(BF16)

    @pl.loop(1, ny)
    def _(k):
        to = along_xy(k)
        pltpu.make_async_remote_copy(
            src_ref=part.at[pl.ds(pl.multiple_of(to * chunk, 16), chunk)],
            dst_ref=gathered_xy.at[ny - 1 - k],
            send_sem=xy_send, recv_sem=xy_recv,
            device_id=(gx, to, grp), device_id_type=MESH,
        ).start()

    @pl.loop(0, Q)
    def _(p):
        value = conv_pair(wide_h, banded_2, p, False).astype(BF16)
        columns = pl.ds(pl.multiple_of(p * 128, 128), 128)
        output[0, :, :, columns] = value.reshape(X, Y, 128)

    xy_all = pltpu.make_async_remote_copy(
        src_ref=gathered_xy, dst_ref=gathered_xy, send_sem=xy_send, recv_sem=xy_recv,
        device_id=me, device_id_type=MESH,
    )
    xy_all.wait_recv()
    total = part[pl.ds(pl.multiple_of(gy * chunk, 16), chunk), :].astype(F32)
    for k in range(ny - 1):
        total = total + gathered_xy[k].astype(F32)
    summed[...] = total

    @pl.loop(1, nz)
    def _(k):
        to = along_z(k)
        pltpu.make_async_remote_copy(
            src_ref=summed.at[pl.ds(pl.multiple_of(to * tile, 8), tile)],
            dst_ref=gathered_z.at[nz - 1 - k],
            send_sem=z_send, recv_sem=z_recv,
            device_id=z_device(to), device_id_type=MESH,
        ).start()

    z_all = pltpu.make_async_remote_copy(
        src_ref=gathered_z, dst_ref=gathered_z, send_sem=z_send, recv_sem=z_recv,
        device_id=me, device_id_type=MESH,
    )
    z_all.wait_recv()
    own_rows = pl.ds(pl.multiple_of(z * tile, 8), tile)
    mine = summed[own_rows, :]
    for k in range(nz - 1):
        mine = mine + gathered_z[k]
    final[...] = mine
    spread_z[own_rows, :] = mine

    @pl.loop(1, nz)
    def _(k):
        pltpu.make_async_remote_copy(
            src_ref=final, dst_ref=spread_z.at[own_rows],
            send_sem=back_z_send, recv_sem=back_z_recv,
            device_id=z_device(along_z(k)), device_id_type=MESH,
        ).start()

    pltpu.make_async_remote_copy(
        src_ref=gathered_z, dst_ref=gathered_z, send_sem=back_z_send, recv_sem=back_z_recv,
        device_id=me, device_id_type=MESH,
    ).wait_recv()

    def rows_of(j):
        return pl.ds(pl.multiple_of(j * chunk, 16), chunk)

    full[core, rows_of(gy), :] = spread_z[...].astype(BF16)

    @pl.loop(1, ny)
    def _(k):
        pltpu.make_async_remote_copy(
            src_ref=full.at[core, rows_of(gy)], dst_ref=full.at[core, rows_of(gy)],
            send_sem=back_xy_send, recv_sem=back_xy_recv.at[k],
            device_id=(gx, along_xy(k), grp), device_id_type=MESH,
        ).start()

    def share(j):
        pltpu.make_async_remote_copy(
            src_ref=full.at[core, rows_of(j)], dst_ref=full.at[core, rows_of(j)],
            send_sem=share_send, recv_sem=share_recv,
            device_id=sibling, device_id_type=MESH,
        ).start()

    share(gy)

    @pl.loop(1, ny)
    def _(k):
        j = along_xy(ny - k)
        pltpu.make_async_remote_copy(
            src_ref=full.at[core, rows_of(j)], dst_ref=full.at[core, rows_of(j)],
            send_sem=back_xy_send, recv_sem=back_xy_recv.at[k],
            device_id=me, device_id_type=MESH,
        ).wait_recv()
        share(j)

    whole = pltpu.make_async_remote_copy(
        src_ref=full.at[core], dst_ref=full.at[1 - core], send_sem=share_send, recv_sem=share_recv,
        device_id=sibling, device_id_type=MESH,
    )
    whole.wait_recv()

    rows = lax.broadcasted_iota(jnp.int32, (128, 128), 0)
    lanes = lax.broadcasted_iota(jnp.int32, (128, 128), 1)
    unit = (rows == lanes).astype(BF16)
    for g, target in ((0, first_out), (1, second_out)):
        for pair in range(PAIRS):
            for v in range(3):
                start = pair * 192 + v * 64
                block = lax.dot_general(
                    unit, full[g, start : start + 64, :], (((1,), (1,)), ((), ())),
                    preferred_element_type=F32,
                ) * factor
                for half in range(2):
                    tap = 2 * pair + half
                    if tap < 9:
                        target[tap * 3 + 2 - v] = block[half * 64 : half * 64 + 64]

    for number in range(3):
        halo_sent(sends.at[number], halo_send.at[number], me)
    pair_copy.wait_send()
    xy_all.wait_send()
    z_all.wait_send()
    pltpu.make_async_remote_copy(
        src_ref=gathered_z, dst_ref=gathered_z, send_sem=back_z_send, recv_sem=back_z_recv,
        device_id=me, device_id_type=MESH,
    ).wait_send()
    pltpu.make_async_remote_copy(
        src_ref=gathered_xy, dst_ref=gathered_xy, send_sem=back_xy_send, recv_sem=xy_recv,
        device_id=me, device_id_type=MESH,
    ).wait_send()
    whole.wait_send()


def shards(sizes, field_in, first_weight, second_weight, cotangent):
    nx, ny, ng = sizes
    nz = nx * ng // 2
    tile = 8 * pl.cdiv(pl.cdiv(PACKED, 8), ny * nz)
    chunk = tile * nz
    rows = chunk * ny
    total = ng * nx * X * ny * Y * NZ
    dma = pltpu.SemaphoreType.DMA
    vmem = pltpu.VMEM
    whole = pl.BlockSpec(memory_space=pltpu.VMEM)
    cells = (XE * YE * Q, 128)
    wide = (Q, ROWS_E, 768)
    output, first_grad, second_grad = pl.pallas_call(
        functools.partial(step, sizes, 1.0 / math.sqrt(total)),
        out_shape=(
            jax.ShapeDtypeStruct(field_in.shape, BF16),
            jax.ShapeDtypeStruct((27, C, C), F32),
            jax.ShapeDtypeStruct((27, C, C), F32),
        ),
        in_specs=[whole] * 4,
        out_specs=(whole,) * 3,
        scratch_shapes=[
            vmem(cells, F32), vmem(cells, F32), vmem(cells, F32),
            vmem(wide, BF16), vmem(wide, BF16), vmem(wide, BF16),
            vmem((768, 384), BF16), vmem((768, 384), BF16), vmem((384, 768), BF16),
            vmem((256, Q * 128), BF16), vmem((256, Q * 128), BF16),
            vmem((Q, X * Y, 128), F32),
            vmem((3, 2 * X + Y, Q, 128), BF16), vmem((3, CELLS, Q, 128), BF16),
            vmem((2, rows, 128), BF16), vmem((rows, 128), BF16), vmem((rows, 128), BF16),
            vmem((ny - 1, chunk, 128), BF16), vmem((chunk, 128), F32),
            vmem((nz - 1, tile, 128), F32), vmem((tile, 128), F32), vmem((chunk, 128), F32),
            vmem((2, rows, 128), BF16),
            dma((3, 5)), dma((3,)), dma, dma, dma, dma, dma, dma,
            dma, dma, dma, dma((ny,)), dma, dma,
        ],
        compiler_params=pltpu.CompilerParams(
            collective_id=0, has_side_effects=True, vmem_limit_bytes=48 * 1024 * 1024
        ),
    )(
        field_in,
        first_weight.reshape(27, C, C),
        second_weight.reshape(27, C, C),
        cotangent,
    )
    shape = (3, 3, 3, C, C)
    return output, first_grad.reshape(shape), second_grad.reshape(shape)


def solution(mesh):
    sizes = (mesh.shape["gx"], mesh.shape["gy"], mesh.shape["grp"])
    return jax.shard_map(
        functools.partial(shards, sizes),
        mesh=mesh,
        in_specs=(P("grp", "gx", "gy", None), P(), P(), P("grp", "gx", "gy", None)),
        out_specs=(P("grp", "gx", "gy", None), P(), P()),
        check_vma=False,
    )
```

```python
import functools
import math

import jax
import jax.numpy as jnp
from jax import lax
from jax.experimental import pallas as pl
from jax.experimental.pallas import tpu as pltpu
from jax.sharding import PartitionSpec as P

C = 64
NZ = 16
X = 8
Y = 16
Q = 8
XE = X + 2
YE = Y + 2
ROWS_E = XE * Y
PAIRS = 5
PACKED = PAIRS * 192
CELLS = 2 * X + Y + 2
F32 = jnp.float32
BF16 = jnp.bfloat16
MESH = pl.DeviceIdType.MESH


def low_lanes(rows):
    return lax.broadcasted_iota(jnp.int32, (rows, 128), 1) < 64


def fill_own(ext, x, q, value):
    ext[pl.ds(((x + 1) * YE + 1) * Q + q, Y, stride=Q), :] = value


def edge_cells(ext, sends, gx):
    near = X - (X - 1) * gx
    for y in range(Y):
        start = pl.multiple_of((near * YE + 1 + y) * Q, Q)
        sends[y] = ext[pl.ds(start, Q), :].astype(BF16)
    for x in range(X):
        sends[Y + x] = ext[pl.ds(((x + 1) * YE + 1) * Q, Q), :].astype(BF16)
        sends[Y + X + x] = ext[pl.ds(((x + 1) * YE + Y) * Q, Q), :].astype(BF16)


def halo_copies(sends, lands, send_sems, recv_sem, gx, gy, grp, count):
    up = lax.rem(gy + 1, count)
    down = lax.rem(gy + count - 1, count)
    other = 1 - gx
    moves = (
        (0, Y, 0, other, gy),
        (Y, X, Y + X, gx, down),
        (Y + X, X, Y, gx, up),
        (0, 1, 2 * X + Y + 1, other, down),
        (Y - 1, 1, 2 * X + Y, other, up),
    )
    for number, (source, size, target, to_x, to_y) in enumerate(moves):
        pltpu.make_async_remote_copy(
            src_ref=sends.at[pl.ds(source, size)],
            dst_ref=lands.at[pl.ds(target, size)],
            send_sem=send_sems.at[number],
            recv_sem=recv_sem,
            device_id=(to_x, to_y, grp),
            device_id_type=MESH,
        ).start()


def halo_arrived(lands, send_sems, recv_sem, me):
    pltpu.make_async_remote_copy(
        src_ref=lands, dst_ref=lands, send_sem=send_sems.at[0], recv_sem=recv_sem,
        device_id=me, device_id_type=MESH,
    ).wait_recv()


def halo_sent(sends, send_sems, me):
    for number, (source, size) in enumerate(((0, Y), (Y, X), (Y + X, X), (0, 1), (Y - 1, 1))):
        part = sends.at[pl.ds(source, size)]
        pltpu.make_async_remote_copy(
            src_ref=part, dst_ref=part, send_sem=send_sems.at[number], recv_sem=send_sems.at[number],
            device_id=me, device_id_type=MESH,
        ).wait_send()


def insert_halo(ext, lands, gx, gy, count):
    front = gx == 1
    back = gx == 0
    below = gy > 0
    above = gy < count - 1

    def put(x, y, cell, valid):
        value = lands[cell].astype(F32)
        ext[pl.ds((x * YE + y) * Q, Q), :] = jnp.where(valid, value, jnp.zeros_like(value))

    for y in range(Y):
        put(0, 1 + y, y, front)
        put(XE - 1, 1 + y, y, back)
    for x in range(X):
        put(1 + x, 0, Y + x, below)
        put(1 + x, YE - 1, Y + X + x, above)
    put(0, 0, 2 * X + Y, front & below)
    put(XE - 1, 0, 2 * X + Y, back & below)
    put(0, YE - 1, 2 * X + Y + 1, front & above)
    put(XE - 1, YE - 1, 2 * X + Y + 1, back & above)


def spread(ext, wide):
    low = low_lanes(Y)
    zero = jnp.zeros((Y, 128), F32)

    @pl.loop(0, XE)
    def _(x):
        rows = pl.ds(pl.multiple_of(x * Y, Y), Y)
        for dy in range(3):
            base = (x * YE + dy) * Q
            pairs = [zero] + [ext[pl.ds(base + q, Y, stride=Q), :] for q in range(Q)] + [zero]
            for q in range(Q):
                mixed = jnp.where(low, pairs[q + 2], pairs[q])
                wide[q, rows, dy * 256 : dy * 256 + 128] = pairs[q + 1].astype(BF16)
                wide[q, rows, dy * 256 + 128 : dy * 256 + 256] = mixed.astype(BF16)


TAPS = ((1, 0), (2, 1), (None, 2), (0, None))


def piece(weight, tap):
    return jnp.zeros((C, C), BF16) if tap is None else weight[tap]


def forward_weight(weight, banded):
    for dy in range(3):
        for slot in range(4):
            rows = slice(dy * 256 + slot * C, dy * 256 + slot * C + C)
            for dx in range(3):
                pieces = [
                    piece(weight, None if t is None else (dx * 3 + dy) * 3 + t) for t in TAPS[slot]
                ]
                banded[rows, dx * 128 : dx * 128 + 128] = jnp.concatenate(pieces, axis=1)


def backward_weight(weight, banded):
    for dx in range(3):
        for b in range(2):
            rows = slice(dx * 128 + b * C, dx * 128 + b * C + C)
            for dy in range(3):
                for half in range(2):
                    pieces = []
                    for slot in (2 * half, 2 * half + 1):
                        t = TAPS[slot][b]
                        tap = None if t is None else ((2 - dx) * 3 + 2 - dy) * 3 + 2 - t
                        pieces.append(piece(weight, tap))
                    start = dy * 256 + half * 128
                    banded[rows, start : start + 128] = jnp.concatenate(pieces, axis=1)


def conv_all(wide, banded, shifted, flipped):
    dims = (((1,), (1 if flipped else 0,)), ((), ()))
    rows = wide[...].reshape(Q * ROWS_E, 768)
    result = lax.dot_general(rows, banded[...], dims, preferred_element_type=F32)
    shifted[...] = result.reshape(Q, ROWS_E, 384)


def conv_pair(shifted, p):
    n = X * Y
    return (
        shifted[p, 0:n, 0:128]
        + shifted[p, Y : Y + n, 128:256]
        + shifted[p, 2 * Y : 2 * Y + n, 256:384]
    )


def kernel_grad(wide, turned, packed, g):
    low = low_lanes(192)
    turned_value = turned[...]

    def moving(tap):
        dx, dy = tap // 3, tap % 3
        block = wide[:, dx * Y : dx * Y + X * Y, dy * 256 : dy * 256 + 128]
        return block.reshape(Q * X * Y, 128)

    for pair in range(PAIRS):
        first = 2 * pair
        if first + 1 < 9:
            rhs = jnp.concatenate([moving(first), moving(first + 1)], axis=1)
        else:
            rhs = moving(first)
        result = jnp.dot(turned_value, rhs, preferred_element_type=F32)
        one = result[:, 0:128]
        two = result[:, 128:256] if first + 1 < 9 else jnp.zeros_like(one)
        straight = jnp.where(low, one[0:192], two[64:256])
        crossed = jnp.where(low, two[0:192], one[64:256])
        total = straight + pltpu.roll(crossed, 64, 1)
        packed[g, pair * 192 : pair * 192 + 192, :] = total.astype(BF16)


def turn(turned, q, block):
    flat = block.astype(F32).T.astype(BF16)
    columns = lambda w: slice(w * 128, w * 128 + 128)
    turned[64:192, columns(q)] = flat
    if q + 1 < Q:
        turned[0:64, columns(q + 1)] = flat[64:128]
    else:
        turned[192:256, columns(q)] = jnp.zeros((64, 128), BF16)
    if q > 0:
        turned[192:256, columns(q - 1)] = flat[0:64]
    else:
        turned[0:64, columns(q)] = jnp.zeros((64, 128), BF16)


def step(
    sizes,
    field_hbm, first_hbm, second_hbm, cotangent_hbm,
    output, full,
    field, first, second, cotangent, load_sems, shifted,
    ext_f, ext_c, ext_h, wide_f, wide_c, wide_h,
    banded_1, banded_2, banded_t, turned_c, turned_p, pre,
    sends, lands, packed, mate, part, gathered_xy, gathered_z,
    halo_send, halo_recv, mate_send, mate_recv, xy_send, xy_recv, z_send, z_recv,
    back_xy_send, back_xy_recv, share_send, share_recv,
):
    nx, ny, ng = sizes
    zl = ng // 2
    nz = nx * zl
    chunk = packed.shape[1] // ny
    loads = [
        pltpu.make_async_copy(source, target, load_sems.at[number])
        for number, (source, target) in enumerate(
            ((field_hbm, field), (cotangent_hbm, cotangent), (first_hbm, first), (second_hbm, second))
        )
    ]
    for load in loads:
        load.start()
    gx, gy, grp = lax.axis_index("gx"), lax.axis_index("gy"), lax.axis_index("grp")
    core = lax.rem(grp, 2)
    z = gx * zl + grp // 2
    me = (gx, gy, grp)
    sibling = (gx, gy, grp + 1 - 2 * core)

    def along_xy(k):
        return lax.rem(gy + k, ny)

    def along_z(k):
        return lax.rem(z + k, nz)

    def z_device(target):
        return (target // zl, gy, 2 * lax.rem(target, zl) + core)

    barrier = pltpu.get_barrier_semaphore()

    def greet(device):
        pl.semaphore_signal(barrier, inc=1, device_id=device, device_id_type=MESH)

    greet((1 - gx, along_xy(1), grp))
    greet((1 - gx, along_xy(ny - 1), grp))
    greet(sibling)

    @pl.loop(1, nz)
    def _(k):
        greet(z_device(along_z(k)))

    @pl.loop(1, ny)
    def _(k):
        greet((gx, along_xy(k), grp))

    fields = ((field, ext_f, 0), (cotangent, ext_c, 1))
    for source, ext, number in fields:
        loads[number].wait()
        for x in range(X):
            for q in range(Q):
                fill_own(ext, x, q, source[0, x, :, q * 128 : q * 128 + 128].astype(F32))
        edge_cells(ext, sends.at[number], gx)
    pl.semaphore_wait(barrier, nz - 1 + ny - 1 + 3)
    for number in range(2):
        halo_copies(
            sends.at[number], lands.at[number], halo_send.at[number], halo_recv.at[number], gx, gy, grp, ny
        )

    loads[2].wait()
    loads[3].wait()
    forward_weight(first, banded_1)
    forward_weight(second, banded_2)
    backward_weight(second, banded_t)
    for q in range(Q):
        turn(turned_c, q, cotangent[0, :, :, q * 128 : q * 128 + 128].reshape(X * Y, 128))

    halo_arrived(lands.at[0], halo_send.at[0], halo_recv.at[0], me)
    insert_halo(ext_f, lands.at[0], gx, gy, ny)
    spread(ext_f, wide_f)

    conv_all(wide_f, banded_1, shifted, False)

    @pl.loop(0, Q)
    def _(p):
        value = conv_pair(shifted, p)
        pre[p] = value
        hidden = (value * jax.nn.sigmoid(value)).astype(BF16).astype(F32)
        for x in range(X):
            fill_own(ext_h, x, p, hidden[x * Y : x * Y + Y])

    edge_cells(ext_h, sends.at[2], gx)
    halo_copies(sends.at[2], lands.at[2], halo_send.at[2], halo_recv.at[2], gx, gy, grp, ny)

    halo_arrived(lands.at[1], halo_send.at[1], halo_recv.at[1], me)
    insert_halo(ext_c, lands.at[1], gx, gy, ny)
    spread(ext_c, wide_c)
    conv_all(wide_c, banded_t, shifted, True)
    for p in range(Q):
        hidden_grad = conv_pair(shifted, p)
        value = pre[p]
        sigma = jax.nn.sigmoid(value)
        turn(turned_p, p, (hidden_grad * sigma * (1.0 + value * (1.0 - sigma))).astype(BF16))
    if packed.shape[1] > PACKED:
        rest = packed.shape[1] - PACKED
        for g in range(2):
            packed[g, PACKED:, :] = jnp.zeros((rest, 128), BF16)
    kernel_grad(wide_f, turned_p, packed, 0)

    halo_arrived(lands.at[2], halo_send.at[2], halo_recv.at[2], me)
    insert_halo(ext_h, lands.at[2], gx, gy, ny)
    spread(ext_h, wide_h)
    kernel_grad(wide_h, turned_c, packed, 1)

    pair_copy = pltpu.make_async_remote_copy(
        src_ref=packed.at[1 - core], dst_ref=mate, send_sem=mate_send, recv_sem=mate_recv,
        device_id=sibling, device_id_type=MESH,
    )
    pair_copy.start()
    pair_copy.wait_recv()
    part[...] = (packed[core].astype(F32) + mate[...].astype(F32)).astype(BF16)

    @pl.loop(1, ny)
    def _(k):
        to = along_xy(k)
        pltpu.make_async_remote_copy(
            src_ref=part.at[pl.ds(pl.multiple_of(to * chunk, 16), chunk)],
            dst_ref=gathered_xy.at[ny - 1 - k],
            send_sem=xy_send, recv_sem=xy_recv,
            device_id=(gx, to, grp), device_id_type=MESH,
        ).start()

    conv_all(wide_h, banded_2, shifted, False)

    @pl.loop(0, Q)
    def _(p):
        value = conv_pair(shifted, p).astype(BF16)
        columns = pl.ds(pl.multiple_of(p * 128, 128), 128)
        output[0, :, :, columns] = value.reshape(X, Y, 128)

    xy_all = pltpu.make_async_remote_copy(
        src_ref=gathered_xy, dst_ref=gathered_xy, send_sem=xy_send, recv_sem=xy_recv,
        device_id=me, device_id_type=MESH,
    )
    xy_all.wait_recv()
    total = part[pl.ds(pl.multiple_of(gy * chunk, 16), chunk), :].astype(F32)
    for k in range(ny - 1):
        total = total + gathered_xy[k].astype(F32)
    gathered_z[z] = total.astype(BF16)

    @pl.loop(1, nz)
    def _(k):
        pltpu.make_async_remote_copy(
            src_ref=gathered_z.at[z], dst_ref=gathered_z.at[z],
            send_sem=z_send, recv_sem=z_recv,
            device_id=z_device(along_z(k)), device_id_type=MESH,
        ).start()

    others = gathered_z.at[pl.ds(0, nz - 1)]
    z_all = pltpu.make_async_remote_copy(
        src_ref=others, dst_ref=others, send_sem=z_send, recv_sem=z_recv,
        device_id=me, device_id_type=MESH,
    )
    z_all.wait_recv()
    grand = gathered_z[0].astype(F32)
    for k in range(1, nz):
        grand = grand + gathered_z[k].astype(F32)

    def rows_of(j):
        return pl.ds(pl.multiple_of(j * chunk, 16), chunk)

    full[core, rows_of(gy), :] = grand.astype(BF16)

    @pl.loop(1, ny)
    def _(k):
        pltpu.make_async_remote_copy(
            src_ref=full.at[core, rows_of(gy)], dst_ref=full.at[core, rows_of(gy)],
            send_sem=back_xy_send, recv_sem=back_xy_recv.at[k],
            device_id=(gx, along_xy(k), grp), device_id_type=MESH,
        ).start()

    def share(j):
        pltpu.make_async_remote_copy(
            src_ref=full.at[core, rows_of(j)], dst_ref=full.at[core, rows_of(j)],
            send_sem=share_send, recv_sem=share_recv,
            device_id=sibling, device_id_type=MESH,
        ).start()

    share(gy)

    @pl.loop(1, ny)
    def _(k):
        j = along_xy(ny - k)
        pltpu.make_async_remote_copy(
            src_ref=full.at[core, rows_of(j)], dst_ref=full.at[core, rows_of(j)],
            send_sem=back_xy_send, recv_sem=back_xy_recv.at[k],
            device_id=me, device_id_type=MESH,
        ).wait_recv()
        share(j)

    whole = pltpu.make_async_remote_copy(
        src_ref=full.at[core], dst_ref=full.at[1 - core], send_sem=share_send, recv_sem=share_recv,
        device_id=sibling, device_id_type=MESH,
    )
    whole.wait_recv()

    for number in range(3):
        halo_sent(sends.at[number], halo_send.at[number], me)
    pair_copy.wait_send()
    xy_all.wait_send()
    z_all.wait_send()
    pltpu.make_async_remote_copy(
        src_ref=gathered_xy, dst_ref=gathered_xy, send_sem=back_xy_send, recv_sem=xy_recv,
        device_id=me, device_id_type=MESH,
    ).wait_send()
    whole.wait_send()


def unpack(factor, output_in, full, output, first_out, second_out, one, two, sems):
    copies = [
        pltpu.make_async_copy(source, target, sems.at[number])
        for number, (source, target) in enumerate(
            ((output_in, output), (one, first_out), (two, second_out))
        )
    ]
    copies[0].start()
    rows = lax.broadcasted_iota(jnp.int32, (128, 128), 0)
    lanes = lax.broadcasted_iota(jnp.int32, (128, 128), 1)
    unit = (rows == lanes).astype(BF16)
    for g, target in ((0, one), (1, two)):
        for pair in range(PAIRS):
            for v in range(3):
                start = pair * 192 + v * 64
                block = lax.dot_general(
                    unit, full[g, start : start + 64, :], (((1,), (1,)), ((), ())),
                    preferred_element_type=F32,
                ) * factor
                for half in range(2):
                    tap = 2 * pair + half
                    if tap < 9:
                        target[tap * 3 + 2 - v] = block[half * 64 : half * 64 + 64]
        copies[g + 1].start()
    for copy in copies:
        copy.wait()


def shards(sizes, field_in, first_weight, second_weight, cotangent):
    nx, ny, ng = sizes
    nz = nx * ng // 2
    chunk = 16 * pl.cdiv(PACKED, 16 * ny)
    rows = chunk * ny
    total = ng * nx * X * ny * Y * NZ
    dma = pltpu.SemaphoreType.DMA
    vmem = pltpu.VMEM
    inside = pl.BlockSpec(memory_space=pltpu.VMEM)
    outside = pl.BlockSpec(memory_space=pltpu.HBM)
    cells = (XE * YE * Q, 128)
    wide = (Q, ROWS_E, 768)
    weight = (27, C, C)
    output, full = pl.pallas_call(
        functools.partial(step, sizes),
        out_shape=(
            jax.ShapeDtypeStruct(field_in.shape, BF16),
            jax.ShapeDtypeStruct((2, rows, 128), BF16),
        ),
        in_specs=[outside] * 4,
        out_specs=(inside,) * 2,
        scratch_shapes=[
            vmem(field_in.shape, BF16), vmem(weight, BF16), vmem(weight, BF16), vmem(field_in.shape, BF16),
            dma((4,)), vmem((Q, ROWS_E, 384), F32),
            vmem(cells, F32), vmem(cells, F32), vmem(cells, F32),
            vmem(wide, BF16), vmem(wide, BF16), vmem(wide, BF16),
            vmem((768, 384), BF16), vmem((768, 384), BF16), vmem((384, 768), BF16),
            vmem((256, Q * 128), BF16), vmem((256, Q * 128), BF16),
            vmem((Q, X * Y, 128), F32),
            vmem((3, 2 * X + Y, Q, 128), BF16), vmem((3, CELLS, Q, 128), BF16),
            vmem((2, rows, 128), BF16), vmem((rows, 128), BF16), vmem((rows, 128), BF16),
            vmem((ny - 1, chunk, 128), BF16), vmem((nz, chunk, 128), BF16),
            dma((3, 5)), dma((3,)), dma, dma, dma, dma, dma, dma,
            dma, dma((ny,)), dma, dma,
        ],
        compiler_params=pltpu.CompilerParams(
            collective_id=0, has_side_effects=True, vmem_limit_bytes=40 * 1024 * 1024
        ),
    )(
        *(
            pltpu.with_memory_space_constraint(array, pltpu.HBM)
            for array in (
                field_in,
                first_weight.reshape(weight),
                second_weight.reshape(weight),
                cotangent,
            )
        )
    )
    output, first_grad, second_grad = pl.pallas_call(
        functools.partial(unpack, 1.0 / math.sqrt(total)),
        out_shape=(
            jax.ShapeDtypeStruct(field_in.shape, BF16),
            jax.ShapeDtypeStruct(weight, F32),
            jax.ShapeDtypeStruct(weight, F32),
        ),
        in_specs=[inside] * 2,
        out_specs=(outside,) * 3,
        scratch_shapes=[vmem(weight, F32), vmem(weight, F32), dma((3,))],
        compiler_params=pltpu.CompilerParams(vmem_limit_bytes=16 * 1024 * 1024),
    )(output, full)
    shape = (3, 3, 3, C, C)
    return output, first_grad.reshape(shape), second_grad.reshape(shape)


def solution(mesh):
    sizes = (mesh.shape["gx"], mesh.shape["gy"], mesh.shape["grp"])
    return jax.shard_map(
        functools.partial(shards, sizes),
        mesh=mesh,
        in_specs=(P("grp", "gx", "gy", None), P(), P(), P("grp", "gx", "gy", None)),
        out_specs=(P("grp", "gx", "gy", None), P(), P()),
        check_vma=False,
    )
```

```python
import functools
import math

import jax
import jax.numpy as jnp
from jax import lax
from jax.experimental import pallas as pl
from jax.experimental.pallas import tpu as pltpu
from jax.sharding import PartitionSpec as P

C = 64
NZ = 16
X = 8
Y = 16
Q = 8
XE = X + 2
SLOT = 32
ROWS_E = XE * Y
PAIRS = 5
PACKED = PAIRS * 192
F32 = jnp.float32
BF16 = jnp.bfloat16
MESH = pl.DeviceIdType.MESH


def low_lanes(rows):
    return lax.broadcasted_iota(jnp.int32, (rows, 128), 1) < 64


def row(q, x, y):
    return (q * XE + x) * SLOT + 8 + y


def clear_halo(ext, shifted):
    edge = jnp.zeros((8, 128), F32)
    plane = jnp.zeros((SLOT, 128), F32)
    for q in range(Q):
        for x in range(XE):
            if x in (0, XE - 1):
                ext[pl.ds(row(q, x, -8), SLOT), :] = plane
            else:
                ext[pl.ds(row(q, x, -8), 8), :] = edge
                ext[pl.ds(row(q, x, Y), 8), :] = edge
        shifted[q, 0:Y, :] = jnp.zeros((Y, 384), F32)
        shifted[q, ROWS_E - Y : ROWS_E, :] = jnp.zeros((Y, 384), F32)


def take_edges(ext, send_x, send_y, send_c, corner, gx):
    near = X - (X - 1) * gx
    for q in range(Q):
        columns = slice(q * 128, q * 128 + 128)
        plane = ext[pl.ds(pl.multiple_of(row(q, near, 0), 8), Y), :]
        send_x[:, columns] = plane.astype(BF16)
        corner[0, q : q + 1, :] = plane[0:1]
        corner[1, q : q + 1, :] = plane[Y - 1 : Y]
        for side, y in ((0, 0), (1, Y - 1)):
            send_y[side, :, columns] = ext[pl.ds(row(q, 1, y), X, stride=SLOT), :].astype(BF16)
    send_c[...] = corner[...].astype(BF16)


def halo_copies(ends, send_sems, recv_sems, place, count):
    send_x, send_y, send_c, land_x, land_y, land_c = ends
    gx, gy, grp = place
    up = lax.rem(gy + 1, count)
    down = lax.rem(gy + count - 1, count)
    moves = (
        (send_x, land_x, (1 - gx, gy, grp)),
        (send_y.at[1], land_y.at[0], (gx, up, grp)),
        (send_y.at[0], land_y.at[1], (gx, down, grp)),
        (send_c.at[1], land_c.at[0], (1 - gx, up, grp)),
        (send_c.at[0], land_c.at[1], (1 - gx, down, grp)),
    )
    return [
        pltpu.make_async_remote_copy(
            src_ref=source, dst_ref=target, send_sem=send_sems.at[number], recv_sem=recv_sems.at[number],
            device_id=device, device_id_type=MESH,
        )
        for number, (source, target, device) in enumerate(moves)
    ]


def insert_y(ext, land_y, sided):
    for side, y in ((0, -1), (1, Y)):
        for q in range(Q):
            value = land_y[side, :, q * 128 : q * 128 + 128].astype(F32)
            value = jnp.where(sided[side], value, jnp.zeros_like(value))
            ext[pl.ds(row(q, 1, y), X, stride=SLOT), :] = value


def insert_x(ext, land_x, land_c, sided, far, corner):
    corner[...] = land_c[...].astype(F32)
    for q in range(Q):
        start = pl.multiple_of(row(q, far, 0), 8)
        ext[pl.ds(start, Y), :] = land_x[:, q * 128 : q * 128 + 128].astype(F32)
        low = corner[0, q : q + 1, :]
        high = corner[1, q : q + 1, :]
        ext[pl.ds(start - 8, 8), :] = jnp.broadcast_to(jnp.where(sided[0], low, jnp.zeros_like(low)), (8, 128))
        ext[pl.ds(start + Y, 8), :] = jnp.broadcast_to(jnp.where(sided[1], high, jnp.zeros_like(high)), (8, 128))


def operand(values, low):
    zero = jnp.zeros_like(values[0])
    padded = [zero] + values + [zero]
    return [
        (padded[q + 1].astype(BF16), jnp.where(low, padded[q + 2], padded[q]).astype(BF16))
        for q in range(Q)
    ]


def conv_own(ext, wide, banded, shifted, flipped):
    low = low_lanes(Y)
    for x in range(X):
        for dy in range(3):
            values = [ext[pl.ds(row(q, x + 1, dy - 1), Y), :] for q in range(Q)]
            for q, (own, mixed) in enumerate(operand(values, low)):
                wide[q, x * Y : x * Y + Y, dy * 256 : dy * 256 + 128] = own
                wide[q, x * Y : x * Y + Y, dy * 256 + 128 : dy * 256 + 256] = mixed
    dims = (((1,), (1 if flipped else 0,)), ((), ()))
    result = lax.dot_general(
        wide[...].reshape(Q * X * Y, 768), banded[...], dims, preferred_element_type=F32
    )
    shifted[:, Y : Y + X * Y, :] = result.reshape(Q, X * Y, 384)


def conv_y(ext, banded, columns, flipped):
    low = low_lanes(X)
    for side, y, dy in ((0, -1, 0), (1, Y, 2)):
        values = [ext[pl.ds(row(q, 1, y), X, stride=SLOT), :] for q in range(Q)]
        padded = [jnp.zeros((X, 128), F32)] + values + [jnp.zeros((X, 128), F32)]
        own = jnp.concatenate(values, axis=0)
        mixed = jnp.concatenate([jnp.where(low, padded[q + 2], padded[q]) for q in range(Q)], axis=0)
        rows = jnp.concatenate([own, mixed], axis=1).astype(BF16)
        if flipped:
            weight = banded[:, dy * 256 : dy * 256 + 256]
        else:
            weight = banded[dy * 256 : dy * 256 + 256, :]
        dims = (((1,), (1 if flipped else 0,)), ((), ()))
        result = lax.dot_general(rows, weight, dims, preferred_element_type=F32)
        for q in range(Q):
            columns[side, q, 8:16, :] = result[q * X : q * X + X]


def conv_x(ext, thin, banded, shifted, flipped, far):
    low = low_lanes(Y)
    for dy in range(3):
        values = [
            ext[pl.ds(pl.multiple_of(row(q, far, 0), 8) + dy - 1, Y), :] for q in range(Q)
        ]
        for q, (own, mixed) in enumerate(operand(values, low)):
            thin[q * Y : q * Y + Y, dy * 256 : dy * 256 + 128] = own
            thin[q * Y : q * Y + Y, dy * 256 + 128 : dy * 256 + 256] = mixed
    dims = (((1,), (1 if flipped else 0,)), ((), ()))
    result = lax.dot_general(thin[...], banded[...], dims, preferred_element_type=F32)
    start = pl.multiple_of(far * Y, Y)
    for q in range(Q):
        shifted[q, pl.ds(start, Y), :] = result[q * Y : q * Y + Y]


def conv_pair(shifted, columns, sums, p):
    n = X * Y
    sums[...] = (
        shifted[p, 0:n, 0:128]
        + shifted[p, Y : Y + n, 128:256]
        + shifted[p, 2 * Y : 2 * Y + n, 256:384]
    )
    for side, y in ((0, 0), (1, Y - 1)):
        extra = (
            columns[side, p, 7:15, 0:128]
            + columns[side, p, 8:16, 128:256]
            + columns[side, p, 9:17, 256:384]
        )
        place = pl.ds(y, X, stride=Y)
        sums[place, :] = sums[place, :] + extra
    return sums[...]


TAPS = ((1, 0), (2, 1), (None, 2), (0, None))


def piece(weight, tap):
    return jnp.zeros((C, C), BF16) if tap is None else weight[tap]


def forward_weight(weight, banded):
    for dy in range(3):
        for slot in range(4):
            rows = slice(dy * 256 + slot * C, dy * 256 + slot * C + C)
            for dx in range(3):
                pieces = [
                    piece(weight, None if t is None else (dx * 3 + dy) * 3 + t) for t in TAPS[slot]
                ]
                banded[rows, dx * 128 : dx * 128 + 128] = jnp.concatenate(pieces, axis=1)


def backward_weight(weight, banded):
    for dx in range(3):
        for b in range(2):
            rows = slice(dx * 128 + b * C, dx * 128 + b * C + C)
            for dy in range(3):
                for half in range(2):
                    pieces = []
                    for slot in (2 * half, 2 * half + 1):
                        t = TAPS[slot][b]
                        tap = None if t is None else ((2 - dx) * 3 + 2 - dy) * 3 + 2 - t
                        pieces.append(piece(weight, tap))
                    start = dy * 256 + half * 128
                    banded[rows, start : start + 128] = jnp.concatenate(pieces, axis=1)


def kernel_grad(ext, turned, packed, g, finished):
    low = low_lanes(192)
    turned_value = turned[...]

    def moving(tap):
        dx, dy = tap // 3, tap % 3
        blocks = [
            ext[pl.ds(row(q, x + dx, dy - 1), Y), :].astype(BF16) for q in range(Q) for x in range(X)
        ]
        return jnp.concatenate(blocks, axis=0)

    for pair in range(PAIRS):
        first = 2 * pair
        if first + 1 < 9:
            rhs = jnp.concatenate([moving(first), moving(first + 1)], axis=1)
        else:
            rhs = moving(first)
        result = jnp.dot(turned_value, rhs, preferred_element_type=F32)
        one = result[:, 0:128]
        two = result[:, 128:256] if first + 1 < 9 else jnp.zeros_like(one)
        straight = jnp.where(low, one[0:192], two[64:256])
        crossed = jnp.where(low, two[0:192], one[64:256])
        total = straight + pltpu.roll(crossed, 64, 1)
        packed[g, pair * 192 : pair * 192 + 192, :] = total.astype(BF16)
        finished(pair)


def turn(turned, q, block):
    flat = block.astype(F32).T.astype(BF16)
    columns = lambda w: slice(w * 128, w * 128 + 128)
    turned[64:192, columns(q)] = flat
    if q + 1 < Q:
        turned[0:64, columns(q + 1)] = flat[64:128]
    else:
        turned[192:256, columns(q)] = jnp.zeros((64, 128), BF16)
    if q > 0:
        turned[192:256, columns(q - 1)] = flat[0:64]
    else:
        turned[0:64, columns(q)] = jnp.zeros((64, 128), BF16)


def step(
    sizes,
    field_hbm, first_hbm, second_hbm, cotangent_hbm,
    output, full,
    field, first, second, cotangent, load_sems, shifted, shifted_c,
    ext_f, ext_c, ext_h, wide, thin, columns, sums,
    banded_1, banded_2, banded_t, turned_c, turned_p, slope,
    send_x, send_y, send_c, land_x, land_y, land_c, corner,
    packed, mate, part, gathered_xy, gathered_z,
    halo_send, halo_recv, mate_send, mate_recv, xy_send, xy_recv, z_send, z_recv,
    back_xy_send, back_xy_recv, share_send, share_recv,
):
    nx, ny, ng = sizes
    zl = ng // 2
    nz = nx * zl
    chunk = packed.shape[1] // ny
    loads = [
        pltpu.make_async_copy(source, target, load_sems.at[number])
        for number, (source, target) in enumerate(
            ((field_hbm, field), (cotangent_hbm, cotangent), (first_hbm, first), (second_hbm, second))
        )
    ]
    for load in loads:
        load.start()
    gx, gy, grp = lax.axis_index("gx"), lax.axis_index("gy"), lax.axis_index("grp")
    core = lax.rem(grp, 2)
    z = gx * zl + grp // 2
    me = (gx, gy, grp)
    sibling = (gx, gy, grp + 1 - 2 * core)

    def along_xy(k):
        return lax.rem(gy + k, ny)

    def along_z(k):
        return lax.rem(z + k, nz)

    def z_device(target):
        return (target // zl, gy, 2 * lax.rem(target, zl) + core)

    barrier = pltpu.get_barrier_semaphore()

    def greet(device):
        pl.semaphore_signal(barrier, inc=1, device_id=device, device_id_type=MESH)

    greet((1 - gx, along_xy(1), grp))
    greet((1 - gx, along_xy(ny - 1), grp))
    greet(sibling)

    @pl.loop(1, nz)
    def _(k):
        greet(z_device(along_z(k)))

    @pl.loop(1, ny)
    def _(k):
        greet((gx, along_xy(k), grp))

    place = (gx, gy, grp)
    sided = (gy > 0, gy < ny - 1)
    far = (XE - 1) * (1 - gx)
    halos = [
        halo_copies(
            tuple(end.at[number] for end in (send_x, send_y, send_c, land_x, land_y, land_c)),
            halo_send.at[number], halo_recv.at[number], place, ny,
        )
        for number in range(3)
    ]

    def dispatch(number, ext):
        take_edges(ext, send_x.at[number], send_y.at[number], send_c.at[number], corner, gx)
        if number == 0:
            pl.semaphore_wait(barrier, nz - 1 + ny - 1 + 3)
        for copy in halos[number]:
            copy.start()

    def arrive(number, ext, then_y, then_x):
        for which in (1, 2):
            halos[number][which].wait_recv()
        insert_y(ext, land_y.at[number], sided)
        then_y()
        for which in (0, 3, 4):
            halos[number][which].wait_recv()
        insert_x(ext, land_x.at[number], land_c.at[number], sided, far, corner)
        then_x()

    def load_own(ext, source):
        for x in range(X):
            for q in range(Q):
                ext[pl.ds(row(q, x + 1, 0), Y), :] = source[0, x, :, q * 128 : q * 128 + 128].astype(F32)

    clear_halo(ext_f, shifted)
    loads[0].wait()
    load_own(ext_f, field)
    dispatch(0, ext_f)
    clear_halo(ext_c, shifted_c)
    loads[1].wait()
    load_own(ext_c, cotangent)
    dispatch(1, ext_c)

    loads[2].wait()
    forward_weight(first, banded_1)
    conv_own(ext_f, wide, banded_1, shifted, False)
    columns[...] = jnp.zeros_like(columns)
    loads[3].wait()
    backward_weight(second, banded_t)
    for q in range(Q):
        turn(turned_c, q, cotangent[0, :, :, q * 128 : q * 128 + 128].reshape(X * Y, 128))

    arrive(
        0, ext_f,
        lambda: conv_y(ext_f, banded_1, columns, False),
        lambda: conv_x(ext_f, thin, banded_1, shifted, False, far),
    )

    for p in range(Q):
        value = conv_pair(shifted, columns, sums, p)
        sigma = jax.nn.sigmoid(value)
        hidden = (value * sigma).astype(BF16).astype(F32)
        slope[p] = sigma * (1.0 + value * (1.0 - sigma))
        for x in range(X):
            ext_h[pl.ds(row(p, x + 1, 0), Y), :] = hidden[x * Y : x * Y + Y]
    dispatch(2, ext_h)
    clear_halo(ext_h, shifted)

    conv_own(ext_c, wide, banded_t, shifted_c, True)
    arrive(
        1, ext_c,
        lambda: conv_y(ext_c, banded_t, columns, True),
        lambda: conv_x(ext_c, thin, banded_t, shifted_c, True, far),
    )
    for p in range(Q):
        hidden_grad = conv_pair(shifted_c, columns, sums, p)
        turn(turned_p, p, (hidden_grad * slope[p]).astype(BF16))
    if packed.shape[1] > PACKED:
        rest = packed.shape[1] - PACKED
        part[PACKED:, :] = jnp.zeros((rest, 128), BF16)

    def mate_copy(g, pair):
        block = pl.ds(pair * 192, 192)
        return pltpu.make_async_remote_copy(
            src_ref=packed.at[g, block], dst_ref=mate.at[block],
            send_sem=mate_send.at[pair], recv_sem=mate_recv.at[pair],
            device_id=sibling, device_id_type=MESH,
        )

    def hand_over(g):
        def finished(pair):
            @pl.when(core == 1 - g)
            def _():
                mate_copy(g, pair).start()

        return finished

    kernel_grad(ext_f, turned_p, packed, 0, hand_over(0))
    forward_weight(second, banded_2)
    arrive(2, ext_h, lambda: None, lambda: None)
    kernel_grad(ext_h, turned_c, packed, 1, hand_over(1))
    for pair in range(PAIRS):
        mate_copy(0, pair).wait_recv()
        block = pl.ds(pair * 192, 192)
        part[block, :] = (packed[core, block, :].astype(F32) + mate[block, :].astype(F32)).astype(BF16)
    @pl.loop(1, ny)
    def _(k):
        to = along_xy(k)
        pltpu.make_async_remote_copy(
            src_ref=part.at[pl.ds(pl.multiple_of(to * chunk, 16), chunk)],
            dst_ref=gathered_xy.at[ny - 1 - k],
            send_sem=xy_send, recv_sem=xy_recv,
            device_id=(gx, to, grp), device_id_type=MESH,
        ).start()

    clear = jnp.zeros((8, 128), F32)
    conv_y(ext_h, banded_2, columns, False)
    conv_x(ext_h, thin, banded_2, shifted, False, far)
    for q in range(Q):
        for x in range(X):
            ext_h[pl.ds(row(q, x + 1, -8), 8), :] = clear
            ext_h[pl.ds(row(q, x + 1, Y), 8), :] = clear
    conv_own(ext_h, wide, banded_2, shifted, False)
    for p in range(Q):
        value = conv_pair(shifted, columns, sums, p).astype(BF16)
        output[0, :, :, p * 128 : p * 128 + 128] = value.reshape(X, Y, 128)

    xy_all = pltpu.make_async_remote_copy(
        src_ref=gathered_xy, dst_ref=gathered_xy, send_sem=xy_send, recv_sem=xy_recv,
        device_id=me, device_id_type=MESH,
    )
    xy_all.wait_recv()
    total = part[pl.ds(pl.multiple_of(gy * chunk, 16), chunk), :].astype(F32)
    for k in range(ny - 1):
        total = total + gathered_xy[k].astype(F32)
    gathered_z[z] = total.astype(BF16)

    @pl.loop(1, nz)
    def _(k):
        pltpu.make_async_remote_copy(
            src_ref=gathered_z.at[z], dst_ref=gathered_z.at[z],
            send_sem=z_send, recv_sem=z_recv,
            device_id=z_device(along_z(k)), device_id_type=MESH,
        ).start()

    others = gathered_z.at[pl.ds(0, nz - 1)]
    z_all = pltpu.make_async_remote_copy(
        src_ref=others, dst_ref=others, send_sem=z_send, recv_sem=z_recv,
        device_id=me, device_id_type=MESH,
    )
    z_all.wait_recv()
    grand = gathered_z[0].astype(F32)
    for k in range(1, nz):
        grand = grand + gathered_z[k].astype(F32)

    def rows_of(j):
        return pl.ds(pl.multiple_of(j * chunk, 16), chunk)

    full[core, rows_of(gy), :] = grand.astype(BF16)

    @pl.loop(1, ny)
    def _(k):
        pltpu.make_async_remote_copy(
            src_ref=full.at[core, rows_of(gy)], dst_ref=full.at[core, rows_of(gy)],
            send_sem=back_xy_send, recv_sem=back_xy_recv.at[k],
            device_id=(gx, along_xy(k), grp), device_id_type=MESH,
        ).start()

    def share(j):
        pltpu.make_async_remote_copy(
            src_ref=full.at[core, rows_of(j)], dst_ref=full.at[core, rows_of(j)],
            send_sem=share_send, recv_sem=share_recv,
            device_id=sibling, device_id_type=MESH,
        ).start()

    share(gy)

    @pl.loop(1, ny)
    def _(k):
        j = along_xy(ny - k)
        pltpu.make_async_remote_copy(
            src_ref=full.at[core, rows_of(j)], dst_ref=full.at[core, rows_of(j)],
            send_sem=back_xy_send, recv_sem=back_xy_recv.at[k],
            device_id=me, device_id_type=MESH,
        ).wait_recv()
        share(j)

    whole = pltpu.make_async_remote_copy(
        src_ref=full.at[core], dst_ref=full.at[1 - core], send_sem=share_send, recv_sem=share_recv,
        device_id=sibling, device_id_type=MESH,
    )
    whole.wait_recv()

    for number in range(3):
        for copy in halos[number]:
            copy.wait_send()
    for pair in range(PAIRS):
        mate_copy(0, pair).wait_send()
    xy_all.wait_send()
    z_all.wait_send()
    pltpu.make_async_remote_copy(
        src_ref=gathered_xy, dst_ref=gathered_xy, send_sem=back_xy_send, recv_sem=xy_recv,
        device_id=me, device_id_type=MESH,
    ).wait_send()
    whole.wait_send()


def unpack(factor, output_in, full, output, first_out, second_out, one, two, sems):
    copies = [
        pltpu.make_async_copy(source, target, sems.at[number])
        for number, (source, target) in enumerate(
            ((output_in, output), (one, first_out), (two, second_out))
        )
    ]
    copies[0].start()
    rows = lax.broadcasted_iota(jnp.int32, (128, 128), 0)
    lanes = lax.broadcasted_iota(jnp.int32, (128, 128), 1)
    unit = (rows == lanes).astype(BF16)
    for g, target in ((0, one), (1, two)):
        for pair in range(PAIRS):
            for v in range(3):
                start = pair * 192 + v * 64
                block = lax.dot_general(
                    unit, full[g, start : start + 64, :], (((1,), (1,)), ((), ())),
                    preferred_element_type=F32,
                ) * factor
                for half in range(2):
                    tap = 2 * pair + half
                    if tap < 9:
                        target[tap * 3 + 2 - v] = block[half * 64 : half * 64 + 64]
        copies[g + 1].start()
    for copy in copies:
        copy.wait()


def shards(sizes, field_in, first_weight, second_weight, cotangent):
    nx, ny, ng = sizes
    nz = nx * ng // 2
    chunk = 16 * pl.cdiv(PACKED, 16 * ny)
    rows = chunk * ny
    total = ng * nx * X * ny * Y * NZ
    dma = pltpu.SemaphoreType.DMA
    vmem = pltpu.VMEM
    inside = pl.BlockSpec(memory_space=pltpu.VMEM)
    outside = pl.BlockSpec(memory_space=pltpu.HBM)
    cells = (Q * XE * SLOT, 128)
    sums = (Q, ROWS_E, 384)
    weight = (27, C, C)
    output, full = pl.pallas_call(
        functools.partial(step, sizes),
        out_shape=(
            jax.ShapeDtypeStruct(field_in.shape, BF16),
            jax.ShapeDtypeStruct((2, rows, 128), BF16),
        ),
        in_specs=[outside] * 4,
        out_specs=(inside,) * 2,
        scratch_shapes=[
            vmem(field_in.shape, BF16), vmem(weight, BF16), vmem(weight, BF16), vmem(field_in.shape, BF16),
            dma((4,)), vmem(sums, F32), vmem(sums, F32),
            vmem(cells, F32), vmem(cells, F32), vmem(cells, F32),
            vmem((Q, X * Y, 768), BF16), vmem((Q * Y, 768), BF16), vmem((2, Q, 24, 384), F32), vmem((X * Y, 128), F32),
            vmem((768, 384), BF16), vmem((768, 384), BF16), vmem((384, 768), BF16),
            vmem((256, Q * 128), BF16), vmem((256, Q * 128), BF16),
            vmem((Q, X * Y, 128), F32),
            vmem((3, Y, 1024), BF16), vmem((3, 2, X, 1024), BF16), vmem((3, 2, Q, 128), BF16),
            vmem((3, Y, 1024), BF16), vmem((3, 2, X, 1024), BF16), vmem((3, 2, Q, 128), BF16),
            vmem((2, Q, 128), F32),
            vmem((2, rows, 128), BF16), vmem((rows, 128), BF16), vmem((rows, 128), BF16),
            vmem((ny - 1, chunk, 128), BF16), vmem((nz, chunk, 128), BF16),
            dma((3, 5)), dma((3, 5)), dma((PAIRS,)), dma((PAIRS,)), dma, dma, dma, dma,
            dma, dma((ny,)), dma, dma,
        ],
        compiler_params=pltpu.CompilerParams(
            collective_id=0, has_side_effects=True, vmem_limit_bytes=40 * 1024 * 1024
        ),
    )(
        *(
            pltpu.with_memory_space_constraint(array, pltpu.HBM)
            for array in (
                field_in,
                first_weight.reshape(weight),
                second_weight.reshape(weight),
                cotangent,
            )
        )
    )
    output, first_grad, second_grad = pl.pallas_call(
        functools.partial(unpack, 1.0 / math.sqrt(total)),
        out_shape=(
            jax.ShapeDtypeStruct(field_in.shape, BF16),
            jax.ShapeDtypeStruct(weight, F32),
            jax.ShapeDtypeStruct(weight, F32),
        ),
        in_specs=[inside] * 2,
        out_specs=(outside,) * 3,
        scratch_shapes=[vmem(weight, F32), vmem(weight, F32), dma((3,))],
        compiler_params=pltpu.CompilerParams(vmem_limit_bytes=16 * 1024 * 1024),
    )(output, full)
    shape = (3, 3, 3, C, C)
    return output, first_grad.reshape(shape), second_grad.reshape(shape)


def solution(mesh):
    sizes = (mesh.shape["gx"], mesh.shape["gy"], mesh.shape["grp"])
    return jax.shard_map(
        functools.partial(shards, sizes),
        mesh=mesh,
        in_specs=(P("grp", "gx", "gy", None), P(), P(), P("grp", "gx", "gy", None)),
        out_specs=(P("grp", "gx", "gy", None), P(), P()),
        check_vma=False,
    )
```

```python
import functools
import math

import jax
import jax.numpy as jnp
from jax import lax
from jax.experimental import pallas as pl
from jax.experimental.pallas import tpu as pltpu
from jax.sharding import PartitionSpec as P

C = 64
NZ = 16
X = 8
Y = 16
Q = 8
XE = X + 2
SLOT = 32
ROWS_E = XE * Y
PAIRS = 5
PACKED = PAIRS * 192
F32 = jnp.float32
BF16 = jnp.bfloat16
MESH = pl.DeviceIdType.MESH


def low_lanes(rows):
    return lax.broadcasted_iota(jnp.int32, (rows, 128), 1) < 64


def row(q, x, y):
    return (q * XE + x) * SLOT + 8 + y


def clear_halo(ext, shifted):
    edge = jnp.zeros((8, 128), F32)
    plane = jnp.zeros((SLOT, 128), F32)
    for q in range(Q):
        for x in range(XE):
            if x in (0, XE - 1):
                ext[pl.ds(row(q, x, -8), SLOT), :] = plane
            else:
                ext[pl.ds(row(q, x, -8), 8), :] = edge
                ext[pl.ds(row(q, x, Y), 8), :] = edge
        shifted[q, 0:Y, :] = jnp.zeros((Y, 384), F32)
        shifted[q, ROWS_E - Y : ROWS_E, :] = jnp.zeros((Y, 384), F32)


def take_edges(ext, send_x, send_y, send_c, corner, gx):
    near = X - (X - 1) * gx
    for q in range(Q):
        columns = slice(q * 128, q * 128 + 128)
        plane = ext[pl.ds(pl.multiple_of(row(q, near, 0), 8), Y), :]
        send_x[:, columns] = plane.astype(BF16)
        corner[0, q : q + 1, :] = plane[0:1]
        corner[1, q : q + 1, :] = plane[Y - 1 : Y]
        for side, y in ((0, 0), (1, Y - 1)):
            send_y[side, :, columns] = ext[pl.ds(row(q, 1, y), X, stride=SLOT), :].astype(BF16)
    send_c[...] = corner[...].astype(BF16)


def halo_copies(ends, send_sems, recv_sems, place, count):
    send_x, send_y, send_c, land_x, land_y, land_c = ends
    gx, gy, grp = place
    up = lax.rem(gy + 1, count)
    down = lax.rem(gy + count - 1, count)
    moves = (
        (send_c.at[1], land_c.at[0], (1 - gx, up, grp)),
        (send_c.at[0], land_c.at[1], (1 - gx, down, grp)),
        (send_x, land_x, (1 - gx, gy, grp)),
        (send_y.at[1], land_y.at[0], (gx, up, grp)),
        (send_y.at[0], land_y.at[1], (gx, down, grp)),
    )
    return [
        pltpu.make_async_remote_copy(
            src_ref=source, dst_ref=target, send_sem=send_sems.at[number], recv_sem=recv_sems.at[number],
            device_id=device, device_id_type=MESH,
        )
        for number, (source, target, device) in enumerate(moves)
    ]


def insert_y(ext, land_y, sided):
    for side, y in ((0, -1), (1, Y)):
        for q in range(Q):
            value = land_y[side, :, q * 128 : q * 128 + 128].astype(F32)
            value = jnp.where(sided[side], value, jnp.zeros_like(value))
            ext[pl.ds(row(q, 1, y), X, stride=SLOT), :] = value


def insert_x(ext, land_x, land_c, sided, far, corner):
    corner[...] = land_c[...].astype(F32)
    for q in range(Q):
        start = pl.multiple_of(row(q, far, 0), 8)
        ext[pl.ds(start, Y), :] = land_x[:, q * 128 : q * 128 + 128].astype(F32)
        low = corner[0, q : q + 1, :]
        high = corner[1, q : q + 1, :]
        ext[pl.ds(start - 8, 8), :] = jnp.broadcast_to(jnp.where(sided[0], low, jnp.zeros_like(low)), (8, 128))
        ext[pl.ds(start + Y, 8), :] = jnp.broadcast_to(jnp.where(sided[1], high, jnp.zeros_like(high)), (8, 128))


def operand(values, low):
    zero = jnp.zeros_like(values[0])
    padded = [zero] + values + [zero]
    return [
        (padded[q + 1].astype(BF16), jnp.where(low, padded[q + 2], padded[q]).astype(BF16))
        for q in range(Q)
    ]


def conv_own(ext, wide, banded, shifted, flipped):
    low = low_lanes(Y)
    for x in range(X):
        for dy in range(3):
            values = [ext[pl.ds(row(q, x + 1, dy - 1), Y), :] for q in range(Q)]
            for q, (own, mixed) in enumerate(operand(values, low)):
                wide[q, x * Y : x * Y + Y, dy * 256 : dy * 256 + 128] = own
                wide[q, x * Y : x * Y + Y, dy * 256 + 128 : dy * 256 + 256] = mixed
    dims = (((1,), (1 if flipped else 0,)), ((), ()))
    result = lax.dot_general(
        wide[...].reshape(Q * X * Y, 768), banded[...], dims, preferred_element_type=F32
    )
    shifted[:, Y : Y + X * Y, :] = result.reshape(Q, X * Y, 384)


def conv_y(ext, banded, columns, flipped):
    low = low_lanes(X)
    for side, y, dy in ((0, -1, 0), (1, Y, 2)):
        values = [ext[pl.ds(row(q, 1, y), X, stride=SLOT), :] for q in range(Q)]
        padded = [jnp.zeros((X, 128), F32)] + values + [jnp.zeros((X, 128), F32)]
        own = jnp.concatenate(values, axis=0)
        mixed = jnp.concatenate([jnp.where(low, padded[q + 2], padded[q]) for q in range(Q)], axis=0)
        rows = jnp.concatenate([own, mixed], axis=1).astype(BF16)
        if flipped:
            weight = banded[:, dy * 256 : dy * 256 + 256]
        else:
            weight = banded[dy * 256 : dy * 256 + 256, :]
        dims = (((1,), (1 if flipped else 0,)), ((), ()))
        result = lax.dot_general(rows, weight, dims, preferred_element_type=F32)
        for q in range(Q):
            columns[side, q, 8:16, :] = result[q * X : q * X + X]


def conv_x(ext, thin, banded, shifted, flipped, far):
    low = low_lanes(Y)
    for dy in range(3):
        values = [
            ext[pl.ds(pl.multiple_of(row(q, far, 0), 8) + dy - 1, Y), :] for q in range(Q)
        ]
        for q, (own, mixed) in enumerate(operand(values, low)):
            thin[q * Y : q * Y + Y, dy * 256 : dy * 256 + 128] = own
            thin[q * Y : q * Y + Y, dy * 256 + 128 : dy * 256 + 256] = mixed
    dims = (((1,), (1 if flipped else 0,)), ((), ()))
    result = lax.dot_general(thin[...], banded[...], dims, preferred_element_type=F32)
    start = pl.multiple_of(far * Y, Y)
    for q in range(Q):
        shifted[q, pl.ds(start, Y), :] = result[q * Y : q * Y + Y]


def conv_pair(shifted, columns, sums, p):
    n = X * Y
    sums[...] = (
        shifted[p, 0:n, 0:128]
        + shifted[p, Y : Y + n, 128:256]
        + shifted[p, 2 * Y : 2 * Y + n, 256:384]
    )
    for side, y in ((0, 0), (1, Y - 1)):
        extra = (
            columns[side, p, 7:15, 0:128]
            + columns[side, p, 8:16, 128:256]
            + columns[side, p, 9:17, 256:384]
        )
        place = pl.ds(y, X, stride=Y)
        sums[place, :] = sums[place, :] + extra
    return sums[...]


TAPS = ((1, 0), (2, 1), (None, 2), (0, None))


def piece(weight, tap):
    return jnp.zeros((C, C), BF16) if tap is None else weight[tap]


def forward_weight(weight, banded):
    for dy in range(3):
        for slot in range(4):
            rows = slice(dy * 256 + slot * C, dy * 256 + slot * C + C)
            for dx in range(3):
                pieces = [
                    piece(weight, None if t is None else (dx * 3 + dy) * 3 + t) for t in TAPS[slot]
                ]
                banded[rows, dx * 128 : dx * 128 + 128] = jnp.concatenate(pieces, axis=1)


def backward_weight(weight, banded):
    for dx in range(3):
        for b in range(2):
            rows = slice(dx * 128 + b * C, dx * 128 + b * C + C)
            for dy in range(3):
                for half in range(2):
                    pieces = []
                    for slot in (2 * half, 2 * half + 1):
                        t = TAPS[slot][b]
                        tap = None if t is None else ((2 - dx) * 3 + 2 - dy) * 3 + 2 - t
                        pieces.append(piece(weight, tap))
                    start = dy * 256 + half * 128
                    banded[rows, start : start + 128] = jnp.concatenate(pieces, axis=1)


def kernel_grad(ext, turned, packed, g, finished):
    low = low_lanes(192)
    turned_value = turned[...]

    def moving(tap):
        dx, dy = tap // 3, tap % 3
        blocks = [
            ext[pl.ds(row(q, x + dx, dy - 1), Y), :].astype(BF16) for q in range(Q) for x in range(X)
        ]
        return jnp.concatenate(blocks, axis=0)

    for pair in range(PAIRS):
        first = 2 * pair
        if first + 1 < 9:
            rhs = jnp.concatenate([moving(first), moving(first + 1)], axis=1)
        else:
            rhs = moving(first)
        result = jnp.dot(turned_value, rhs, preferred_element_type=F32)
        one = result[:, 0:128]
        two = result[:, 128:256] if first + 1 < 9 else jnp.zeros_like(one)
        straight = jnp.where(low, one[0:192], two[64:256])
        crossed = jnp.where(low, two[0:192], one[64:256])
        total = straight + pltpu.roll(crossed, 64, 1)
        packed[g, pair * 192 : pair * 192 + 192, :] = total.astype(BF16)
        finished(pair)


def turn(turned, q, block):
    flat = block.astype(F32).T.astype(BF16)
    columns = lambda w: slice(w * 128, w * 128 + 128)
    turned[64:192, columns(q)] = flat
    if q + 1 < Q:
        turned[0:64, columns(q + 1)] = flat[64:128]
    else:
        turned[192:256, columns(q)] = jnp.zeros((64, 128), BF16)
    if q > 0:
        turned[192:256, columns(q - 1)] = flat[0:64]
    else:
        turned[0:64, columns(q)] = jnp.zeros((64, 128), BF16)


def step(
    sizes,
    field_hbm, first_hbm, second_hbm, cotangent_hbm,
    output, full,
    field, first, second, cotangent, load_sems, shifted, shifted_c,
    ext_f, ext_c, ext_h, wide, thin, columns, sums,
    banded_1, banded_2, banded_t, turned_c, turned_p, slope,
    send_x, send_y, send_c, land_x, land_y, land_c, corner,
    packed, gathered_xy, own_sum, pass_out, pass_in, gathered_z,
    halo_send, halo_recv, pass_send, pass_recv, xy_send, xy_recv, z_send, z_recv,
    back_xy_send, back_xy_recv, share_send, share_recv,
):
    nx, ny, ng = sizes
    zl = ng // 2
    nz = nx * zl
    chunk = gathered_xy.shape[2]
    owners = PACKED // chunk
    loads = [
        pltpu.make_async_copy(source, target, load_sems.at[number])
        for number, (source, target) in enumerate(
            ((field_hbm, field), (cotangent_hbm, cotangent), (first_hbm, first), (second_hbm, second))
        )
    ]
    for load in loads:
        load.start()
    gx, gy, grp = lax.axis_index("gx"), lax.axis_index("gy"), lax.axis_index("grp")
    core = lax.rem(grp, 2)
    z = gx * zl + grp // 2
    me = (gx, gy, grp)
    sibling = (gx, gy, grp + 1 - 2 * core)

    def along_xy(k):
        return lax.rem(gy + k, ny)

    def along_z(k):
        return lax.rem(z + k, nz)

    def z_device(target):
        return (target // zl, gy, 2 * lax.rem(target, zl) + core)

    barrier = pltpu.get_barrier_semaphore()

    def greet(device):
        pl.semaphore_signal(barrier, inc=1, device_id=device, device_id_type=MESH)

    greet((1 - gx, along_xy(1), grp))
    greet((1 - gx, along_xy(ny - 1), grp))
    greet(sibling)

    @pl.loop(1, nz)
    def _(k):
        greet(z_device(along_z(k)))

    @pl.loop(1, ny)
    def _(k):
        greet((gx, along_xy(k), grp))

    place = (gx, gy, grp)
    sided = (gy > 0, gy < ny - 1)
    far = (XE - 1) * (1 - gx)
    halos = [
        halo_copies(
            tuple(end.at[number] for end in (send_x, send_y, send_c, land_x, land_y, land_c)),
            halo_send.at[number], halo_recv.at[number], place, ny,
        )
        for number in range(3)
    ]

    def dispatch(number, ext):
        take_edges(ext, send_x.at[number], send_y.at[number], send_c.at[number], corner, gx)
        if number == 0:
            pl.semaphore_wait(barrier, nz - 1 + ny - 1 + 3)
        for copy in halos[number]:
            copy.start()

    def arrive(number, ext, then_y, then_x):
        for which in (3, 4):
            halos[number][which].wait_recv()
        insert_y(ext, land_y.at[number], sided)
        then_y()
        for which in (0, 1, 2):
            halos[number][which].wait_recv()
        insert_x(ext, land_x.at[number], land_c.at[number], sided, far, corner)
        then_x()

    def load_own(ext, source):
        for x in range(X):
            for q in range(Q):
                ext[pl.ds(row(q, x + 1, 0), Y), :] = source[0, x, :, q * 128 : q * 128 + 128].astype(F32)

    clear_halo(ext_f, shifted)
    loads[0].wait()
    load_own(ext_f, field)
    dispatch(0, ext_f)
    clear_halo(ext_c, shifted_c)
    loads[1].wait()
    load_own(ext_c, cotangent)
    dispatch(1, ext_c)

    loads[2].wait()
    forward_weight(first, banded_1)
    conv_own(ext_f, wide, banded_1, shifted, False)
    columns[...] = jnp.zeros_like(columns)
    loads[3].wait()
    backward_weight(second, banded_t)
    for q in range(Q):
        turn(turned_c, q, cotangent[0, :, :, q * 128 : q * 128 + 128].reshape(X * Y, 128))

    conv_own(ext_c, wide, banded_t, shifted_c, True)

    arrive(
        0, ext_f,
        lambda: conv_y(ext_f, banded_1, columns, False),
        lambda: conv_x(ext_f, thin, banded_1, shifted, False, far),
    )

    for p in range(Q):
        value = conv_pair(shifted, columns, sums, p)
        sigma = jax.nn.sigmoid(value)
        hidden = (value * sigma).astype(BF16).astype(F32)
        slope[p] = sigma * (1.0 + value * (1.0 - sigma))
        for x in range(X):
            ext_h[pl.ds(row(p, x + 1, 0), Y), :] = hidden[x * Y : x * Y + Y]
    dispatch(2, ext_h)
    clear_halo(ext_h, shifted)

    arrive(
        1, ext_c,
        lambda: conv_y(ext_c, banded_t, columns, True),
        lambda: conv_x(ext_c, thin, banded_t, shifted_c, True, far),
    )
    for p in range(Q):
        hidden_grad = conv_pair(shifted_c, columns, sums, p)
        turn(turned_p, p, (hidden_grad * slope[p]).astype(BF16))

    owner = gy < owners

    def scatter(g):
        def finished(pair):
            for j in range(owners):
                if not pair * 192 < (j + 1) * chunk <= (pair + 1) * 192:
                    continue

                @pl.when(gy != j)
                def _():
                    pltpu.make_async_remote_copy(
                        src_ref=packed.at[g, pl.ds(j * chunk, chunk)], dst_ref=gathered_xy.at[g, gy],
                        send_sem=xy_send.at[g], recv_sem=xy_recv.at[g],
                        device_id=(gx, j, grp), device_id_type=MESH,
                    ).start()

        return finished

    kernel_grad(ext_f, turned_p, packed, 0, scatter(0))
    forward_weight(second, banded_2)
    conv_own(ext_h, wide, banded_2, shifted, False)
    arrive(2, ext_h, lambda: None, lambda: None)
    kernel_grad(ext_h, turned_c, packed, 1, scatter(1))

    conv_y(ext_h, banded_2, columns, False)
    conv_x(ext_h, thin, banded_2, shifted, False, far)
    for p in range(Q):
        value = conv_pair(shifted, columns, sums, p).astype(BF16)
        output[0, :, :, p * 128 : p * 128 + 128] = value.reshape(X, Y, 128)

    def rows_of(j):
        return pl.ds(pl.multiple_of(j * chunk, 16), chunk)

    def several(g, count):
        part = gathered_xy.at[g, pl.ds(0, count)]
        return pltpu.make_async_remote_copy(
            src_ref=part, dst_ref=part, send_sem=xy_send.at[g], recv_sem=xy_recv.at[g],
            device_id=me, device_id_type=MESH,
        )

    pass_on = pltpu.make_async_remote_copy(
        src_ref=pass_out, dst_ref=pass_in, send_sem=pass_send, recv_sem=pass_recv,
        device_id=sibling, device_id_type=MESH,
    )

    for g in range(2):

        @pl.when(owner)
        def _():
            several(g, ny - 1).wait_recv()
            gathered_xy[g, gy] = packed[g, rows_of(gy), :]
            total = gathered_xy[g, 0].astype(F32)
            for k in range(1, ny):
                total = total + gathered_xy[g, k].astype(F32)

            @pl.when(core == 1 - g)
            def _():
                pass_out[...] = total
                pass_on.start()

            @pl.when(core == g)
            def _():
                own_sum[...] = total
                pass_on.wait_recv()
                gathered_z[z] = (own_sum[...] + pass_in[...]).astype(BF16)

                @pl.loop(1, nz)
                def _(k):
                    pltpu.make_async_remote_copy(
                        src_ref=gathered_z.at[z], dst_ref=gathered_z.at[z],
                        send_sem=z_send, recv_sem=z_recv,
                        device_id=z_device(along_z(k)), device_id_type=MESH,
                    ).start()

    def share(j):
        pltpu.make_async_remote_copy(
            src_ref=full.at[core, rows_of(j)], dst_ref=full.at[core, rows_of(j)],
            send_sem=share_send, recv_sem=share_recv,
            device_id=sibling, device_id_type=MESH,
        ).start()

    others = gathered_z.at[pl.ds(0, nz - 1)]
    z_all = pltpu.make_async_remote_copy(
        src_ref=others, dst_ref=others, send_sem=z_send, recv_sem=z_recv,
        device_id=me, device_id_type=MESH,
    )

    @pl.when(owner)
    def _():
        z_all.wait_recv()
        grand = gathered_z[0].astype(F32)
        for k in range(1, nz):
            grand = grand + gathered_z[k].astype(F32)
        full[core, rows_of(gy), :] = grand.astype(BF16)

        @pl.loop(1, ny)
        def _(k):
            pltpu.make_async_remote_copy(
                src_ref=full.at[core, rows_of(gy)], dst_ref=full.at[core, rows_of(gy)],
                send_sem=back_xy_send, recv_sem=back_xy_recv.at[k],
                device_id=(gx, along_xy(k), grp), device_id_type=MESH,
            ).start()

        share(gy)

    @pl.loop(1, ny)
    def _(k):
        j = along_xy(ny - k)

        @pl.when(j < owners)
        def _():
            pltpu.make_async_remote_copy(
                src_ref=full.at[core, rows_of(j)], dst_ref=full.at[core, rows_of(j)],
                send_sem=back_xy_send, recv_sem=back_xy_recv.at[k],
                device_id=me, device_id_type=MESH,
            ).wait_recv()
            share(j)

    whole = pltpu.make_async_remote_copy(
        src_ref=full.at[core], dst_ref=full.at[1 - core], send_sem=share_send, recv_sem=share_recv,
        device_id=sibling, device_id_type=MESH,
    )
    whole.wait_recv()

    for number in range(3):
        for copy in halos[number]:
            copy.wait_send()

    @pl.when(owner)
    def _():
        for g in range(2):
            several(g, owners - 1).wait_send()
        pass_on.wait_send()
        z_all.wait_send()
        pltpu.make_async_remote_copy(
            src_ref=gathered_xy.at[0, pl.ds(0, ny - 1)], dst_ref=gathered_xy.at[0, pl.ds(0, ny - 1)],
            send_sem=back_xy_send, recv_sem=share_recv,
            device_id=me, device_id_type=MESH,
        ).wait_send()

    if owners < ny:

        @pl.when(jnp.logical_not(owner))
        def _():
            for g in range(2):
                several(g, owners).wait_send()

    whole.wait_send()


def unpack(factor, output_in, full, output, first_out, second_out, one, two, sems):
    copies = [
        pltpu.make_async_copy(source, target, sems.at[number])
        for number, (source, target) in enumerate(
            ((output_in, output), (one, first_out), (two, second_out))
        )
    ]
    copies[0].start()
    rows = lax.broadcasted_iota(jnp.int32, (128, 128), 0)
    lanes = lax.broadcasted_iota(jnp.int32, (128, 128), 1)
    unit = (rows == lanes).astype(BF16)
    for g, target in ((0, one), (1, two)):
        for pair in range(PAIRS):
            for v in range(3):
                start = pair * 192 + v * 64
                block = lax.dot_general(
                    unit, full[g, start : start + 64, :], (((1,), (1,)), ((), ())),
                    preferred_element_type=F32,
                ) * factor
                for half in range(2):
                    tap = 2 * pair + half
                    if tap < 9:
                        target[tap * 3 + 2 - v] = block[half * 64 : half * 64 + 64]
        copies[g + 1].start()
    for copy in copies:
        copy.wait()


def shards(sizes, field_in, first_weight, second_weight, cotangent):
    nx, ny, ng = sizes
    nz = nx * ng // 2
    chunk = 16 * pl.cdiv(PACKED, 16 * ny)
    assert PACKED % chunk == 0
    rows = PACKED
    total = ng * nx * X * ny * Y * NZ
    dma = pltpu.SemaphoreType.DMA
    vmem = pltpu.VMEM
    inside = pl.BlockSpec(memory_space=pltpu.VMEM)
    outside = pl.BlockSpec(memory_space=pltpu.HBM)
    cells = (Q * XE * SLOT, 128)
    sums = (Q, ROWS_E, 384)
    weight = (27, C, C)
    output, full = pl.pallas_call(
        functools.partial(step, sizes),
        out_shape=(
            jax.ShapeDtypeStruct(field_in.shape, BF16),
            jax.ShapeDtypeStruct((2, rows, 128), BF16),
        ),
        in_specs=[outside] * 4,
        out_specs=(inside,) * 2,
        scratch_shapes=[
            vmem(field_in.shape, BF16), vmem(weight, BF16), vmem(weight, BF16), vmem(field_in.shape, BF16),
            dma((4,)), vmem(sums, F32), vmem(sums, F32),
            vmem(cells, F32), vmem(cells, F32), vmem(cells, F32),
            vmem((Q, X * Y, 768), BF16), vmem((Q * Y, 768), BF16), vmem((2, Q, 24, 384), F32), vmem((X * Y, 128), F32),
            vmem((768, 384), BF16), vmem((768, 384), BF16), vmem((384, 768), BF16),
            vmem((256, Q * 128), BF16), vmem((256, Q * 128), BF16),
            vmem((Q, X * Y, 128), F32),
            vmem((3, Y, 1024), BF16), vmem((3, 2, X, 1024), BF16), vmem((3, 2, Q, 128), BF16),
            vmem((3, Y, 1024), BF16), vmem((3, 2, X, 1024), BF16), vmem((3, 2, Q, 128), BF16),
            vmem((2, Q, 128), F32),
            vmem((2, rows, 128), BF16), vmem((2, ny, chunk, 128), BF16),
            vmem((chunk, 128), F32), vmem((chunk, 128), F32), vmem((chunk, 128), F32), vmem((nz, chunk, 128), BF16),
            dma((3, 5)), dma((3, 5)), dma, dma, dma((2,)), dma((2,)), dma, dma,
            dma, dma((ny,)), dma, dma,
        ],
        compiler_params=pltpu.CompilerParams(
            collective_id=0, has_side_effects=True, vmem_limit_bytes=40 * 1024 * 1024
        ),
    )(
        *(
            pltpu.with_memory_space_constraint(array, pltpu.HBM)
            for array in (
                field_in,
                first_weight.reshape(weight),
                second_weight.reshape(weight),
                cotangent,
            )
        )
    )
    output, first_grad, second_grad = pl.pallas_call(
        functools.partial(unpack, 1.0 / math.sqrt(total)),
        out_shape=(
            jax.ShapeDtypeStruct(field_in.shape, BF16),
            jax.ShapeDtypeStruct(weight, F32),
            jax.ShapeDtypeStruct(weight, F32),
        ),
        in_specs=[inside] * 2,
        out_specs=(outside,) * 3,
        scratch_shapes=[vmem(weight, F32), vmem(weight, F32), dma((3,))],
        compiler_params=pltpu.CompilerParams(vmem_limit_bytes=16 * 1024 * 1024),
    )(output, full)
    shape = (3, 3, 3, C, C)
    return output, first_grad.reshape(shape), second_grad.reshape(shape)


def solution(mesh):
    sizes = (mesh.shape["gx"], mesh.shape["gy"], mesh.shape["grp"])
    return jax.shard_map(
        functools.partial(shards, sizes),
        mesh=mesh,
        in_specs=(P("grp", "gx", "gy", None), P(), P(), P("grp", "gx", "gy", None)),
        out_specs=(P("grp", "gx", "gy", None), P(), P()),
        check_vma=False,
    )
```

```python
import functools
import math

import jax
import jax.numpy as jnp
from jax import lax
from jax.experimental import pallas as pl
from jax.experimental.pallas import tpu as pltpu
from jax.sharding import PartitionSpec as P

C = 64
NZ = 16
X = 8
Y = 16
Q = 8
XE = X + 2
SLOT = 32
ROWS_E = XE * Y
PAIRS = 5
PACKED = PAIRS * 192
F32 = jnp.float32
BF16 = jnp.bfloat16
MESH = pl.DeviceIdType.MESH


def low_lanes(rows):
    return lax.broadcasted_iota(jnp.int32, (rows, 128), 1) < 64


def row(q, x, y):
    return (q * XE + x) * SLOT + 8 + y


def clear_halo(ext, shifted):
    edge = jnp.zeros((8, 128), F32)
    plane = jnp.zeros((SLOT, 128), F32)
    for q in range(Q):
        for x in range(XE):
            if x in (0, XE - 1):
                ext[pl.ds(row(q, x, -8), SLOT), :] = plane
            else:
                ext[pl.ds(row(q, x, -8), 8), :] = edge
                ext[pl.ds(row(q, x, Y), 8), :] = edge
        shifted[q, 0:Y, :] = jnp.zeros((Y, 384), F32)
        shifted[q, ROWS_E - Y : ROWS_E, :] = jnp.zeros((Y, 384), F32)


def take_edges(ext, send_x, send_y, send_c, corner, gx):
    near = X - (X - 1) * gx
    for q in range(Q):
        columns = slice(q * 128, q * 128 + 128)
        plane = ext[pl.ds(pl.multiple_of(row(q, near, 0), 8), Y), :]
        send_x[:, columns] = plane.astype(BF16)
        corner[0, q : q + 1, :] = plane[0:1]
        corner[1, q : q + 1, :] = plane[Y - 1 : Y]
        for side, y in ((0, 0), (1, Y - 1)):
            send_y[side, :, columns] = ext[pl.ds(row(q, 1, y), X, stride=SLOT), :].astype(BF16)
    send_c[...] = corner[...].astype(BF16)


def halo_copies(ends, send_sems, recv_sems, place, count):
    send_x, send_y, send_c, land_x, land_y, land_c = ends
    gx, gy, grp = place
    up = lax.rem(gy + 1, count)
    down = lax.rem(gy + count - 1, count)
    moves = (
        (send_c.at[1], land_c.at[0], (1 - gx, up, grp)),
        (send_c.at[0], land_c.at[1], (1 - gx, down, grp)),
        (send_x, land_x, (1 - gx, gy, grp)),
        (send_y.at[1], land_y.at[0], (gx, up, grp)),
        (send_y.at[0], land_y.at[1], (gx, down, grp)),
    )
    return [
        pltpu.make_async_remote_copy(
            src_ref=source, dst_ref=target, send_sem=send_sems.at[number], recv_sem=recv_sems.at[number],
            device_id=device, device_id_type=MESH,
        )
        for number, (source, target, device) in enumerate(moves)
    ]


def insert_y(ext, land_y, sided):
    for side, y in ((0, -1), (1, Y)):
        for q in range(Q):
            value = land_y[side, :, q * 128 : q * 128 + 128].astype(F32)
            value = jnp.where(sided[side], value, jnp.zeros_like(value))
            ext[pl.ds(row(q, 1, y), X, stride=SLOT), :] = value


def insert_x(ext, land_x, land_c, sided, far, corner):
    corner[...] = land_c[...].astype(F32)
    for q in range(Q):
        start = pl.multiple_of(row(q, far, 0), 8)
        ext[pl.ds(start, Y), :] = land_x[:, q * 128 : q * 128 + 128].astype(F32)
        low = corner[0, q : q + 1, :]
        high = corner[1, q : q + 1, :]
        ext[pl.ds(start - 8, 8), :] = jnp.broadcast_to(jnp.where(sided[0], low, jnp.zeros_like(low)), (8, 128))
        ext[pl.ds(start + Y, 8), :] = jnp.broadcast_to(jnp.where(sided[1], high, jnp.zeros_like(high)), (8, 128))


def operand(values, low):
    zero = jnp.zeros_like(values[0])
    padded = [zero] + values + [zero]
    return [
        (padded[q + 1].astype(BF16), jnp.where(low, padded[q + 2], padded[q]).astype(BF16))
        for q in range(Q)
    ]


def conv_own(ext, wide, banded, shifted, flipped):
    low = low_lanes(Y)
    for x in range(X):
        for dy in range(3):
            values = [ext[pl.ds(row(q, x + 1, dy - 1), Y), :] for q in range(Q)]
            for q, (own, mixed) in enumerate(operand(values, low)):
                wide[q, x * Y : x * Y + Y, dy * 256 : dy * 256 + 128] = own
                wide[q, x * Y : x * Y + Y, dy * 256 + 128 : dy * 256 + 256] = mixed
    dims = (((1,), (1 if flipped else 0,)), ((), ()))
    result = lax.dot_general(
        wide[...].reshape(Q * X * Y, 768), banded[...], dims, preferred_element_type=F32
    )
    shifted[:, Y : Y + X * Y, :] = result.reshape(Q, X * Y, 384)


def conv_y(ext, banded, columns, flipped):
    low = low_lanes(X)
    for side, y, dy in ((0, -1, 0), (1, Y, 2)):
        values = [ext[pl.ds(row(q, 1, y), X, stride=SLOT), :] for q in range(Q)]
        padded = [jnp.zeros((X, 128), F32)] + values + [jnp.zeros((X, 128), F32)]
        own = jnp.concatenate(values, axis=0)
        mixed = jnp.concatenate([jnp.where(low, padded[q + 2], padded[q]) for q in range(Q)], axis=0)
        rows = jnp.concatenate([own, mixed], axis=1).astype(BF16)
        if flipped:
            weight = banded[:, dy * 256 : dy * 256 + 256]
        else:
            weight = banded[dy * 256 : dy * 256 + 256, :]
        dims = (((1,), (1 if flipped else 0,)), ((), ()))
        result = lax.dot_general(rows, weight, dims, preferred_element_type=F32)
        for q in range(Q):
            columns[side, q, 8:16, :] = result[q * X : q * X + X]


def conv_x(ext, thin, banded, shifted, flipped, far):
    low = low_lanes(Y)
    for dy in range(3):
        values = [
            ext[pl.ds(pl.multiple_of(row(q, far, 0), 8) + dy - 1, Y), :] for q in range(Q)
        ]
        for q, (own, mixed) in enumerate(operand(values, low)):
            thin[q * Y : q * Y + Y, dy * 256 : dy * 256 + 128] = own
            thin[q * Y : q * Y + Y, dy * 256 + 128 : dy * 256 + 256] = mixed
    dims = (((1,), (1 if flipped else 0,)), ((), ()))
    result = lax.dot_general(thin[...], banded[...], dims, preferred_element_type=F32)
    start = pl.multiple_of(far * Y, Y)
    for q in range(Q):
        shifted[q, pl.ds(start, Y), :] = result[q * Y : q * Y + Y]


def conv_pair(shifted, columns, sums, p):
    n = X * Y
    sums[...] = (
        shifted[p, 0:n, 0:128]
        + shifted[p, Y : Y + n, 128:256]
        + shifted[p, 2 * Y : 2 * Y + n, 256:384]
    )
    for side, y in ((0, 0), (1, Y - 1)):
        extra = (
            columns[side, p, 7:15, 0:128]
            + columns[side, p, 8:16, 128:256]
            + columns[side, p, 9:17, 256:384]
        )
        place = pl.ds(y, X, stride=Y)
        sums[place, :] = sums[place, :] + extra
    return sums[...]


TAPS = ((1, 0), (2, 1), (None, 2), (0, None))


def piece(weight, tap):
    return jnp.zeros((C, C), BF16) if tap is None else weight[tap]


def forward_weight(weight, banded):
    for dy in range(3):
        for slot in range(4):
            rows = slice(dy * 256 + slot * C, dy * 256 + slot * C + C)
            for dx in range(3):
                pieces = [
                    piece(weight, None if t is None else (dx * 3 + dy) * 3 + t) for t in TAPS[slot]
                ]
                banded[rows, dx * 128 : dx * 128 + 128] = jnp.concatenate(pieces, axis=1)


def backward_weight(weight, banded):
    for dx in range(3):
        for b in range(2):
            rows = slice(dx * 128 + b * C, dx * 128 + b * C + C)
            for dy in range(3):
                for half in range(2):
                    pieces = []
                    for slot in (2 * half, 2 * half + 1):
                        t = TAPS[slot][b]
                        tap = None if t is None else ((2 - dx) * 3 + 2 - dy) * 3 + 2 - t
                        pieces.append(piece(weight, tap))
                    start = dy * 256 + half * 128
                    banded[rows, start : start + 128] = jnp.concatenate(pieces, axis=1)


def kernel_grad(ext, turned, packed, g, finished):
    low = low_lanes(192)
    turned_value = turned[...]

    def moving(tap):
        dx, dy = tap // 3, tap % 3
        blocks = [
            ext[pl.ds(row(q, x + dx, dy - 1), Y), :].astype(BF16) for q in range(Q) for x in range(X)
        ]
        return jnp.concatenate(blocks, axis=0)

    for pair in range(PAIRS):
        first = 2 * pair
        if first + 1 < 9:
            rhs = jnp.concatenate([moving(first), moving(first + 1)], axis=1)
        else:
            rhs = moving(first)
        result = jnp.dot(turned_value, rhs, preferred_element_type=F32)
        one = result[:, 0:128]
        two = result[:, 128:256] if first + 1 < 9 else jnp.zeros_like(one)
        straight = jnp.where(low, one[0:192], two[64:256])
        crossed = jnp.where(low, two[0:192], one[64:256])
        total = straight + pltpu.roll(crossed, 64, 1)
        packed[g, pair * 192 : pair * 192 + 192, :] = total.astype(BF16)
        finished(pair)


def turn(turned, q, block):
    flat = block.astype(F32).T.astype(BF16)
    columns = lambda w: slice(w * 128, w * 128 + 128)
    turned[64:192, columns(q)] = flat
    if q + 1 < Q:
        turned[0:64, columns(q + 1)] = flat[64:128]
    else:
        turned[192:256, columns(q)] = jnp.zeros((64, 128), BF16)
    if q > 0:
        turned[192:256, columns(q - 1)] = flat[0:64]
    else:
        turned[0:64, columns(q)] = jnp.zeros((64, 128), BF16)


def step(
    sizes,
    field_hbm, first_hbm, second_hbm, cotangent_hbm,
    output, full,
    field, first, second, cotangent, load_sems, shifted, shifted_c,
    ext_f, ext_c, ext_h, wide, thin, columns, sums,
    banded_1, banded_2, banded_t, turned_c, turned_p, slope,
    send_x, send_y, send_c, land_x, land_y, land_c, corner,
    packed, gathered_xy, own_sum, pass_out, pass_in, gathered_z,
    halo_send, halo_recv, pass_send, pass_recv, xy_send, xy_recv, z_send, z_recv,
    back_xy_send, back_xy_recv, share_send, share_recv,
):
    nx, ny, ng = sizes
    zl = ng // 2
    nz = nx * zl
    chunk = gathered_xy.shape[2]
    owners = PACKED // chunk
    loads = [
        pltpu.make_async_copy(source, target, load_sems.at[number])
        for number, (source, target) in enumerate(
            ((field_hbm, field), (cotangent_hbm, cotangent), (first_hbm, first), (second_hbm, second))
        )
    ]
    for load in loads:
        load.start()
    gx, gy, grp = lax.axis_index("gx"), lax.axis_index("gy"), lax.axis_index("grp")
    core = lax.rem(grp, 2)
    z = gx * zl + grp // 2
    me = (gx, gy, grp)
    sibling = (gx, gy, grp + 1 - 2 * core)

    def along_xy(k):
        return lax.rem(gy + k, ny)

    def along_z(k):
        return lax.rem(z + k, nz)

    def z_device(target):
        return (target // zl, gy, 2 * lax.rem(target, zl) + core)

    barrier = pltpu.get_barrier_semaphore()

    def greet(device):
        pl.semaphore_signal(barrier, inc=1, device_id=device, device_id_type=MESH)

    greet((1 - gx, along_xy(1), grp))
    greet((1 - gx, along_xy(ny - 1), grp))
    greet(sibling)

    @pl.loop(1, nz)
    def _(k):
        greet(z_device(along_z(k)))

    @pl.loop(1, ny)
    def _(k):
        greet((gx, along_xy(k), grp))

    place = (gx, gy, grp)
    sided = (gy > 0, gy < ny - 1)
    far = (XE - 1) * (1 - gx)
    halos = [
        halo_copies(
            tuple(end.at[number] for end in (send_x, send_y, send_c, land_x, land_y, land_c)),
            halo_send.at[number], halo_recv.at[number], place, ny,
        )
        for number in range(3)
    ]

    def dispatch(number, ext):
        take_edges(ext, send_x.at[number], send_y.at[number], send_c.at[number], corner, gx)
        if number == 0:
            pl.semaphore_wait(barrier, nz - 1 + ny - 1 + 3)
        for copy in halos[number]:
            copy.start()

    def arrive(number, ext, then_y, then_x):
        for which in (3, 4):
            halos[number][which].wait_recv()
        insert_y(ext, land_y.at[number], sided)
        then_y()
        for which in (0, 1, 2):
            halos[number][which].wait_recv()
        insert_x(ext, land_x.at[number], land_c.at[number], sided, far, corner)
        then_x()

    def load_own(ext, source):
        for x in range(X):
            for q in range(Q):
                ext[pl.ds(row(q, x + 1, 0), Y), :] = source[0, x, :, q * 128 : q * 128 + 128].astype(F32)

    clear_halo(ext_f, shifted)
    loads[0].wait()
    load_own(ext_f, field)
    dispatch(0, ext_f)
    clear_halo(ext_c, shifted_c)
    loads[1].wait()
    load_own(ext_c, cotangent)
    dispatch(1, ext_c)

    loads[2].wait()
    forward_weight(first, banded_1)
    conv_own(ext_f, wide, banded_1, shifted, False)
    columns[...] = jnp.zeros_like(columns)
    loads[3].wait()
    backward_weight(second, banded_t)
    for q in range(Q):
        turn(turned_c, q, cotangent[0, :, :, q * 128 : q * 128 + 128].reshape(X * Y, 128))

    conv_own(ext_c, wide, banded_t, shifted_c, True)

    arrive(
        0, ext_f,
        lambda: conv_y(ext_f, banded_1, columns, False),
        lambda: conv_x(ext_f, thin, banded_1, shifted, False, far),
    )

    for p in range(Q):
        value = conv_pair(shifted, columns, sums, p)
        sigma = jax.nn.sigmoid(value)
        hidden = (value * sigma).astype(BF16).astype(F32)
        slope[p] = sigma * (1.0 + value * (1.0 - sigma))
        for x in range(X):
            ext_h[pl.ds(row(p, x + 1, 0), Y), :] = hidden[x * Y : x * Y + Y]
    dispatch(2, ext_h)
    clear_halo(ext_h, shifted)

    arrive(
        1, ext_c,
        lambda: conv_y(ext_c, banded_t, columns, True),
        lambda: conv_x(ext_c, thin, banded_t, shifted_c, True, far),
    )
    for p in range(Q):
        hidden_grad = conv_pair(shifted_c, columns, sums, p)
        turn(turned_p, p, (hidden_grad * slope[p]).astype(BF16))

    owner = gy < owners

    def scatter(g):
        def finished(pair):
            for j in range(owners):
                if not pair * 192 < (j + 1) * chunk <= (pair + 1) * 192:
                    continue

                @pl.when(gy != j)
                def _():
                    pltpu.make_async_remote_copy(
                        src_ref=packed.at[g, pl.ds(j * chunk, chunk)], dst_ref=gathered_xy.at[g, gy],
                        send_sem=xy_send.at[g], recv_sem=xy_recv.at[g],
                        device_id=(gx, j, grp), device_id_type=MESH,
                    ).start()

        return finished

    kernel_grad(ext_f, turned_p, packed, 0, scatter(0))
    forward_weight(second, banded_2)
    conv_own(ext_h, wide, banded_2, shifted, False)
    arrive(2, ext_h, lambda: None, lambda: None)
    kernel_grad(ext_h, turned_c, packed, 1, scatter(1))

    conv_y(ext_h, banded_2, columns, False)
    conv_x(ext_h, thin, banded_2, shifted, False, far)
    for p in range(Q):
        value = conv_pair(shifted, columns, sums, p).astype(BF16)
        output[0, :, :, p * 128 : p * 128 + 128] = value.reshape(X, Y, 128)

    def rows_of(j):
        return pl.ds(pl.multiple_of(j * chunk, 16), chunk)

    def several(g, count):
        part = gathered_xy.at[g, pl.ds(0, count)]
        return pltpu.make_async_remote_copy(
            src_ref=part, dst_ref=part, send_sem=xy_send.at[g], recv_sem=xy_recv.at[g],
            device_id=me, device_id_type=MESH,
        )

    pass_on = pltpu.make_async_remote_copy(
        src_ref=pass_out, dst_ref=pass_in, send_sem=pass_send, recv_sem=pass_recv,
        device_id=sibling, device_id_type=MESH,
    )

    for g in range(2):

        @pl.when(owner)
        def _():
            several(g, ny - 1).wait_recv()
            gathered_xy[g, gy] = packed[g, rows_of(gy), :]
            total = gathered_xy[g, 0].astype(F32)
            for k in range(1, ny):
                total = total + gathered_xy[g, k].astype(F32)

            @pl.when(core == 1 - g)
            def _():
                pass_out[...] = total
                pass_on.start()

            @pl.when(core == g)
            def _():
                own_sum[...] = total
                pass_on.wait_recv()
                gathered_z[z] = (own_sum[...] + pass_in[...]).astype(BF16)

                @pl.loop(1, nz)
                def _(k):
                    pltpu.make_async_remote_copy(
                        src_ref=gathered_z.at[z], dst_ref=gathered_z.at[z],
                        send_sem=z_send, recv_sem=z_recv,
                        device_id=z_device(along_z(k)), device_id_type=MESH,
                    ).start()

    def share(j):
        pltpu.make_async_remote_copy(
            src_ref=full.at[core, rows_of(j)], dst_ref=full.at[core, rows_of(j)],
            send_sem=share_send, recv_sem=share_recv,
            device_id=sibling, device_id_type=MESH,
        ).start()

    others = gathered_z.at[pl.ds(0, nz - 1)]
    z_all = pltpu.make_async_remote_copy(
        src_ref=others, dst_ref=others, send_sem=z_send, recv_sem=z_recv,
        device_id=me, device_id_type=MESH,
    )

    @pl.when(owner)
    def _():
        z_all.wait_recv()
        grand = gathered_z[0].astype(F32)
        for k in range(1, nz):
            grand = grand + gathered_z[k].astype(F32)
        rows = lax.broadcasted_iota(jnp.int32, (128, 128), 0)
        lanes = lax.broadcasted_iota(jnp.int32, (128, 128), 1)
        unit = (rows == lanes).astype(BF16)
        turned = []
        for start in range(0, chunk, C):
            block = lax.dot_general(
                unit, grand[start : start + C].astype(BF16), (((1,), (1,)), ((), ())),
                preferred_element_type=F32,
            )
            turned.append(jnp.concatenate([block[0:C], block[C : 2 * C]], axis=1))
        full[core, rows_of(gy), :] = jnp.concatenate(turned, axis=0).astype(BF16)

        @pl.loop(1, ny)
        def _(k):
            pltpu.make_async_remote_copy(
                src_ref=full.at[core, rows_of(gy)], dst_ref=full.at[core, rows_of(gy)],
                send_sem=back_xy_send, recv_sem=back_xy_recv.at[k],
                device_id=(gx, along_xy(k), grp), device_id_type=MESH,
            ).start()

        share(gy)

    @pl.loop(1, ny)
    def _(k):
        j = along_xy(ny - k)

        @pl.when(j < owners)
        def _():
            pltpu.make_async_remote_copy(
                src_ref=full.at[core, rows_of(j)], dst_ref=full.at[core, rows_of(j)],
                send_sem=back_xy_send, recv_sem=back_xy_recv.at[k],
                device_id=me, device_id_type=MESH,
            ).wait_recv()
            share(j)

    whole = pltpu.make_async_remote_copy(
        src_ref=full.at[core], dst_ref=full.at[1 - core], send_sem=share_send, recv_sem=share_recv,
        device_id=sibling, device_id_type=MESH,
    )
    whole.wait_recv()

    for number in range(3):
        for copy in halos[number]:
            copy.wait_send()

    @pl.when(owner)
    def _():
        for g in range(2):
            several(g, owners - 1).wait_send()
        pass_on.wait_send()
        z_all.wait_send()
        pltpu.make_async_remote_copy(
            src_ref=gathered_xy.at[0, pl.ds(0, ny - 1)], dst_ref=gathered_xy.at[0, pl.ds(0, ny - 1)],
            send_sem=back_xy_send, recv_sem=share_recv,
            device_id=me, device_id_type=MESH,
        ).wait_send()

    if owners < ny:

        @pl.when(jnp.logical_not(owner))
        def _():
            for g in range(2):
                several(g, owners).wait_send()

    whole.wait_send()


def unpack(factor, output_in, full, output, first_out, second_out, one, two, sems):
    copies = [
        pltpu.make_async_copy(source, target, sems.at[number])
        for number, (source, target) in enumerate(
            ((output_in, output), (one, first_out), (two, second_out))
        )
    ]
    copies[0].start()
    for g, target in ((0, one), (1, two)):
        for pair in range(PAIRS):
            for v in range(3):
                start = (pair * 3 + v) * C
                block = full[g, start : start + C, :].astype(F32) * factor
                target[2 * pair * 3 + 2 - v] = block[:, 0:C]
                if 2 * pair + 1 < 9:
                    target[(2 * pair + 1) * 3 + 2 - v] = block[:, C : 2 * C]
        copies[g + 1].start()
    for copy in copies:
        copy.wait()


def shards(sizes, field_in, first_weight, second_weight, cotangent):
    nx, ny, ng = sizes
    nz = nx * ng // 2
    chunk = C * pl.cdiv(PACKED, C * ny)
    assert PACKED % chunk == 0
    rows = PACKED
    total = ng * nx * X * ny * Y * NZ
    dma = pltpu.SemaphoreType.DMA
    vmem = pltpu.VMEM
    inside = pl.BlockSpec(memory_space=pltpu.VMEM)
    outside = pl.BlockSpec(memory_space=pltpu.HBM)
    cells = (Q * XE * SLOT, 128)
    sums = (Q, ROWS_E, 384)
    weight = (27, C, C)
    output, full = pl.pallas_call(
        functools.partial(step, sizes),
        out_shape=(
            jax.ShapeDtypeStruct(field_in.shape, BF16),
            jax.ShapeDtypeStruct((2, rows, 128), BF16),
        ),
        in_specs=[outside] * 4,
        out_specs=(inside,) * 2,
        scratch_shapes=[
            vmem(field_in.shape, BF16), vmem(weight, BF16), vmem(weight, BF16), vmem(field_in.shape, BF16),
            dma((4,)), vmem(sums, F32), vmem(sums, F32),
            vmem(cells, F32), vmem(cells, F32), vmem(cells, F32),
            vmem((Q, X * Y, 768), BF16), vmem((Q * Y, 768), BF16), vmem((2, Q, 24, 384), F32), vmem((X * Y, 128), F32),
            vmem((768, 384), BF16), vmem((768, 384), BF16), vmem((384, 768), BF16),
            vmem((256, Q * 128), BF16), vmem((256, Q * 128), BF16),
            vmem((Q, X * Y, 128), F32),
            vmem((3, Y, 1024), BF16), vmem((3, 2, X, 1024), BF16), vmem((3, 2, Q, 128), BF16),
            vmem((3, Y, 1024), BF16), vmem((3, 2, X, 1024), BF16), vmem((3, 2, Q, 128), BF16),
            vmem((2, Q, 128), F32),
            vmem((2, rows, 128), BF16), vmem((2, ny, chunk, 128), BF16),
            vmem((chunk, 128), F32), vmem((chunk, 128), F32), vmem((chunk, 128), F32), vmem((nz, chunk, 128), BF16),
            dma((3, 5)), dma((3, 5)), dma, dma, dma((2,)), dma((2,)), dma, dma,
            dma, dma((ny,)), dma, dma,
        ],
        compiler_params=pltpu.CompilerParams(
            collective_id=0, has_side_effects=True, vmem_limit_bytes=40 * 1024 * 1024
        ),
    )(
        *(
            pltpu.with_memory_space_constraint(array, pltpu.HBM)
            for array in (
                field_in,
                first_weight.reshape(weight),
                second_weight.reshape(weight),
                cotangent,
            )
        )
    )
    output, first_grad, second_grad = pl.pallas_call(
        functools.partial(unpack, 1.0 / math.sqrt(total)),
        out_shape=(
            jax.ShapeDtypeStruct(field_in.shape, BF16),
            jax.ShapeDtypeStruct(weight, F32),
            jax.ShapeDtypeStruct(weight, F32),
        ),
        in_specs=[inside] * 2,
        out_specs=(outside,) * 3,
        scratch_shapes=[vmem(weight, F32), vmem(weight, F32), dma((3,))],
        compiler_params=pltpu.CompilerParams(vmem_limit_bytes=16 * 1024 * 1024),
    )(output, full)
    shape = (3, 3, 3, C, C)
    return output, first_grad.reshape(shape), second_grad.reshape(shape)


def solution(mesh):
    sizes = (mesh.shape["gx"], mesh.shape["gy"], mesh.shape["grp"])
    return jax.shard_map(
        functools.partial(shards, sizes),
        mesh=mesh,
        in_specs=(P("grp", "gx", "gy", None), P(), P(), P("grp", "gx", "gy", None)),
        out_specs=(P("grp", "gx", "gy", None), P(), P()),
        check_vma=False,
    )
```

```python
import functools
import math

import jax
import jax.numpy as jnp
from jax import lax
from jax.experimental import pallas as pl
from jax.experimental.pallas import tpu as pltpu
from jax.sharding import PartitionSpec as P

C = 64
NZ = 16
X = 8
Y = 16
Q = 8
XE = X + 2
PLANES = 16
FAR = 10
SLOT = 32
MARGIN = 8
ROWS_E = XE * Y
PAIRS = 5
PACKED = PAIRS * 192
F32 = jnp.float32
BF16 = jnp.bfloat16
MESH = pl.DeviceIdType.MESH


def low_lanes(rows):
    return lax.broadcasted_iota(jnp.int32, (rows, 128), 1) < 64


def row(q, x, y):
    return (q * PLANES + x) * SLOT + MARGIN + 8 + y


def clear_halo(ext, shifted):
    edge = jnp.zeros((8, 128), F32)
    plane = jnp.zeros((SLOT, 128), F32)
    for q in range(Q):
        for x in range(XE):
            if x in (0, XE - 1):
                ext[pl.ds(row(q, x, -8), SLOT), :] = plane
            else:
                ext[pl.ds(row(q, x, -8), 8), :] = edge
                ext[pl.ds(row(q, x, Y), 8), :] = edge
        if shifted is not None:
            shifted[q, 0:Y, :] = jnp.zeros((Y, 384), F32)
            shifted[q, ROWS_E - Y : ROWS_E, :] = jnp.zeros((Y, 384), F32)


def take_edges(ext, send_x, send_y, send_c, corner, gx):
    deep = send_x.shape[0]
    for q in range(Q):
        columns = slice(q * 128, q * 128 + 128)
        for d in range(deep):
            near = (X - d) - (X - 1 - 2 * d) * gx
            plane = ext[pl.ds(pl.multiple_of(row(q, near, 0), 8), Y), :]
            send_x[d, :, columns] = plane.astype(BF16)
            for e in range(deep):
                corner[0, d * deep + e, q : q + 1, :] = plane[e : e + 1]
                corner[1, d * deep + e, q : q + 1, :] = plane[Y - 1 - e : Y - e]
        for e in range(deep):
            for side, y in ((0, e), (1, Y - 1 - e)):
                send_y[side, e, :, columns] = ext[pl.ds(row(q, 1, y), X, stride=SLOT), :].astype(BF16)
    send_c[...] = corner[...].astype(BF16)


def halo_copies(ends, send_sems, recv_sems, place, count):
    send_x, send_y, send_c, land_x, land_y, land_c = ends
    gx, gy, grp = place
    up = lax.rem(gy + 1, count)
    down = lax.rem(gy + count - 1, count)
    moves = (
        (send_c.at[1], land_c.at[0], (1 - gx, up, grp)),
        (send_c.at[0], land_c.at[1], (1 - gx, down, grp)),
        (send_x, land_x, (1 - gx, gy, grp)),
        (send_y.at[1], land_y.at[0], (gx, up, grp)),
        (send_y.at[0], land_y.at[1], (gx, down, grp)),
    )
    return [
        pltpu.make_async_remote_copy(
            src_ref=source, dst_ref=target, send_sem=send_sems.at[number], recv_sem=recv_sems.at[number],
            device_id=device, device_id_type=MESH,
        )
        for number, (source, target, device) in enumerate(moves)
    ]


def insert_y(ext, land_y, sided):
    for e in range(land_y.shape[1]):
        for side, y in ((0, -1 - e), (1, Y + e)):
            for q in range(Q):
                value = land_y[side, e, :, q * 128 : q * 128 + 128].astype(F32)
                value = jnp.where(sided[side], value, jnp.zeros_like(value))
                ext[pl.ds(row(q, 1, y), X, stride=SLOT), :] = value


def insert_x(ext, land_x, land_c, sided, far, corner):
    deep = land_x.shape[0]
    corner[...] = land_c[...].astype(F32)
    rows = lax.broadcasted_iota(jnp.int32, (8, 128), 0)
    for d in range(deep):
        plane = far if d == 0 else FAR
        for q in range(Q):
            start = pl.multiple_of(row(q, plane, 0), 8)
            ext[pl.ds(start, Y), :] = land_x[d, :, q * 128 : q * 128 + 128].astype(F32)
            low = jnp.zeros((8, 128), F32)
            high = jnp.zeros((8, 128), F32)
            for e in range(deep):
                cell = d * deep + e
                low = jnp.where((rows == 7 - e) & sided[0], corner[0, cell, q : q + 1, :], low)
                high = jnp.where((rows == e) & sided[1], corner[1, cell, q : q + 1, :], high)
            ext[pl.ds(start - 8, 8), :] = low
            ext[pl.ds(start + Y, 8), :] = high


def operand(values, low):
    zero = jnp.zeros_like(values[0])
    padded = [zero] + values + [zero]
    return [
        (padded[q + 1].astype(BF16), jnp.where(low, padded[q + 2], padded[q]).astype(BF16))
        for q in range(Q)
    ]


def conv_own(ext, wide, banded, shifted, flipped):
    low = low_lanes(Y)
    for x in range(X):
        for dy in range(3):
            values = [ext[pl.ds(row(q, x + 1, dy - 1), Y), :] for q in range(Q)]
            for q, (own, mixed) in enumerate(operand(values, low)):
                wide[q, x * Y : x * Y + Y, dy * 256 : dy * 256 + 128] = own
                wide[q, x * Y : x * Y + Y, dy * 256 + 128 : dy * 256 + 256] = mixed
    dims = (((1,), (1 if flipped else 0,)), ((), ()))
    result = lax.dot_general(
        wide[...].reshape(Q * X * Y, 768), banded[...], dims, preferred_element_type=F32
    )
    shifted[:, Y : Y + X * Y, :] = result.reshape(Q, X * Y, 384)


def conv_y(ext, banded, columns, flipped):
    low = low_lanes(X)
    for side, y, dy in ((0, -1, 0), (1, Y, 2)):
        values = [ext[pl.ds(row(q, 1, y), X, stride=SLOT), :] for q in range(Q)]
        padded = [jnp.zeros((X, 128), F32)] + values + [jnp.zeros((X, 128), F32)]
        own = jnp.concatenate(values, axis=0)
        mixed = jnp.concatenate([jnp.where(low, padded[q + 2], padded[q]) for q in range(Q)], axis=0)
        rows = jnp.concatenate([own, mixed], axis=1).astype(BF16)
        if flipped:
            weight = banded[:, dy * 256 : dy * 256 + 256]
        else:
            weight = banded[dy * 256 : dy * 256 + 256, :]
        dims = (((1,), (1 if flipped else 0,)), ((), ()))
        result = lax.dot_general(rows, weight, dims, preferred_element_type=F32)
        for q in range(Q):
            columns[side, q, 8:16, :] = result[q * X : q * X + X]


def conv_x(ext, thin, banded, shifted, flipped, far):
    low = low_lanes(Y)
    for dy in range(3):
        values = [
            ext[pl.ds(pl.multiple_of(row(q, far, 0), 8) + dy - 1, Y), :] for q in range(Q)
        ]
        for q, (own, mixed) in enumerate(operand(values, low)):
            thin[q * Y : q * Y + Y, dy * 256 : dy * 256 + 128] = own
            thin[q * Y : q * Y + Y, dy * 256 + 128 : dy * 256 + 256] = mixed
    dims = (((1,), (1 if flipped else 0,)), ((), ()))
    result = lax.dot_general(thin[...], banded[...], dims, preferred_element_type=F32)
    start = pl.multiple_of(far * Y, Y)
    for q in range(Q):
        shifted[q, pl.ds(start, Y), :] = result[q * Y : q * Y + Y]


def silu(value):
    return (value * jax.nn.sigmoid(value)).astype(BF16).astype(F32)


def lanes_of(values, low):
    padded = [jnp.zeros_like(values[0])] + values + [jnp.zeros_like(values[0])]
    own = jnp.concatenate(values, axis=0)
    mixed = jnp.concatenate([jnp.where(low, padded[q + 2], padded[q]) for q in range(Q)], axis=0)
    return [own.astype(BF16), mixed.astype(BF16)]


def ring_x(ext, hidden_ext, banded, sided, gx, far):
    low = low_lanes(SLOT)
    total = jnp.zeros((Q * SLOT, 128), F32)
    for dx, plane in enumerate((X + 2 * gx, far, FAR - (XE - 1) * gx)):
        parts = []
        for dy in range(3):
            starts = [pl.multiple_of(row(q, plane, -8), 8) + dy - 1 for q in range(Q)]
            parts += lanes_of([ext[pl.ds(start, SLOT), :] for start in starts], low)
        total = total + jnp.dot(
            jnp.concatenate(parts, axis=1), banded[:, dx * 128 : dx * 128 + 128], preferred_element_type=F32
        )
    hidden = silu(total)
    y = lax.broadcasted_iota(jnp.int32, (SLOT, 128), 0) - 8
    inside = ((y >= 0) & (y < Y)) | ((y == -1) & sided[0]) | ((y == Y) & sided[1])
    for q in range(Q):
        part = hidden[q * SLOT : q * SLOT + SLOT]
        hidden_ext[pl.ds(pl.multiple_of(row(q, far, -8), 8), SLOT), :] = jnp.where(inside, part, jnp.zeros_like(part))


def ring_y(ext, hidden_ext, banded, ring, sided):
    low = low_lanes(PLANES)
    for side, y in ((0, -1), (1, Y)):
        parts = []
        for dy in range(3):
            parts += lanes_of(
                [ext[pl.ds(row(q, 0, y + dy - 1), PLANES, stride=SLOT), :] for q in range(Q)], low
            )
        ring[...] = jnp.dot(jnp.concatenate(parts, axis=1), banded[...], preferred_element_type=F32)
        for q in range(Q):
            start = q * PLANES
            total = (
                ring[start : start + X, 0:128]
                + ring[start + 1 : start + 1 + X, 128:256]
                + ring[start + 2 : start + 2 + X, 256:384]
            )
            hidden = silu(total)
            hidden_ext[pl.ds(row(q, 1, y), X, stride=SLOT), :] = jnp.where(
                sided[side], hidden, jnp.zeros_like(hidden)
            )


def plane_sum(shifted, p):
    n = X * Y
    return (
        shifted[p, 0:n, 0:128]
        + shifted[p, Y : Y + n, 128:256]
        + shifted[p, 2 * Y : 2 * Y + n, 256:384]
    )


def conv_pair(shifted, columns, sums, p):
    sums[...] = plane_sum(shifted, p)
    for side, y in ((0, 0), (1, Y - 1)):
        extra = (
            columns[side, p, 7:15, 0:128]
            + columns[side, p, 8:16, 128:256]
            + columns[side, p, 9:17, 256:384]
        )
        place = pl.ds(y, X, stride=Y)
        sums[place, :] = sums[place, :] + extra
    return sums[...]


TAPS = ((1, 0), (2, 1), (None, 2), (0, None))


def piece(weight, tap):
    return jnp.zeros((C, C), BF16) if tap is None else weight[tap]


def forward_weight(weight, banded):
    for dy in range(3):
        for slot in range(4):
            rows = slice(dy * 256 + slot * C, dy * 256 + slot * C + C)
            for dx in range(3):
                pieces = [
                    piece(weight, None if t is None else (dx * 3 + dy) * 3 + t) for t in TAPS[slot]
                ]
                banded[rows, dx * 128 : dx * 128 + 128] = jnp.concatenate(pieces, axis=1)


def backward_weight(weight, banded):
    for dx in range(3):
        for b in range(2):
            rows = slice(dx * 128 + b * C, dx * 128 + b * C + C)
            for dy in range(3):
                for half in range(2):
                    pieces = []
                    for slot in (2 * half, 2 * half + 1):
                        t = TAPS[slot][b]
                        tap = None if t is None else ((2 - dx) * 3 + 2 - dy) * 3 + 2 - t
                        pieces.append(piece(weight, tap))
                    start = dy * 256 + half * 128
                    banded[rows, start : start + 128] = jnp.concatenate(pieces, axis=1)


def kernel_grad(ext, turned, packed, g, finished):
    low = low_lanes(192)
    turned_value = turned[...]

    def moving(tap):
        dx, dy = tap // 3, tap % 3
        blocks = [
            ext[pl.ds(row(q, x + dx, dy - 1), Y), :].astype(BF16) for q in range(Q) for x in range(X)
        ]
        return jnp.concatenate(blocks, axis=0)

    for pair in range(PAIRS):
        first = 2 * pair
        if first + 1 < 9:
            rhs = jnp.concatenate([moving(first), moving(first + 1)], axis=1)
        else:
            rhs = moving(first)
        result = jnp.dot(turned_value, rhs, preferred_element_type=F32)
        one = result[:, 0:128]
        two = result[:, 128:256] if first + 1 < 9 else jnp.zeros_like(one)
        straight = jnp.where(low, one[0:192], two[64:256])
        crossed = jnp.where(low, two[0:192], one[64:256])
        total = straight + pltpu.roll(crossed, 64, 1)
        packed[g, pair * 192 : pair * 192 + 192, :] = total.astype(BF16)
        finished(pair)


def turn(turned, q, block):
    flat = block.astype(F32).T.astype(BF16)
    columns = lambda w: slice(w * 128, w * 128 + 128)
    turned[64:192, columns(q)] = flat
    if q + 1 < Q:
        turned[0:64, columns(q + 1)] = flat[64:128]
    else:
        turned[192:256, columns(q)] = jnp.zeros((64, 128), BF16)
    if q > 0:
        turned[192:256, columns(q - 1)] = flat[0:64]
    else:
        turned[0:64, columns(q)] = jnp.zeros((64, 128), BF16)


def step(
    sizes,
    field_hbm, first_hbm, second_hbm, cotangent_hbm,
    output, full,
    field, first, second, cotangent, load_sems, shifted, shifted_c,
    ext_f, ext_c, ext_h, wide, thin, columns, sums,
    banded_1, banded_2, banded_t, turned_c, turned_p, slope,
    send_xf, send_yf, send_cf, land_xf, land_yf, land_cf, corner_f,
    send_xc, send_yc, send_cc, land_xc, land_yc, land_cc, corner_c, ring,
    packed, gathered_xy, own_sum, pass_out, pass_in, gathered_z,
    halo_send, halo_recv, pass_send, pass_recv, xy_send, xy_recv, z_send, z_recv,
    back_xy_send, back_xy_recv, share_send, share_recv,
):
    nx, ny, ng = sizes
    zl = ng // 2
    nz = nx * zl
    chunk = gathered_xy.shape[2]
    owners = PACKED // chunk
    loads = [
        pltpu.make_async_copy(source, target, load_sems.at[number])
        for number, (source, target) in enumerate(
            ((field_hbm, field), (cotangent_hbm, cotangent), (first_hbm, first), (second_hbm, second))
        )
    ]
    for load in loads:
        load.start()
    gx, gy, grp = lax.axis_index("gx"), lax.axis_index("gy"), lax.axis_index("grp")
    core = lax.rem(grp, 2)
    z = gx * zl + grp // 2
    me = (gx, gy, grp)
    sibling = (gx, gy, grp + 1 - 2 * core)

    def along_xy(k):
        return lax.rem(gy + k, ny)

    def along_z(k):
        return lax.rem(z + k, nz)

    def z_device(target):
        return (target // zl, gy, 2 * lax.rem(target, zl) + core)

    barrier = pltpu.get_barrier_semaphore()

    def greet(device):
        pl.semaphore_signal(barrier, inc=1, device_id=device, device_id_type=MESH)

    greet((1 - gx, along_xy(1), grp))
    greet((1 - gx, along_xy(ny - 1), grp))
    greet(sibling)

    @pl.loop(1, nz)
    def _(k):
        greet(z_device(along_z(k)))

    @pl.loop(1, ny)
    def _(k):
        greet((gx, along_xy(k), grp))

    place = (gx, gy, grp)
    sided = (gy > 0, gy < ny - 1)
    far = (XE - 1) * (1 - gx)
    ends = (
        (send_xf, send_yf, send_cf, land_xf, land_yf, land_cf),
        (send_xc, send_yc, send_cc, land_xc, land_yc, land_cc),
    )
    corners = (corner_f, corner_c)
    halos = [
        halo_copies(ends[number], halo_send.at[number], halo_recv.at[number], place, ny)
        for number in range(2)
    ]

    def dispatch(number, ext):
        take_edges(ext, *ends[number][:3], corners[number], gx)
        if number == 0:
            pl.semaphore_wait(barrier, nz - 1 + ny - 1 + 3)
        for copy in halos[number]:
            copy.start()

    def arrive(number, ext, then_y, then_x):
        land_x, land_y, land_c = ends[number][3:]
        for which in (3, 4):
            halos[number][which].wait_recv()
        insert_y(ext, land_y, sided)
        then_y()
        for which in (0, 1, 2):
            halos[number][which].wait_recv()
        insert_x(ext, land_x, land_c, sided, far, corners[number])
        then_x()

    def load_own(ext, source):
        for x in range(X):
            for q in range(Q):
                ext[pl.ds(row(q, x + 1, 0), Y), :] = source[0, x, :, q * 128 : q * 128 + 128].astype(F32)

    clear_halo(ext_f, shifted)
    loads[0].wait()
    load_own(ext_f, field)
    dispatch(0, ext_f)
    clear_halo(ext_c, shifted_c)
    loads[1].wait()
    load_own(ext_c, cotangent)
    dispatch(1, ext_c)

    loads[2].wait()
    forward_weight(first, banded_1)
    conv_own(ext_f, wide, banded_1, shifted, False)
    columns[...] = jnp.zeros_like(columns)
    loads[3].wait()
    backward_weight(second, banded_t)
    for q in range(Q):
        turn(turned_c, q, cotangent[0, :, :, q * 128 : q * 128 + 128].reshape(X * Y, 128))

    conv_own(ext_c, wide, banded_t, shifted_c, True)
    forward_weight(second, banded_2)
    clear_halo(ext_h, None)

    arrive(
        0, ext_f,
        lambda: conv_y(ext_f, banded_1, columns, False),
        lambda: conv_x(ext_f, thin, banded_1, shifted, False, far),
    )

    for p in range(Q):
        value = conv_pair(shifted, columns, sums, p)
        sigma = jax.nn.sigmoid(value)
        hidden = (value * sigma).astype(BF16).astype(F32)
        slope[p] = sigma * (1.0 + value * (1.0 - sigma))
        for x in range(X):
            ext_h[pl.ds(row(p, x + 1, 0), Y), :] = hidden[x * Y : x * Y + Y]
    ring_x(ext_f, ext_h, banded_1, sided, gx, far)
    ring_y(ext_f, ext_h, banded_1, ring, sided)

    owner = gy < owners

    def scatter(g):
        def finished(pair):
            for j in range(owners):
                if not pair * 192 < (j + 1) * chunk <= (pair + 1) * 192:
                    continue

                @pl.when(gy != j)
                def _():
                    pltpu.make_async_remote_copy(
                        src_ref=packed.at[g, pl.ds(j * chunk, chunk)], dst_ref=gathered_xy.at[g, gy],
                        send_sem=xy_send.at[g], recv_sem=xy_recv.at[g],
                        device_id=(gx, j, grp), device_id_type=MESH,
                    ).start()

        return finished

    kernel_grad(ext_h, turned_c, packed, 1, scatter(1))
    arrive(
        1, ext_c,
        lambda: conv_y(ext_c, banded_t, columns, True),
        lambda: conv_x(ext_c, thin, banded_t, shifted_c, True, far),
    )
    for p in range(Q):
        hidden_grad = conv_pair(shifted_c, columns, sums, p)
        turn(turned_p, p, (hidden_grad * slope[p]).astype(BF16))
    kernel_grad(ext_f, turned_p, packed, 0, scatter(0))

    conv_own(ext_h, wide, banded_2, shifted, False)
    conv_x(ext_h, thin, banded_2, shifted, False, far)
    for p in range(Q):
        value = plane_sum(shifted, p).astype(BF16)
        output[0, :, :, p * 128 : p * 128 + 128] = value.reshape(X, Y, 128)

    def rows_of(j):
        return pl.ds(pl.multiple_of(j * chunk, 16), chunk)

    def several(g, count):
        part = gathered_xy.at[g, pl.ds(0, count)]
        return pltpu.make_async_remote_copy(
            src_ref=part, dst_ref=part, send_sem=xy_send.at[g], recv_sem=xy_recv.at[g],
            device_id=me, device_id_type=MESH,
        )

    pass_on = pltpu.make_async_remote_copy(
        src_ref=pass_out, dst_ref=pass_in, send_sem=pass_send, recv_sem=pass_recv,
        device_id=sibling, device_id_type=MESH,
    )

    for g in (1, 0):

        @pl.when(owner)
        def _():
            several(g, ny - 1).wait_recv()
            gathered_xy[g, gy] = packed[g, rows_of(gy), :]
            total = gathered_xy[g, 0].astype(F32)
            for k in range(1, ny):
                total = total + gathered_xy[g, k].astype(F32)

            @pl.when(core == 1 - g)
            def _():
                pass_out[...] = total
                pass_on.start()

            @pl.when(core == g)
            def _():
                own_sum[...] = total
                pass_on.wait_recv()
                gathered_z[z] = (own_sum[...] + pass_in[...]).astype(BF16)

                @pl.loop(1, nz)
                def _(k):
                    pltpu.make_async_remote_copy(
                        src_ref=gathered_z.at[z], dst_ref=gathered_z.at[z],
                        send_sem=z_send, recv_sem=z_recv,
                        device_id=z_device(along_z(k)), device_id_type=MESH,
                    ).start()

    def share(j):
        pltpu.make_async_remote_copy(
            src_ref=full.at[core, rows_of(j)], dst_ref=full.at[core, rows_of(j)],
            send_sem=share_send, recv_sem=share_recv,
            device_id=sibling, device_id_type=MESH,
        ).start()

    others = gathered_z.at[pl.ds(0, nz - 1)]
    z_all = pltpu.make_async_remote_copy(
        src_ref=others, dst_ref=others, send_sem=z_send, recv_sem=z_recv,
        device_id=me, device_id_type=MESH,
    )

    @pl.when(owner)
    def _():
        z_all.wait_recv()
        grand = gathered_z[0].astype(F32)
        for k in range(1, nz):
            grand = grand + gathered_z[k].astype(F32)
        rows = lax.broadcasted_iota(jnp.int32, (128, 128), 0)
        lanes = lax.broadcasted_iota(jnp.int32, (128, 128), 1)
        unit = (rows == lanes).astype(BF16)
        turned = []
        for start in range(0, chunk, C):
            block = lax.dot_general(
                unit, grand[start : start + C].astype(BF16), (((1,), (1,)), ((), ())),
                preferred_element_type=F32,
            )
            turned.append(jnp.concatenate([block[0:C], block[C : 2 * C]], axis=1))
        full[core, rows_of(gy), :] = jnp.concatenate(turned, axis=0).astype(BF16)

        @pl.loop(1, ny)
        def _(k):
            pltpu.make_async_remote_copy(
                src_ref=full.at[core, rows_of(gy)], dst_ref=full.at[core, rows_of(gy)],
                send_sem=back_xy_send, recv_sem=back_xy_recv.at[k],
                device_id=(gx, along_xy(k), grp), device_id_type=MESH,
            ).start()

        share(gy)

    @pl.loop(1, ny)
    def _(k):
        j = along_xy(ny - k)

        @pl.when(j < owners)
        def _():
            pltpu.make_async_remote_copy(
                src_ref=full.at[core, rows_of(j)], dst_ref=full.at[core, rows_of(j)],
                send_sem=back_xy_send, recv_sem=back_xy_recv.at[k],
                device_id=me, device_id_type=MESH,
            ).wait_recv()
            share(j)

    whole = pltpu.make_async_remote_copy(
        src_ref=full.at[core], dst_ref=full.at[1 - core], send_sem=share_send, recv_sem=share_recv,
        device_id=sibling, device_id_type=MESH,
    )
    whole.wait_recv()

    for number in range(2):
        for copy in halos[number]:
            copy.wait_send()

    @pl.when(owner)
    def _():
        for g in range(2):
            several(g, owners - 1).wait_send()
        pass_on.wait_send()
        z_all.wait_send()
        pltpu.make_async_remote_copy(
            src_ref=gathered_xy.at[0, pl.ds(0, ny - 1)], dst_ref=gathered_xy.at[0, pl.ds(0, ny - 1)],
            send_sem=back_xy_send, recv_sem=share_recv,
            device_id=me, device_id_type=MESH,
        ).wait_send()

    if owners < ny:

        @pl.when(jnp.logical_not(owner))
        def _():
            for g in range(2):
                several(g, owners).wait_send()

    whole.wait_send()


def unpack(factor, output_in, full, output, first_out, second_out, one, two, sems):
    copies = [
        pltpu.make_async_copy(source, target, sems.at[number])
        for number, (source, target) in enumerate(
            ((output_in, output), (one, first_out), (two, second_out))
        )
    ]
    copies[0].start()
    for g, target in ((0, one), (1, two)):
        for pair in range(PAIRS):
            for v in range(3):
                start = (pair * 3 + v) * C
                block = full[g, start : start + C, :].astype(F32) * factor
                target[2 * pair * 3 + 2 - v] = block[:, 0:C]
                if 2 * pair + 1 < 9:
                    target[(2 * pair + 1) * 3 + 2 - v] = block[:, C : 2 * C]
        copies[g + 1].start()
    for copy in copies:
        copy.wait()


def halo_buffers(deep):
    ends = [
        pltpu.VMEM((deep, Y, 1024), BF16),
        pltpu.VMEM((2, deep, X, 1024), BF16),
        pltpu.VMEM((2, deep * deep, Q, 128), BF16),
    ]
    return ends + ends + [pltpu.VMEM((2, deep * deep, Q, 128), F32)]


def shards(sizes, field_in, first_weight, second_weight, cotangent):
    nx, ny, ng = sizes
    nz = nx * ng // 2
    chunk = C * pl.cdiv(PACKED, C * ny)
    assert PACKED % chunk == 0
    rows = PACKED
    total = ng * nx * X * ny * Y * NZ
    dma = pltpu.SemaphoreType.DMA
    vmem = pltpu.VMEM
    inside = pl.BlockSpec(memory_space=pltpu.VMEM)
    outside = pl.BlockSpec(memory_space=pltpu.HBM)
    cells = (Q * PLANES * SLOT + 2 * MARGIN, 128)
    sums = (Q, ROWS_E, 384)
    weight = (27, C, C)
    output, full = pl.pallas_call(
        functools.partial(step, sizes),
        out_shape=(
            jax.ShapeDtypeStruct(field_in.shape, BF16),
            jax.ShapeDtypeStruct((2, rows, 128), BF16),
        ),
        in_specs=[outside] * 4,
        out_specs=(inside,) * 2,
        scratch_shapes=[
            vmem(field_in.shape, BF16), vmem(weight, BF16), vmem(weight, BF16), vmem(field_in.shape, BF16),
            dma((4,)), vmem(sums, F32), vmem(sums, F32),
            vmem(cells, F32), vmem(cells, F32), vmem(cells, F32),
            vmem((Q, X * Y, 768), BF16), vmem((Q * Y, 768), BF16), vmem((2, Q, 24, 384), F32), vmem((X * Y, 128), F32),
            vmem((768, 384), BF16), vmem((768, 384), BF16), vmem((384, 768), BF16),
            vmem((256, Q * 128), BF16), vmem((256, Q * 128), BF16),
            vmem((Q, X * Y, 128), F32),
            *halo_buffers(2), *halo_buffers(1), vmem((Q * PLANES, 384), F32),
            vmem((2, rows, 128), BF16), vmem((2, ny, chunk, 128), BF16),
            vmem((chunk, 128), F32), vmem((chunk, 128), F32), vmem((chunk, 128), F32), vmem((nz, chunk, 128), BF16),
            dma((2, 5)), dma((2, 5)), dma, dma, dma((2,)), dma((2,)), dma, dma,
            dma, dma((ny,)), dma, dma,
        ],
        compiler_params=pltpu.CompilerParams(
            collective_id=0, has_side_effects=True, vmem_limit_bytes=40 * 1024 * 1024
        ),
    )(
        *(
            pltpu.with_memory_space_constraint(array, pltpu.HBM)
            for array in (
                field_in,
                first_weight.reshape(weight),
                second_weight.reshape(weight),
                cotangent,
            )
        )
    )
    output, first_grad, second_grad = pl.pallas_call(
        functools.partial(unpack, 1.0 / math.sqrt(total)),
        out_shape=(
            jax.ShapeDtypeStruct(field_in.shape, BF16),
            jax.ShapeDtypeStruct(weight, F32),
            jax.ShapeDtypeStruct(weight, F32),
        ),
        in_specs=[inside] * 2,
        out_specs=(outside,) * 3,
        scratch_shapes=[vmem(weight, F32), vmem(weight, F32), dma((3,))],
        compiler_params=pltpu.CompilerParams(vmem_limit_bytes=16 * 1024 * 1024),
    )(output, full)
    shape = (3, 3, 3, C, C)
    return output, first_grad.reshape(shape), second_grad.reshape(shape)


def solution(mesh):
    sizes = (mesh.shape["gx"], mesh.shape["gy"], mesh.shape["grp"])
    return jax.shard_map(
        functools.partial(shards, sizes),
        mesh=mesh,
        in_specs=(P("grp", "gx", "gy", None), P(), P(), P("grp", "gx", "gy", None)),
        out_specs=(P("grp", "gx", "gy", None), P(), P()),
        check_vma=False,
    )
```

```python
import functools
import math

import jax
import jax.numpy as jnp
from jax import lax
from jax.experimental import pallas as pl
from jax.experimental.pallas import tpu as pltpu
from jax.sharding import PartitionSpec as P

C = 64
NZ = 16
X = 8
Y = 16
Q = 8
XE = X + 2
PLANES = 16
FAR = 10
SLOT = 32
MARGIN = 8
ROWS_E = XE * Y
PAIRS = 5
PACKED = PAIRS * 192
F32 = jnp.float32
BF16 = jnp.bfloat16
MESH = pl.DeviceIdType.MESH


def low_lanes(rows):
    return lax.broadcasted_iota(jnp.int32, (rows, 128), 1) < 64


def row(q, x, y):
    return (q * PLANES + x) * SLOT + MARGIN + 8 + y


def clear_halo(ext, shifted):
    edge = jnp.zeros((8, 128), F32)
    plane = jnp.zeros((SLOT, 128), F32)
    for q in range(Q):
        for x in range(XE):
            if x in (0, XE - 1):
                ext[pl.ds(row(q, x, -8), SLOT), :] = plane
            else:
                ext[pl.ds(row(q, x, -8), 8), :] = edge
                ext[pl.ds(row(q, x, Y), 8), :] = edge
        if shifted is not None:
            shifted[q, 0:Y, :] = jnp.zeros((Y, 384), F32)
            shifted[q, ROWS_E - Y : ROWS_E, :] = jnp.zeros((Y, 384), F32)


def take_edges(ext, send_x, send_y, send_c, corner, gx):
    deep = send_x.shape[0]
    for q in range(Q):
        columns = slice(q * 128, q * 128 + 128)
        for d in range(deep):
            near = (X - d) - (X - 1 - 2 * d) * gx
            plane = ext[pl.ds(pl.multiple_of(row(q, near, 0), 8), Y), :]
            send_x[d, :, columns] = plane.astype(BF16)
            for e in range(deep):
                corner[0, d * deep + e, q : q + 1, :] = plane[e : e + 1]
                corner[1, d * deep + e, q : q + 1, :] = plane[Y - 1 - e : Y - e]
        for e in range(deep):
            for side, y in ((0, e), (1, Y - 1 - e)):
                send_y[side, e, :, columns] = ext[pl.ds(row(q, 1, y), X, stride=SLOT), :].astype(BF16)
    send_c[...] = corner[...].astype(BF16)


def halo_copies(ends, send_sems, recv_sems, place, count):
    send_x, send_y, send_c, land_x, land_y, land_c = ends
    gx, gy, grp = place
    up = lax.rem(gy + 1, count)
    down = lax.rem(gy + count - 1, count)
    moves = (
        (send_c.at[1], land_c.at[0], (1 - gx, up, grp)),
        (send_c.at[0], land_c.at[1], (1 - gx, down, grp)),
        (send_x, land_x, (1 - gx, gy, grp)),
        (send_y.at[1], land_y.at[0], (gx, up, grp)),
        (send_y.at[0], land_y.at[1], (gx, down, grp)),
    )
    return [
        pltpu.make_async_remote_copy(
            src_ref=source, dst_ref=target, send_sem=send_sems.at[number], recv_sem=recv_sems.at[number],
            device_id=device, device_id_type=MESH,
        )
        for number, (source, target, device) in enumerate(moves)
    ]


def insert_y(ext, land_y, sided):
    for e in range(land_y.shape[1]):
        for side, y in ((0, -1 - e), (1, Y + e)):
            for q in range(Q):
                value = land_y[side, e, :, q * 128 : q * 128 + 128].astype(F32)
                value = jnp.where(sided[side], value, jnp.zeros_like(value))
                ext[pl.ds(row(q, 1, y), X, stride=SLOT), :] = value


def insert_x(ext, land_x, land_c, sided, far, corner):
    deep = land_x.shape[0]
    corner[...] = land_c[...].astype(F32)
    rows = lax.broadcasted_iota(jnp.int32, (8, 128), 0)
    for d in range(deep):
        plane = far if d == 0 else FAR
        for q in range(Q):
            start = pl.multiple_of(row(q, plane, 0), 8)
            ext[pl.ds(start, Y), :] = land_x[d, :, q * 128 : q * 128 + 128].astype(F32)
            low = jnp.zeros((8, 128), F32)
            high = jnp.zeros((8, 128), F32)
            for e in range(deep):
                cell = d * deep + e
                low = jnp.where((rows == 7 - e) & sided[0], corner[0, cell, q : q + 1, :], low)
                high = jnp.where((rows == e) & sided[1], corner[1, cell, q : q + 1, :], high)
            ext[pl.ds(start - 8, 8), :] = low
            ext[pl.ds(start + Y, 8), :] = high


def operand(values, low):
    zero = jnp.zeros_like(values[0])
    padded = [zero] + values + [zero]
    return [
        (padded[q + 1].astype(BF16), jnp.where(low, padded[q + 2], padded[q]).astype(BF16))
        for q in range(Q)
    ]


def conv_own(ext, wide, banded, shifted, flipped):
    low = low_lanes(Y)
    for x in range(X):
        for dy in range(3):
            values = [ext[pl.ds(row(q, x + 1, dy - 1), Y), :] for q in range(Q)]
            for q, (own, mixed) in enumerate(operand(values, low)):
                wide[q, x * Y : x * Y + Y, dy * 256 : dy * 256 + 128] = own
                wide[q, x * Y : x * Y + Y, dy * 256 + 128 : dy * 256 + 256] = mixed
    dims = (((1,), (1 if flipped else 0,)), ((), ()))
    result = lax.dot_general(
        wide[...].reshape(Q * X * Y, 768), banded[...], dims, preferred_element_type=F32
    )
    shifted[:, Y : Y + X * Y, :] = result.reshape(Q, X * Y, 384)


def conv_y(ext, banded, columns, flipped):
    low = low_lanes(X)
    for side, y, dy in ((0, -1, 0), (1, Y, 2)):
        values = [ext[pl.ds(row(q, 1, y), X, stride=SLOT), :] for q in range(Q)]
        padded = [jnp.zeros((X, 128), F32)] + values + [jnp.zeros((X, 128), F32)]
        own = jnp.concatenate(values, axis=0)
        mixed = jnp.concatenate([jnp.where(low, padded[q + 2], padded[q]) for q in range(Q)], axis=0)
        rows = jnp.concatenate([own, mixed], axis=1).astype(BF16)
        if flipped:
            weight = banded[:, dy * 256 : dy * 256 + 256]
        else:
            weight = banded[dy * 256 : dy * 256 + 256, :]
        dims = (((1,), (1 if flipped else 0,)), ((), ()))
        result = lax.dot_general(rows, weight, dims, preferred_element_type=F32)
        for q in range(Q):
            columns[side, q, 8:16, :] = result[q * X : q * X + X]


def conv_x(ext, thin, banded, flipped, gx, far):
    low = low_lanes(Y)
    for dy in range(3):
        values = [
            ext[pl.ds(pl.multiple_of(row(q, far, 0), 8) + dy - 1, Y), :] for q in range(Q)
        ]
        for q, (own, mixed) in enumerate(operand(values, low)):
            thin[q * Y : q * Y + Y, dy * 256 : dy * 256 + 128] = own
            thin[q * Y : q * Y + Y, dy * 256 + 128 : dy * 256 + 256] = mixed
    tap = pl.ds(pl.multiple_of((1 - gx) * 256, 128), 128)
    weight = banded[tap, :] if flipped else banded[:, tap]
    dims = (((1,), (1 if flipped else 0,)), ((), ()))
    return lax.dot_general(thin[...], weight, dims, preferred_element_type=F32)


def add_plane(sums, added, gx):
    edge = pl.ds(pl.multiple_of((X - 1) * (1 - gx) * Y, Y), Y)
    for q in range(Q):
        sums[q, edge, :] = sums[q, edge, :] + added[q * Y : q * Y + Y]


def silu(value):
    return (value * jax.nn.sigmoid(value)).astype(BF16).astype(F32)


def lanes_of(values, low):
    padded = [jnp.zeros_like(values[0])] + values + [jnp.zeros_like(values[0])]
    own = jnp.concatenate(values, axis=0)
    mixed = jnp.concatenate([jnp.where(low, padded[q + 2], padded[q]) for q in range(Q)], axis=0)
    return [own.astype(BF16), mixed.astype(BF16)]


def ring_x(ext, hidden_ext, banded, sided, gx, far):
    low = low_lanes(SLOT)
    total = jnp.zeros((Q * SLOT, 128), F32)
    for dx, plane in enumerate((X + 2 * gx, far, FAR - (XE - 1) * gx)):
        parts = []
        for dy in range(3):
            starts = [pl.multiple_of(row(q, plane, -8), 8) + dy - 1 for q in range(Q)]
            parts += lanes_of([ext[pl.ds(start, SLOT), :] for start in starts], low)
        total = total + jnp.dot(
            jnp.concatenate(parts, axis=1), banded[:, dx * 128 : dx * 128 + 128], preferred_element_type=F32
        )
    hidden = silu(total)
    y = lax.broadcasted_iota(jnp.int32, (SLOT, 128), 0) - 8
    inside = ((y >= 0) & (y < Y)) | ((y == -1) & sided[0]) | ((y == Y) & sided[1])
    for q in range(Q):
        part = hidden[q * SLOT : q * SLOT + SLOT]
        hidden_ext[pl.ds(pl.multiple_of(row(q, far, -8), 8), SLOT), :] = jnp.where(inside, part, jnp.zeros_like(part))


def ring_y(ext, hidden_ext, banded, ring, sided):
    low = low_lanes(PLANES)
    for side, y in ((0, -1), (1, Y)):
        parts = []
        for dy in range(3):
            parts += lanes_of(
                [ext[pl.ds(row(q, 0, y + dy - 1), PLANES, stride=SLOT), :] for q in range(Q)], low
            )
        ring[...] = jnp.dot(jnp.concatenate(parts, axis=1), banded[...], preferred_element_type=F32)
        for q in range(Q):
            start = q * PLANES
            total = (
                ring[start : start + X, 0:128]
                + ring[start + 1 : start + 1 + X, 128:256]
                + ring[start + 2 : start + 2 + X, 256:384]
            )
            hidden = silu(total)
            hidden_ext[pl.ds(row(q, 1, y), X, stride=SLOT), :] = jnp.where(
                sided[side], hidden, jnp.zeros_like(hidden)
            )


def plane_sum(shifted, p):
    n = X * Y
    return (
        shifted[p, 0:n, 0:128]
        + shifted[p, Y : Y + n, 128:256]
        + shifted[p, 2 * Y : 2 * Y + n, 256:384]
    )


def conv_sum(shifted, columns, sums, p):
    sums[p] = plane_sum(shifted, p)
    if columns is None:
        return
    for side, y in ((0, 0), (1, Y - 1)):
        extra = (
            columns[side, p, 7:15, 0:128]
            + columns[side, p, 8:16, 128:256]
            + columns[side, p, 9:17, 256:384]
        )
        place = pl.ds(y, X, stride=Y)
        sums[p, place, :] = sums[p, place, :] + extra


TAPS = ((1, 0), (2, 1), (None, 2), (0, None))


def piece(weight, tap):
    return jnp.zeros((C, C), BF16) if tap is None else weight[tap]


def forward_weight(weight, banded):
    for dy in range(3):
        for slot in range(4):
            rows = slice(dy * 256 + slot * C, dy * 256 + slot * C + C)
            for dx in range(3):
                pieces = [
                    piece(weight, None if t is None else (dx * 3 + dy) * 3 + t) for t in TAPS[slot]
                ]
                banded[rows, dx * 128 : dx * 128 + 128] = jnp.concatenate(pieces, axis=1)


def backward_weight(weight, banded):
    for dx in range(3):
        for b in range(2):
            rows = slice(dx * 128 + b * C, dx * 128 + b * C + C)
            for dy in range(3):
                for half in range(2):
                    pieces = []
                    for slot in (2 * half, 2 * half + 1):
                        t = TAPS[slot][b]
                        tap = None if t is None else ((2 - dx) * 3 + 2 - dy) * 3 + 2 - t
                        pieces.append(piece(weight, tap))
                    start = dy * 256 + half * 128
                    banded[rows, start : start + 128] = jnp.concatenate(pieces, axis=1)


def kernel_grad(ext, turned, packed, g, finished):
    low = low_lanes(192)
    turned_value = turned[...]

    def moving(tap):
        dx, dy = tap // 3, tap % 3
        blocks = [
            ext[pl.ds(row(q, x + dx, dy - 1), Y), :].astype(BF16) for q in range(Q) for x in range(X)
        ]
        return jnp.concatenate(blocks, axis=0)

    for pair in range(PAIRS):
        first = 2 * pair
        if first + 1 < 9:
            rhs = jnp.concatenate([moving(first), moving(first + 1)], axis=1)
        else:
            rhs = moving(first)
        result = jnp.dot(turned_value, rhs, preferred_element_type=F32)
        one = result[:, 0:128]
        two = result[:, 128:256] if first + 1 < 9 else jnp.zeros_like(one)
        straight = jnp.where(low, one[0:192], two[64:256])
        crossed = jnp.where(low, two[0:192], one[64:256])
        total = straight + pltpu.roll(crossed, 64, 1)
        packed[g, pair * 192 : pair * 192 + 192, :] = total.astype(BF16)
        finished(pair)


def turn(turned, q, block):
    flat = block.astype(F32).T.astype(BF16)
    columns = lambda w: slice(w * 128, w * 128 + 128)
    turned[64:192, columns(q)] = flat
    if q + 1 < Q:
        turned[0:64, columns(q + 1)] = flat[64:128]
    else:
        turned[192:256, columns(q)] = jnp.zeros((64, 128), BF16)
    if q > 0:
        turned[192:256, columns(q - 1)] = flat[0:64]
    else:
        turned[0:64, columns(q)] = jnp.zeros((64, 128), BF16)


def step(
    sizes,
    field_hbm, first_hbm, second_hbm, cotangent_hbm,
    output, full,
    field, first, second, cotangent, load_sems, shifted, shifted_c,
    ext_f, ext_c, ext_h, wide, thin, columns, columns_c, pre, sums_c,
    banded_1, banded_2, banded_t, turned_c, turned_p, slope,
    send_xf, send_yf, send_cf, land_xf, land_yf, land_cf, corner_f,
    send_xc, send_yc, send_cc, land_xc, land_yc, land_cc, corner_c, ring,
    packed, gathered_xy, own_sum, pass_out, pass_in, gathered_z,
    halo_send, halo_recv, pass_send, pass_recv, xy_send, xy_recv, z_send, z_recv,
    back_xy_send, back_xy_recv, share_send, share_recv,
):
    nx, ny, ng = sizes
    zl = ng // 2
    nz = nx * zl
    chunk = gathered_xy.shape[2]
    owners = PACKED // chunk
    loads = [
        pltpu.make_async_copy(source, target, load_sems.at[number])
        for number, (source, target) in enumerate(
            ((field_hbm, field), (cotangent_hbm, cotangent), (first_hbm, first), (second_hbm, second))
        )
    ]
    for load in loads:
        load.start()
    gx, gy, grp = lax.axis_index("gx"), lax.axis_index("gy"), lax.axis_index("grp")
    core = lax.rem(grp, 2)
    z = gx * zl + grp // 2
    me = (gx, gy, grp)
    sibling = (gx, gy, grp + 1 - 2 * core)

    def along_xy(k):
        return lax.rem(gy + k, ny)

    def along_z(k):
        return lax.rem(z + k, nz)

    def z_device(target):
        return (target // zl, gy, 2 * lax.rem(target, zl) + core)

    barrier = pltpu.get_barrier_semaphore()

    def greet(device):
        pl.semaphore_signal(barrier, inc=1, device_id=device, device_id_type=MESH)

    greet((1 - gx, along_xy(1), grp))
    greet((1 - gx, along_xy(ny - 1), grp))
    greet((1 - gx, gy, grp))
    greet((gx, along_xy(1), grp))
    greet((gx, along_xy(ny - 1), grp))
    greet(sibling)
    for k in range(1, nz):
        if k != zl:
            greet(z_device(along_z(k)))

    @pl.loop(2, ny - 1)
    def _(k):
        greet((gx, along_xy(k), grp))

    place = (gx, gy, grp)
    sided = (gy > 0, gy < ny - 1)
    far = (XE - 1) * (1 - gx)
    ends = (
        (send_xf, send_yf, send_cf, land_xf, land_yf, land_cf),
        (send_xc, send_yc, send_cc, land_xc, land_yc, land_cc),
    )
    corners = (corner_f, corner_c)
    halos = [
        halo_copies(ends[number], halo_send.at[number], halo_recv.at[number], place, ny)
        for number in range(2)
    ]

    def dispatch(number, ext):
        take_edges(ext, *ends[number][:3], corners[number], gx)
        if number == 0:
            pl.semaphore_wait(barrier, nz - 1 + ny - 1 + 3)
        for copy in halos[number]:
            copy.start()

    def arrive_y(number, ext):
        for which in (3, 4):
            halos[number][which].wait_recv()
        insert_y(ext, ends[number][4], sided)

    def arrive_x(number, ext):
        for which in (0, 1, 2):
            halos[number][which].wait_recv()
        insert_x(ext, ends[number][3], ends[number][5], sided, far, corners[number])

    def load_own(ext, source):
        for x in range(X):
            for q in range(Q):
                ext[pl.ds(row(q, x + 1, 0), Y), :] = source[0, x, :, q * 128 : q * 128 + 128].astype(F32)

    clear_halo(ext_f, shifted)
    loads[0].wait()
    load_own(ext_f, field)
    dispatch(0, ext_f)
    clear_halo(ext_c, shifted_c)
    loads[1].wait()
    load_own(ext_c, cotangent)
    dispatch(1, ext_c)

    loads[2].wait()
    forward_weight(first, banded_1)
    conv_own(ext_f, wide, banded_1, shifted, False)
    columns[...] = jnp.zeros_like(columns)
    columns_c[...] = jnp.zeros_like(columns_c)
    loads[3].wait()
    backward_weight(second, banded_t)
    for q in range(Q):
        turn(turned_c, q, cotangent[0, :, :, q * 128 : q * 128 + 128].reshape(X * Y, 128))

    conv_own(ext_c, wide, banded_t, shifted_c, True)
    forward_weight(second, banded_2)
    clear_halo(ext_h, None)

    def activate(value):
        sigma = jax.nn.sigmoid(value)
        return (value * sigma).astype(BF16).astype(F32), sigma * (1.0 + value * (1.0 - sigma))

    arrive_y(0, ext_f)
    conv_y(ext_f, banded_1, columns, False)
    for p in range(Q):
        conv_sum(shifted, columns, pre, p)
        hidden, slope[p] = activate(pre[p])
        for x in range(X):
            ext_h[pl.ds(row(p, x + 1, 0), Y), :] = hidden[x * Y : x * Y + Y]
    arrive_y(1, ext_c)
    conv_y(ext_c, banded_t, columns_c, True)
    for p in range(Q):
        conv_sum(shifted_c, columns_c, sums_c, p)

    arrive_x(0, ext_f)
    add_plane(pre, conv_x(ext_f, thin, banded_1, False, gx, far), gx)
    edge = (X - 1) * (1 - gx)
    edge_rows = pl.ds(pl.multiple_of(edge * Y, Y), Y)
    for p in range(Q):
        hidden, slope[p, edge_rows, :] = activate(pre[p, edge_rows, :])
        ext_h[pl.ds(pl.multiple_of(row(p, edge + 1, 0), 8), Y), :] = hidden
    ring_x(ext_f, ext_h, banded_1, sided, gx, far)
    ring_y(ext_f, ext_h, banded_1, ring, sided)

    owner = gy < owners

    def scatter(g):
        def finished(pair):
            for j in range(owners):
                if not pair * 192 < (j + 1) * chunk <= (pair + 1) * 192:
                    continue

                @pl.when(gy != j)
                def _():
                    pltpu.make_async_remote_copy(
                        src_ref=packed.at[g, pl.ds(j * chunk, chunk)], dst_ref=gathered_xy.at[g, gy],
                        send_sem=xy_send.at[g], recv_sem=xy_recv.at[g],
                        device_id=(gx, j, grp), device_id_type=MESH,
                    ).start()

        return finished

    kernel_grad(ext_h, turned_c, packed, 1, scatter(1))
    arrive_x(1, ext_c)
    add_plane(sums_c, conv_x(ext_c, thin, banded_t, True, gx, far), gx)
    for p in range(Q):
        turn(turned_p, p, (sums_c[p] * slope[p]).astype(BF16))

    kernel_grad(ext_f, turned_p, packed, 0, scatter(0))

    conv_own(ext_h, wide, banded_2, shifted, False)
    for p in range(Q):
        conv_sum(shifted, None, pre, p)
    add_plane(pre, conv_x(ext_h, thin, banded_2, False, gx, far), gx)
    for p in range(Q):
        output[0, :, :, p * 128 : p * 128 + 128] = pre[p].astype(BF16).reshape(X, Y, 128)

    def rows_of(j):
        return pl.ds(pl.multiple_of(j * chunk, 16), chunk)

    def several(g, count):
        part = gathered_xy.at[g, pl.ds(0, count)]
        return pltpu.make_async_remote_copy(
            src_ref=part, dst_ref=part, send_sem=xy_send.at[g], recv_sem=xy_recv.at[g],
            device_id=me, device_id_type=MESH,
        )

    pass_on = pltpu.make_async_remote_copy(
        src_ref=pass_out, dst_ref=pass_in, send_sem=pass_send, recv_sem=pass_recv,
        device_id=sibling, device_id_type=MESH,
    )

    for g in (1, 0):

        @pl.when(owner)
        def _():
            several(g, ny - 1).wait_recv()
            gathered_xy[g, gy] = packed[g, rows_of(gy), :]
            total = gathered_xy[g, 0].astype(F32)
            for k in range(1, ny):
                total = total + gathered_xy[g, k].astype(F32)

            @pl.when(core == 1 - g)
            def _():
                pass_out[...] = total
                pass_on.start()

            @pl.when(core == g)
            def _():
                own_sum[...] = total
                pass_on.wait_recv()
                gathered_z[z] = (own_sum[...] + pass_in[...]).astype(BF16)

                for k in sorted(range(1, nz), key=lambda k: -min(k, nz - k)):
                    pltpu.make_async_remote_copy(
                        src_ref=gathered_z.at[z], dst_ref=gathered_z.at[z],
                        send_sem=z_send, recv_sem=z_recv,
                        device_id=z_device(along_z(k)), device_id_type=MESH,
                    ).start()

    def share(j):
        pltpu.make_async_remote_copy(
            src_ref=full.at[core, rows_of(j)], dst_ref=full.at[core, rows_of(j)],
            send_sem=share_send, recv_sem=share_recv,
            device_id=sibling, device_id_type=MESH,
        ).start()

    by_distance = sorted(
        range(1, ny), key=lambda k: -(min(k // 4, 4 - k // 4) + min(k % 4, 4 - k % 4))
    )
    others = gathered_z.at[pl.ds(0, nz - 1)]
    z_all = pltpu.make_async_remote_copy(
        src_ref=others, dst_ref=others, send_sem=z_send, recv_sem=z_recv,
        device_id=me, device_id_type=MESH,
    )

    @pl.when(owner)
    def _():
        z_all.wait_recv()
        grand = gathered_z[0].astype(F32)
        for k in range(1, nz):
            grand = grand + gathered_z[k].astype(F32)
        rows = lax.broadcasted_iota(jnp.int32, (128, 128), 0)
        lanes = lax.broadcasted_iota(jnp.int32, (128, 128), 1)
        unit = (rows == lanes).astype(BF16)
        turned = []
        for start in range(0, chunk, C):
            block = lax.dot_general(
                unit, grand[start : start + C].astype(BF16), (((1,), (1,)), ((), ())),
                preferred_element_type=F32,
            )
            turned.append(jnp.concatenate([block[0:C], block[C : 2 * C]], axis=1))
        full[core, rows_of(gy), :] = jnp.concatenate(turned, axis=0).astype(BF16)

        for k in by_distance:
            pltpu.make_async_remote_copy(
                src_ref=full.at[core, rows_of(gy)], dst_ref=full.at[core, rows_of(gy)],
                send_sem=back_xy_send, recv_sem=back_xy_recv.at[k],
                device_id=(gx, along_xy(k), grp), device_id_type=MESH,
            ).start()

        share(gy)

    for k in reversed(by_distance):
        j = along_xy(ny - k)

        @pl.when(j < owners)
        def _(j=j, k=k):
            pltpu.make_async_remote_copy(
                src_ref=full.at[core, rows_of(j)], dst_ref=full.at[core, rows_of(j)],
                send_sem=back_xy_send, recv_sem=back_xy_recv.at[k],
                device_id=me, device_id_type=MESH,
            ).wait_recv()
            share(j)

    whole = pltpu.make_async_remote_copy(
        src_ref=full.at[core], dst_ref=full.at[1 - core], send_sem=share_send, recv_sem=share_recv,
        device_id=sibling, device_id_type=MESH,
    )
    whole.wait_recv()

    for number in range(2):
        for copy in halos[number]:
            copy.wait_send()

    @pl.when(owner)
    def _():
        for g in range(2):
            several(g, owners - 1).wait_send()
        pass_on.wait_send()
        z_all.wait_send()
        pltpu.make_async_remote_copy(
            src_ref=gathered_xy.at[0, pl.ds(0, ny - 1)], dst_ref=gathered_xy.at[0, pl.ds(0, ny - 1)],
            send_sem=back_xy_send, recv_sem=share_recv,
            device_id=me, device_id_type=MESH,
        ).wait_send()

    if owners < ny:

        @pl.when(jnp.logical_not(owner))
        def _():
            for g in range(2):
                several(g, owners).wait_send()

    whole.wait_send()


def unpack(factor, output_in, full, output, first_out, second_out, one, two, sems):
    copies = [
        pltpu.make_async_copy(source, target, sems.at[number])
        for number, (source, target) in enumerate(
            ((output_in, output), (one, first_out), (two, second_out))
        )
    ]
    copies[0].start()
    for g, target in ((0, one), (1, two)):
        for pair in range(PAIRS):
            for v in range(3):
                start = (pair * 3 + v) * C
                block = full[g, start : start + C, :].astype(F32) * factor
                target[2 * pair * 3 + 2 - v] = block[:, 0:C]
                if 2 * pair + 1 < 9:
                    target[(2 * pair + 1) * 3 + 2 - v] = block[:, C : 2 * C]
        copies[g + 1].start()
    for copy in copies:
        copy.wait()


def halo_buffers(deep):
    ends = [
        pltpu.VMEM((deep, Y, 1024), BF16),
        pltpu.VMEM((2, deep, X, 1024), BF16),
        pltpu.VMEM((2, deep * deep, Q, 128), BF16),
    ]
    return ends + ends + [pltpu.VMEM((2, deep * deep, Q, 128), F32)]


def shards(sizes, field_in, first_weight, second_weight, cotangent):
    nx, ny, ng = sizes
    nz = nx * ng // 2
    chunk = C * pl.cdiv(PACKED, C * ny)
    assert PACKED % chunk == 0
    rows = PACKED
    total = ng * nx * X * ny * Y * NZ
    dma = pltpu.SemaphoreType.DMA
    vmem = pltpu.VMEM
    inside = pl.BlockSpec(memory_space=pltpu.VMEM)
    outside = pl.BlockSpec(memory_space=pltpu.HBM)
    cells = (Q * PLANES * SLOT + 2 * MARGIN, 128)
    sums = (Q, ROWS_E, 384)
    weight = (27, C, C)
    output, full = pl.pallas_call(
        functools.partial(step, sizes),
        out_shape=(
            jax.ShapeDtypeStruct(field_in.shape, BF16),
            jax.ShapeDtypeStruct((2, rows, 128), BF16),
        ),
        in_specs=[outside] * 4,
        out_specs=(inside,) * 2,
        scratch_shapes=[
            vmem(field_in.shape, BF16), vmem(weight, BF16), vmem(weight, BF16), vmem(field_in.shape, BF16),
            dma((4,)), vmem(sums, F32), vmem(sums, F32),
            vmem(cells, F32), vmem(cells, F32), vmem(cells, F32),
            vmem((Q, X * Y, 768), BF16), vmem((Q * Y, 768), BF16), vmem((2, Q, 24, 384), F32), vmem((2, Q, 24, 384), F32),
            vmem((Q, X * Y, 128), F32), vmem((Q, X * Y, 128), F32),
            vmem((768, 384), BF16), vmem((768, 384), BF16), vmem((384, 768), BF16),
            vmem((256, Q * 128), BF16), vmem((256, Q * 128), BF16),
            vmem((Q, X * Y, 128), F32),
            *halo_buffers(2), *halo_buffers(1), vmem((Q * PLANES, 384), F32),
            vmem((2, rows, 128), BF16), vmem((2, ny, chunk, 128), BF16),
            vmem((chunk, 128), F32), vmem((chunk, 128), F32), vmem((chunk, 128), F32), vmem((nz, chunk, 128), BF16),
            dma((2, 5)), dma((2, 5)), dma, dma, dma((2,)), dma((2,)), dma, dma,
            dma, dma((ny,)), dma, dma,
        ],
        compiler_params=pltpu.CompilerParams(
            collective_id=0, has_side_effects=True, vmem_limit_bytes=40 * 1024 * 1024
        ),
    )(
        *(
            pltpu.with_memory_space_constraint(array, pltpu.HBM)
            for array in (
                field_in,
                first_weight.reshape(weight),
                second_weight.reshape(weight),
                cotangent,
            )
        )
    )
    output, first_grad, second_grad = pl.pallas_call(
        functools.partial(unpack, 1.0 / math.sqrt(total)),
        out_shape=(
            jax.ShapeDtypeStruct(field_in.shape, BF16),
            jax.ShapeDtypeStruct(weight, F32),
            jax.ShapeDtypeStruct(weight, F32),
        ),
        in_specs=[inside] * 2,
        out_specs=(outside,) * 3,
        scratch_shapes=[vmem(weight, F32), vmem(weight, F32), dma((3,))],
        compiler_params=pltpu.CompilerParams(vmem_limit_bytes=16 * 1024 * 1024),
    )(output, full)
    shape = (3, 3, 3, C, C)
    return output, first_grad.reshape(shape), second_grad.reshape(shape)


def solution(mesh):
    sizes = (mesh.shape["gx"], mesh.shape["gy"], mesh.shape["grp"])
    return jax.shard_map(
        functools.partial(shards, sizes),
        mesh=mesh,
        in_specs=(P("grp", "gx", "gy", None), P(), P(), P("grp", "gx", "gy", None)),
        out_specs=(P("grp", "gx", "gy", None), P(), P()),
        check_vma=False,
    )
```

```python
import functools
import math

import jax
import jax.numpy as jnp
from jax import lax
from jax.experimental import pallas as pl
from jax.experimental.pallas import tpu as pltpu
from jax.sharding import PartitionSpec as P

C = 64
NZ = 16
X = 8
Y = 16
Q = 8
XE = X + 2
PLANES = 16
FAR = 10
SLOT = 32
MARGIN = 8
ROWS_E = XE * Y
PAIRS = 5
PACKED = PAIRS * 192
F32 = jnp.float32
BF16 = jnp.bfloat16
MESH = pl.DeviceIdType.MESH


def low_lanes(rows):
    return lax.broadcasted_iota(jnp.int32, (rows, 128), 1) < 64


def row(q, x, y):
    return (q * PLANES + x) * SLOT + MARGIN + 8 + y


def clear_halo(ext, shifted):
    edge = jnp.zeros((8, 128), F32)
    plane = jnp.zeros((SLOT, 128), F32)
    for q in range(Q):
        for x in range(XE):
            if x in (0, XE - 1):
                ext[pl.ds(row(q, x, -8), SLOT), :] = plane
            else:
                ext[pl.ds(row(q, x, -8), 8), :] = edge
                ext[pl.ds(row(q, x, Y), 8), :] = edge
        if shifted is not None:
            shifted[q, 0:Y, :] = jnp.zeros((Y, 384), F32)
            shifted[q, ROWS_E - Y : ROWS_E, :] = jnp.zeros((Y, 384), F32)


def take_edges(ext, send_x, send_y, send_c, corner, gx):
    deep = send_x.shape[0]
    for q in range(Q):
        columns = slice(q * 128, q * 128 + 128)
        for d in range(deep):
            near = (X - d) - (X - 1 - 2 * d) * gx
            plane = ext[pl.ds(pl.multiple_of(row(q, near, 0), 8), Y), :]
            send_x[d, :, columns] = plane.astype(BF16)
            for e in range(deep):
                corner[0, d * deep + e, q : q + 1, :] = plane[e : e + 1]
                corner[1, d * deep + e, q : q + 1, :] = plane[Y - 1 - e : Y - e]
        for e in range(deep):
            for side, y in ((0, e), (1, Y - 1 - e)):
                send_y[side, e, :, columns] = ext[pl.ds(row(q, 1, y), X, stride=SLOT), :].astype(BF16)
    send_c[...] = corner[...].astype(BF16)


def halo_copies(ends, send_sems, recv_sems, place, count):
    send_x, send_y, send_c, land_x, land_y, land_c = ends
    gx, gy, grp = place
    up = lax.rem(gy + 1, count)
    down = lax.rem(gy + count - 1, count)
    moves = (
        (send_c.at[1], land_c.at[0], (1 - gx, up, grp)),
        (send_c.at[0], land_c.at[1], (1 - gx, down, grp)),
        (send_x, land_x, (1 - gx, gy, grp)),
        (send_y.at[1], land_y.at[0], (gx, up, grp)),
        (send_y.at[0], land_y.at[1], (gx, down, grp)),
    )
    return [
        pltpu.make_async_remote_copy(
            src_ref=source, dst_ref=target, send_sem=send_sems.at[number], recv_sem=recv_sems.at[number],
            device_id=device, device_id_type=MESH,
        )
        for number, (source, target, device) in enumerate(moves)
    ]


def insert_y(ext, land_y, sided):
    for e in range(land_y.shape[1]):
        for side, y in ((0, -1 - e), (1, Y + e)):
            for q in range(Q):
                value = land_y[side, e, :, q * 128 : q * 128 + 128].astype(F32)
                value = jnp.where(sided[side], value, jnp.zeros_like(value))
                ext[pl.ds(row(q, 1, y), X, stride=SLOT), :] = value


def insert_x(ext, land_x, land_c, sided, far, corner):
    deep = land_x.shape[0]
    corner[...] = land_c[...].astype(F32)
    rows = lax.broadcasted_iota(jnp.int32, (8, 128), 0)
    for d in range(deep):
        plane = far if d == 0 else FAR
        for q in range(Q):
            start = pl.multiple_of(row(q, plane, 0), 8)
            ext[pl.ds(start, Y), :] = land_x[d, :, q * 128 : q * 128 + 128].astype(F32)
            low = jnp.zeros((8, 128), F32)
            high = jnp.zeros((8, 128), F32)
            for e in range(deep):
                cell = d * deep + e
                low = jnp.where((rows == 7 - e) & sided[0], corner[0, cell, q : q + 1, :], low)
                high = jnp.where((rows == e) & sided[1], corner[1, cell, q : q + 1, :], high)
            ext[pl.ds(start - 8, 8), :] = low
            ext[pl.ds(start + Y, 8), :] = high


def operand(values, low):
    zero = jnp.zeros_like(values[0])
    padded = [zero] + values + [zero]
    return [
        (padded[q + 1].astype(BF16), jnp.where(low, padded[q + 2], padded[q]).astype(BF16))
        for q in range(Q)
    ]


def conv_own(ext, wide, banded, shifted, flipped):
    low = low_lanes(Y)
    for x in range(X):
        for dy in range(3):
            values = [ext[pl.ds(row(q, x + 1, dy - 1), Y), :] for q in range(Q)]
            for q, (own, mixed) in enumerate(operand(values, low)):
                wide[q, x * Y : x * Y + Y, dy * 256 : dy * 256 + 128] = own
                wide[q, x * Y : x * Y + Y, dy * 256 + 128 : dy * 256 + 256] = mixed
    dims = (((1,), (1 if flipped else 0,)), ((), ()))
    result = lax.dot_general(
        wide[...].reshape(Q * X * Y, 768), banded[...], dims, preferred_element_type=F32
    )
    shifted[:, Y : Y + X * Y, :] = result.reshape(Q, X * Y, 384)


def conv_y(ext, banded, columns, flipped):
    low = low_lanes(X)
    for side, y, dy in ((0, -1, 0), (1, Y, 2)):
        values = [ext[pl.ds(row(q, 1, y), X, stride=SLOT), :] for q in range(Q)]
        padded = [jnp.zeros((X, 128), F32)] + values + [jnp.zeros((X, 128), F32)]
        own = jnp.concatenate(values, axis=0)
        mixed = jnp.concatenate([jnp.where(low, padded[q + 2], padded[q]) for q in range(Q)], axis=0)
        rows = jnp.concatenate([own, mixed], axis=1).astype(BF16)
        if flipped:
            weight = banded[:, dy * 256 : dy * 256 + 256]
        else:
            weight = banded[dy * 256 : dy * 256 + 256, :]
        dims = (((1,), (1 if flipped else 0,)), ((), ()))
        result = lax.dot_general(rows, weight, dims, preferred_element_type=F32)
        for q in range(Q):
            columns[side, q, 8:16, :] = result[q * X : q * X + X]


def conv_x(ext, thin, banded, flipped, gx, far):
    low = low_lanes(Y)
    for dy in range(3):
        values = [
            ext[pl.ds(pl.multiple_of(row(q, far, 0), 8) + dy - 1, Y), :] for q in range(Q)
        ]
        for q, (own, mixed) in enumerate(operand(values, low)):
            thin[q * Y : q * Y + Y, dy * 256 : dy * 256 + 128] = own
            thin[q * Y : q * Y + Y, dy * 256 + 128 : dy * 256 + 256] = mixed
    tap = pl.ds(pl.multiple_of((1 - gx) * 256, 128), 128)
    weight = banded[tap, :] if flipped else banded[:, tap]
    dims = (((1,), (1 if flipped else 0,)), ((), ()))
    return lax.dot_general(thin[...], weight, dims, preferred_element_type=F32)


def add_plane(sums, added, gx):
    edge = pl.ds(pl.multiple_of((X - 1) * (1 - gx) * Y, Y), Y)
    for q in range(Q):
        sums[q, edge, :] = sums[q, edge, :] + added[q * Y : q * Y + Y]


def silu(value):
    return (value * jax.nn.sigmoid(value)).astype(BF16).astype(F32)


def lanes_of(values, low):
    padded = [jnp.zeros_like(values[0])] + values + [jnp.zeros_like(values[0])]
    own = jnp.concatenate(values, axis=0)
    mixed = jnp.concatenate([jnp.where(low, padded[q + 2], padded[q]) for q in range(Q)], axis=0)
    return [own.astype(BF16), mixed.astype(BF16)]


def slot_operand(ext, plane):
    low = low_lanes(SLOT)
    parts = []
    for dy in range(3):
        starts = [pl.multiple_of(row(q, plane, -8), 8) + dy - 1 for q in range(Q)]
        parts += lanes_of([ext[pl.ds(start, SLOT), :] for start in starts], low)
    return jnp.concatenate(parts, axis=1)


def ring_near(ext, banded, near_part, gx):
    tap = pl.ds(pl.multiple_of(256 * gx, 128), 128)
    near_part[...] = jnp.dot(
        slot_operand(ext, X - (X - 1) * gx), banded[:, tap], preferred_element_type=F32
    )


def ring_far(ext, hidden_ext, banded, near_part, edge_part, sided, gx, far):
    tap = pl.ds(pl.multiple_of((1 - gx) * 256, 128), 128)
    both = jnp.concatenate([banded[:, tap], banded[:, 128:256]], axis=1)
    result = jnp.dot(slot_operand(ext, far), both, preferred_element_type=F32)
    edge_part[...] = result[:, 0:128]
    total = near_part[...] + result[:, 128:256]
    total = total + jnp.dot(slot_operand(ext, FAR), banded[:, tap], preferred_element_type=F32)
    hidden = silu(total)
    y = lax.broadcasted_iota(jnp.int32, (SLOT, 128), 0) - 8
    inside = ((y >= 0) & (y < Y)) | ((y == -1) & sided[0]) | ((y == Y) & sided[1])
    for q in range(Q):
        part = hidden[q * SLOT : q * SLOT + SLOT]
        hidden_ext[pl.ds(pl.multiple_of(row(q, far, -8), 8), SLOT), :] = jnp.where(inside, part, jnp.zeros_like(part))


def ring_y(ext, hidden_ext, banded, ring, ring_pre, sided):
    low = low_lanes(PLANES)
    for side, y in ((0, -1), (1, Y)):
        parts = []
        for dy in range(3):
            parts += lanes_of(
                [ext[pl.ds(row(q, 0, y + dy - 1), PLANES, stride=SLOT), :] for q in range(Q)], low
            )
        ring[...] = jnp.dot(jnp.concatenate(parts, axis=1), banded[...], preferred_element_type=F32)
        for q in range(Q):
            start = q * PLANES
            total = (
                ring[start : start + X, 0:128]
                + ring[start + 1 : start + 1 + X, 128:256]
                + ring[start + 2 : start + 2 + X, 256:384]
            )
            ring_pre[side, pl.ds(q, X, stride=Q), :] = total
            hidden = silu(total)
            hidden_ext[pl.ds(row(q, 1, y), X, stride=SLOT), :] = jnp.where(
                sided[side], hidden, jnp.zeros_like(hidden)
            )


def plane_sum(shifted, p):
    n = X * Y
    return (
        shifted[p, 0:n, 0:128]
        + shifted[p, Y : Y + n, 128:256]
        + shifted[p, 2 * Y : 2 * Y + n, 256:384]
    )


def conv_sum(shifted, columns, sums, p):
    sums[p] = plane_sum(shifted, p)
    if columns is None:
        return
    for side, y in ((0, 0), (1, Y - 1)):
        extra = (
            columns[side, p, 7:15, 0:128]
            + columns[side, p, 8:16, 128:256]
            + columns[side, p, 9:17, 256:384]
        )
        place = pl.ds(y, X, stride=Y)
        sums[p, place, :] = sums[p, place, :] + extra


TAPS = ((1, 0), (2, 1), (None, 2), (0, None))


def piece(weight, tap):
    return jnp.zeros((C, C), BF16) if tap is None else weight[tap]


def forward_weight(weight, banded):
    for dy in range(3):
        for slot in range(4):
            rows = slice(dy * 256 + slot * C, dy * 256 + slot * C + C)
            for dx in range(3):
                pieces = [
                    piece(weight, None if t is None else (dx * 3 + dy) * 3 + t) for t in TAPS[slot]
                ]
                banded[rows, dx * 128 : dx * 128 + 128] = jnp.concatenate(pieces, axis=1)


def backward_weight(weight, banded):
    for dx in range(3):
        for b in range(2):
            rows = slice(dx * 128 + b * C, dx * 128 + b * C + C)
            for dy in range(3):
                for half in range(2):
                    pieces = []
                    for slot in (2 * half, 2 * half + 1):
                        t = TAPS[slot][b]
                        tap = None if t is None else ((2 - dx) * 3 + 2 - dy) * 3 + 2 - t
                        pieces.append(piece(weight, tap))
                    start = dy * 256 + half * 128
                    banded[rows, start : start + 128] = jnp.concatenate(pieces, axis=1)


def kernel_grad(ext, turned, packed, g, finished):
    low = low_lanes(192)
    turned_value = turned[...]

    def moving(tap):
        dx, dy = tap // 3, tap % 3
        blocks = [
            ext[pl.ds(row(q, x + dx, dy - 1), Y), :].astype(BF16) for q in range(Q) for x in range(X)
        ]
        return jnp.concatenate(blocks, axis=0)

    for pair in range(PAIRS):
        first = 2 * pair
        if first + 1 < 9:
            rhs = jnp.concatenate([moving(first), moving(first + 1)], axis=1)
        else:
            rhs = moving(first)
        result = jnp.dot(turned_value, rhs, preferred_element_type=F32)
        one = result[:, 0:128]
        two = result[:, 128:256] if first + 1 < 9 else jnp.zeros_like(one)
        straight = jnp.where(low, one[0:192], two[64:256])
        crossed = jnp.where(low, two[0:192], one[64:256])
        total = straight + pltpu.roll(crossed, 64, 1)
        packed[g, pair * 192 : pair * 192 + 192, :] = total.astype(BF16)
        finished(pair)


def turn(turned, q, block):
    flat = block.astype(F32).T.astype(BF16)
    columns = lambda w: slice(w * 128, w * 128 + 128)
    turned[64:192, columns(q)] = flat
    if q + 1 < Q:
        turned[0:64, columns(q + 1)] = flat[64:128]
    else:
        turned[192:256, columns(q)] = jnp.zeros((64, 128), BF16)
    if q > 0:
        turned[192:256, columns(q - 1)] = flat[0:64]
    else:
        turned[0:64, columns(q)] = jnp.zeros((64, 128), BF16)


def step(
    sizes,
    field_hbm, first_hbm, second_hbm, cotangent_hbm,
    output, full,
    field, first, second, cotangent, load_sems, shifted, shifted_c,
    ext_f, ext_c, ext_h, wide, thin, columns, columns_c, pre, sums_c,
    banded_1, banded_2, banded_t, turned_c, turned_p, slope,
    send_xf, send_yf, send_cf, land_xf, land_yf, land_cf, corner_f,
    send_xc, send_yc, send_cc, land_xc, land_yc, land_cc, corner_c, ring,
    ring_pre, near_part, edge_part,
    packed, gathered_xy, own_sum, pass_out, pass_in, gathered_z,
    halo_send, halo_recv, pass_send, pass_recv, xy_send, xy_recv, z_send, z_recv,
    back_xy_send, back_xy_recv, share_send, share_recv,
):
    nx, ny, ng = sizes
    zl = ng // 2
    nz = nx * zl
    chunk = gathered_xy.shape[2]
    owners = PACKED // chunk
    loads = [
        pltpu.make_async_copy(source, target, load_sems.at[number])
        for number, (source, target) in enumerate(
            ((field_hbm, field), (cotangent_hbm, cotangent), (first_hbm, first), (second_hbm, second))
        )
    ]
    for load in loads:
        load.start()
    gx, gy, grp = lax.axis_index("gx"), lax.axis_index("gy"), lax.axis_index("grp")
    core = lax.rem(grp, 2)
    z = gx * zl + grp // 2
    me = (gx, gy, grp)
    sibling = (gx, gy, grp + 1 - 2 * core)

    def along_xy(k):
        return lax.rem(gy + k, ny)

    def along_z(k):
        return lax.rem(z + k, nz)

    def z_device(target):
        return (target // zl, gy, 2 * lax.rem(target, zl) + core)

    barrier = pltpu.get_barrier_semaphore()

    def greet(device):
        pl.semaphore_signal(barrier, inc=1, device_id=device, device_id_type=MESH)

    greet((1 - gx, along_xy(1), grp))
    greet((1 - gx, along_xy(ny - 1), grp))
    greet((1 - gx, gy, grp))
    greet((gx, along_xy(1), grp))
    greet((gx, along_xy(ny - 1), grp))
    greet(sibling)
    for k in range(1, nz):
        if k != zl:
            greet(z_device(along_z(k)))

    @pl.loop(2, ny - 1)
    def _(k):
        greet((gx, along_xy(k), grp))

    place = (gx, gy, grp)
    sided = (gy > 0, gy < ny - 1)
    far = (XE - 1) * (1 - gx)
    ends = (
        (send_xf, send_yf, send_cf, land_xf, land_yf, land_cf),
        (send_xc, send_yc, send_cc, land_xc, land_yc, land_cc),
    )
    corners = (corner_f, corner_c)
    halos = [
        halo_copies(ends[number], halo_send.at[number], halo_recv.at[number], place, ny)
        for number in range(2)
    ]

    def dispatch(number, ext):
        take_edges(ext, *ends[number][:3], corners[number], gx)
        if number == 0:
            pl.semaphore_wait(barrier, nz - 1 + ny - 1 + 3)
        for copy in halos[number]:
            copy.start()

    def arrive_y(number, ext):
        for which in (3, 4):
            halos[number][which].wait_recv()
        insert_y(ext, ends[number][4], sided)

    def arrive_x(number, ext):
        for which in (0, 1, 2):
            halos[number][which].wait_recv()
        insert_x(ext, ends[number][3], ends[number][5], sided, far, corners[number])

    def load_own(ext, source):
        for x in range(X):
            for q in range(Q):
                ext[pl.ds(row(q, x + 1, 0), Y), :] = source[0, x, :, q * 128 : q * 128 + 128].astype(F32)

    clear_halo(ext_f, shifted)
    loads[0].wait()
    load_own(ext_f, field)
    dispatch(0, ext_f)
    clear_halo(ext_c, shifted_c)
    loads[1].wait()
    load_own(ext_c, cotangent)
    dispatch(1, ext_c)

    loads[2].wait()
    forward_weight(first, banded_1)
    conv_own(ext_f, wide, banded_1, shifted, False)
    columns[...] = jnp.zeros_like(columns)
    columns_c[...] = jnp.zeros_like(columns_c)
    loads[3].wait()
    backward_weight(second, banded_t)
    for q in range(Q):
        turn(turned_c, q, cotangent[0, :, :, q * 128 : q * 128 + 128].reshape(X * Y, 128))

    conv_own(ext_c, wide, banded_t, shifted_c, True)
    forward_weight(second, banded_2)
    clear_halo(ext_h, None)

    def activate(value):
        sigma = jax.nn.sigmoid(value)
        return (value * sigma).astype(BF16).astype(F32), sigma * (1.0 + value * (1.0 - sigma))

    arrive_y(0, ext_f)
    conv_y(ext_f, banded_1, columns, False)
    for p in range(Q):
        conv_sum(shifted, columns, pre, p)
        hidden, slope[p] = activate(pre[p])
        for x in range(X):
            ext_h[pl.ds(row(p, x + 1, 0), Y), :] = hidden[x * Y : x * Y + Y]
    arrive_y(1, ext_c)
    conv_y(ext_c, banded_t, columns_c, True)
    for p in range(Q):
        conv_sum(shifted_c, columns_c, sums_c, p)
    ring_y(ext_f, ext_h, banded_1, ring, ring_pre, sided)
    ring_near(ext_f, banded_1, near_part, gx)

    arrive_x(0, ext_f)
    ring_far(ext_f, ext_h, banded_1, near_part, edge_part, sided, gx, far)
    edge = (X - 1) * (1 - gx)
    edge_rows = pl.ds(pl.multiple_of(edge * Y, Y), Y)
    for p in range(Q):
        added = edge_part[p * SLOT + 8 : p * SLOT + 8 + Y, :]
        hidden, slope[p, edge_rows, :] = activate(pre[p, edge_rows, :] + added)
        ext_h[pl.ds(pl.multiple_of(row(p, edge + 1, 0), 8), Y), :] = hidden
    for side, y in ((0, -1), (1, Y)):
        added = edge_part[pl.ds(8 + y, Q, stride=SLOT), :]
        hidden = silu(ring_pre[side, pl.ds(pl.multiple_of(edge * Q, Q), Q), :] + added)
        ext_h[pl.ds(row(0, edge + 1, y), Q, stride=PLANES * SLOT), :] = jnp.where(
            sided[side], hidden, jnp.zeros_like(hidden)
        )

    owner = gy < owners

    def scatter(g):
        def finished(pair):
            for j in range(owners):
                if not pair * 192 < (j + 1) * chunk <= (pair + 1) * 192:
                    continue

                @pl.when(gy != j)
                def _():
                    pltpu.make_async_remote_copy(
                        src_ref=packed.at[g, pl.ds(j * chunk, chunk)], dst_ref=gathered_xy.at[g, gy],
                        send_sem=xy_send.at[g], recv_sem=xy_recv.at[g],
                        device_id=(gx, j, grp), device_id_type=MESH,
                    ).start()

        return finished

    kernel_grad(ext_h, turned_c, packed, 1, scatter(1))
    arrive_x(1, ext_c)
    add_plane(sums_c, conv_x(ext_c, thin, banded_t, True, gx, far), gx)
    for p in range(Q):
        turn(turned_p, p, (sums_c[p] * slope[p]).astype(BF16))

    kernel_grad(ext_f, turned_p, packed, 0, scatter(0))

    conv_own(ext_h, wide, banded_2, shifted, False)
    for p in range(Q):
        conv_sum(shifted, None, pre, p)
    add_plane(pre, conv_x(ext_h, thin, banded_2, False, gx, far), gx)
    for p in range(Q):
        output[0, :, :, p * 128 : p * 128 + 128] = pre[p].astype(BF16).reshape(X, Y, 128)

    def rows_of(j):
        return pl.ds(pl.multiple_of(j * chunk, 16), chunk)

    def several(g, count):
        part = gathered_xy.at[g, pl.ds(0, count)]
        return pltpu.make_async_remote_copy(
            src_ref=part, dst_ref=part, send_sem=xy_send.at[g], recv_sem=xy_recv.at[g],
            device_id=me, device_id_type=MESH,
        )

    pass_on = pltpu.make_async_remote_copy(
        src_ref=pass_out, dst_ref=pass_in, send_sem=pass_send, recv_sem=pass_recv,
        device_id=sibling, device_id_type=MESH,
    )

    for g in (1, 0):

        @pl.when(owner)
        def _():
            several(g, ny - 1).wait_recv()
            gathered_xy[g, gy] = packed[g, rows_of(gy), :]
            total = gathered_xy[g, 0].astype(F32)
            for k in range(1, ny):
                total = total + gathered_xy[g, k].astype(F32)

            @pl.when(core == 1 - g)
            def _():
                pass_out[...] = total
                pass_on.start()

            @pl.when(core == g)
            def _():
                own_sum[...] = total
                pass_on.wait_recv()
                gathered_z[z] = (own_sum[...] + pass_in[...]).astype(BF16)

                for k in sorted(range(1, nz), key=lambda k: -min(k, nz - k)):
                    pltpu.make_async_remote_copy(
                        src_ref=gathered_z.at[z], dst_ref=gathered_z.at[z],
                        send_sem=z_send, recv_sem=z_recv,
                        device_id=z_device(along_z(k)), device_id_type=MESH,
                    ).start()

    def share(j):
        pltpu.make_async_remote_copy(
            src_ref=full.at[core, rows_of(j)], dst_ref=full.at[core, rows_of(j)],
            send_sem=share_send, recv_sem=share_recv,
            device_id=sibling, device_id_type=MESH,
        ).start()

    by_distance = sorted(
        range(1, ny), key=lambda k: -(min(k // 4, 4 - k // 4) + min(k % 4, 4 - k % 4))
    )
    others = gathered_z.at[pl.ds(0, nz - 1)]
    z_all = pltpu.make_async_remote_copy(
        src_ref=others, dst_ref=others, send_sem=z_send, recv_sem=z_recv,
        device_id=me, device_id_type=MESH,
    )

    @pl.when(owner)
    def _():
        z_all.wait_recv()
        grand = gathered_z[0].astype(F32)
        for k in range(1, nz):
            grand = grand + gathered_z[k].astype(F32)
        rows = lax.broadcasted_iota(jnp.int32, (128, 128), 0)
        lanes = lax.broadcasted_iota(jnp.int32, (128, 128), 1)
        unit = (rows == lanes).astype(BF16)
        turned = []
        for start in range(0, chunk, C):
            block = lax.dot_general(
                unit, grand[start : start + C].astype(BF16), (((1,), (1,)), ((), ())),
                preferred_element_type=F32,
            )
            turned.append(jnp.concatenate([block[0:C], block[C : 2 * C]], axis=1))
        full[core, rows_of(gy), :] = jnp.concatenate(turned, axis=0).astype(BF16)

        for k in by_distance:
            pltpu.make_async_remote_copy(
                src_ref=full.at[core, rows_of(gy)], dst_ref=full.at[core, rows_of(gy)],
                send_sem=back_xy_send, recv_sem=back_xy_recv.at[k],
                device_id=(gx, along_xy(k), grp), device_id_type=MESH,
            ).start()

        share(gy)

    for k in reversed(by_distance):
        j = along_xy(ny - k)

        @pl.when(j < owners)
        def _(j=j, k=k):
            pltpu.make_async_remote_copy(
                src_ref=full.at[core, rows_of(j)], dst_ref=full.at[core, rows_of(j)],
                send_sem=back_xy_send, recv_sem=back_xy_recv.at[k],
                device_id=me, device_id_type=MESH,
            ).wait_recv()
            share(j)

    whole = pltpu.make_async_remote_copy(
        src_ref=full.at[core], dst_ref=full.at[1 - core], send_sem=share_send, recv_sem=share_recv,
        device_id=sibling, device_id_type=MESH,
    )
    whole.wait_recv()

    for number in range(2):
        for copy in halos[number]:
            copy.wait_send()

    @pl.when(owner)
    def _():
        for g in range(2):
            several(g, owners - 1).wait_send()
        pass_on.wait_send()
        z_all.wait_send()
        pltpu.make_async_remote_copy(
            src_ref=gathered_xy.at[0, pl.ds(0, ny - 1)], dst_ref=gathered_xy.at[0, pl.ds(0, ny - 1)],
            send_sem=back_xy_send, recv_sem=share_recv,
            device_id=me, device_id_type=MESH,
        ).wait_send()

    if owners < ny:

        @pl.when(jnp.logical_not(owner))
        def _():
            for g in range(2):
                several(g, owners).wait_send()

    whole.wait_send()


def unpack(factor, output_in, full, output, first_out, second_out, one, two, sems):
    copies = [
        pltpu.make_async_copy(source, target, sems.at[number])
        for number, (source, target) in enumerate(
            ((output_in, output), (one, first_out), (two, second_out))
        )
    ]
    copies[0].start()
    for g, target in ((0, one), (1, two)):
        for pair in range(PAIRS):
            for v in range(3):
                start = (pair * 3 + v) * C
                block = full[g, start : start + C, :].astype(F32) * factor
                target[2 * pair * 3 + 2 - v] = block[:, 0:C]
                if 2 * pair + 1 < 9:
                    target[(2 * pair + 1) * 3 + 2 - v] = block[:, C : 2 * C]
        copies[g + 1].start()
    for copy in copies:
        copy.wait()


def halo_buffers(deep):
    ends = [
        pltpu.VMEM((deep, Y, 1024), BF16),
        pltpu.VMEM((2, deep, X, 1024), BF16),
        pltpu.VMEM((2, deep * deep, Q, 128), BF16),
    ]
    return ends + ends + [pltpu.VMEM((2, deep * deep, Q, 128), F32)]


def shards(sizes, field_in, first_weight, second_weight, cotangent):
    nx, ny, ng = sizes
    nz = nx * ng // 2
    chunk = C * pl.cdiv(PACKED, C * ny)
    assert PACKED % chunk == 0
    rows = PACKED
    total = ng * nx * X * ny * Y * NZ
    dma = pltpu.SemaphoreType.DMA
    vmem = pltpu.VMEM
    inside = pl.BlockSpec(memory_space=pltpu.VMEM)
    outside = pl.BlockSpec(memory_space=pltpu.HBM)
    cells = (Q * PLANES * SLOT + 2 * MARGIN, 128)
    sums = (Q, ROWS_E, 384)
    weight = (27, C, C)
    output, full = pl.pallas_call(
        functools.partial(step, sizes),
        out_shape=(
            jax.ShapeDtypeStruct(field_in.shape, BF16),
            jax.ShapeDtypeStruct((2, rows, 128), BF16),
        ),
        in_specs=[outside] * 4,
        out_specs=(inside,) * 2,
        scratch_shapes=[
            vmem(field_in.shape, BF16), vmem(weight, BF16), vmem(weight, BF16), vmem(field_in.shape, BF16),
            dma((4,)), vmem(sums, F32), vmem(sums, F32),
            vmem(cells, F32), vmem(cells, F32), vmem(cells, F32),
            vmem((Q, X * Y, 768), BF16), vmem((Q * Y, 768), BF16), vmem((2, Q, 24, 384), F32), vmem((2, Q, 24, 384), F32),
            vmem((Q, X * Y, 128), F32), vmem((Q, X * Y, 128), F32),
            vmem((768, 384), BF16), vmem((768, 384), BF16), vmem((384, 768), BF16),
            vmem((256, Q * 128), BF16), vmem((256, Q * 128), BF16),
            vmem((Q, X * Y, 128), F32),
            *halo_buffers(2), *halo_buffers(1), vmem((Q * PLANES, 384), F32),
            vmem((2, X * Q, 128), F32), vmem((Q * SLOT, 128), F32), vmem((Q * SLOT, 128), F32),
            vmem((2, rows, 128), BF16), vmem((2, ny, chunk, 128), BF16),
            vmem((chunk, 128), F32), vmem((chunk, 128), F32), vmem((chunk, 128), F32), vmem((nz, chunk, 128), BF16),
            dma((2, 5)), dma((2, 5)), dma, dma, dma((2,)), dma((2,)), dma, dma,
            dma, dma((ny,)), dma, dma,
        ],
        compiler_params=pltpu.CompilerParams(
            collective_id=0, has_side_effects=True, vmem_limit_bytes=40 * 1024 * 1024
        ),
    )(
        *(
            pltpu.with_memory_space_constraint(array, pltpu.HBM)
            for array in (
                field_in,
                first_weight.reshape(weight),
                second_weight.reshape(weight),
                cotangent,
            )
        )
    )
    output, first_grad, second_grad = pl.pallas_call(
        functools.partial(unpack, 1.0 / math.sqrt(total)),
        out_shape=(
            jax.ShapeDtypeStruct(field_in.shape, BF16),
            jax.ShapeDtypeStruct(weight, F32),
            jax.ShapeDtypeStruct(weight, F32),
        ),
        in_specs=[inside] * 2,
        out_specs=(outside,) * 3,
        scratch_shapes=[vmem(weight, F32), vmem(weight, F32), dma((3,))],
        compiler_params=pltpu.CompilerParams(vmem_limit_bytes=16 * 1024 * 1024),
    )(output, full)
    shape = (3, 3, 3, C, C)
    return output, first_grad.reshape(shape), second_grad.reshape(shape)


def solution(mesh):
    sizes = (mesh.shape["gx"], mesh.shape["gy"], mesh.shape["grp"])
    return jax.shard_map(
        functools.partial(shards, sizes),
        mesh=mesh,
        in_specs=(P("grp", "gx", "gy", None), P(), P(), P("grp", "gx", "gy", None)),
        out_specs=(P("grp", "gx", "gy", None), P(), P()),
        check_vma=False,
    )
```

```python
import functools
import math

import jax
import jax.numpy as jnp
from jax import lax
from jax.experimental import pallas as pl
from jax.experimental.pallas import tpu as pltpu
from jax.sharding import PartitionSpec as P

C = 64
NZ = 16
X = 8
Y = 16
Q = 8
XE = X + 2
PLANES = 16
FAR = 10
SLOT = 32
MARGIN = 8
ROWS_E = XE * Y
PAIRS = 5
PACKED = PAIRS * 192
F32 = jnp.float32
BF16 = jnp.bfloat16
MESH = pl.DeviceIdType.MESH


def low_lanes(rows):
    return lax.broadcasted_iota(jnp.int32, (rows, 128), 1) < 64


def row(q, x, y):
    return (q * PLANES + x) * SLOT + MARGIN + 8 + y


def clear_halo(ext, shifted):
    edge = jnp.zeros((8, 128), F32)
    plane = jnp.zeros((SLOT, 128), F32)
    for q in range(Q):
        for x in range(XE):
            if x in (0, XE - 1):
                ext[pl.ds(row(q, x, -8), SLOT), :] = plane
            else:
                ext[pl.ds(row(q, x, -8), 8), :] = edge
                ext[pl.ds(row(q, x, Y), 8), :] = edge
        if shifted is not None:
            shifted[q, 0:Y, :] = jnp.zeros((Y, 384), F32)
            shifted[q, ROWS_E - Y : ROWS_E, :] = jnp.zeros((Y, 384), F32)


def take_edges(ext, send_x, send_y, send_c, corner, gx):
    deep = send_x.shape[0]
    for q in range(Q):
        columns = slice(q * 128, q * 128 + 128)
        for d in range(deep):
            near = (X - d) - (X - 1 - 2 * d) * gx
            plane = ext[pl.ds(pl.multiple_of(row(q, near, 0), 8), Y), :]
            send_x[d, :, columns] = plane.astype(BF16)
            for e in range(deep):
                corner[0, d * deep + e, q : q + 1, :] = plane[e : e + 1]
                corner[1, d * deep + e, q : q + 1, :] = plane[Y - 1 - e : Y - e]
        for e in range(deep):
            for side, y in ((0, e), (1, Y - 1 - e)):
                send_y[side, e, :, columns] = ext[pl.ds(row(q, 1, y), X, stride=SLOT), :].astype(BF16)
    send_c[...] = corner[...].astype(BF16)


def halo_copies(ends, send_sems, recv_sems, place, count):
    send_x, send_y, send_c, land_x, land_y, land_c = ends
    gx, gy, grp = place
    up = lax.rem(gy + 1, count)
    down = lax.rem(gy + count - 1, count)
    moves = (
        (send_c.at[1], land_c.at[0], (1 - gx, up, grp)),
        (send_c.at[0], land_c.at[1], (1 - gx, down, grp)),
        (send_x, land_x, (1 - gx, gy, grp)),
        (send_y.at[1], land_y.at[0], (gx, up, grp)),
        (send_y.at[0], land_y.at[1], (gx, down, grp)),
    )
    return [
        pltpu.make_async_remote_copy(
            src_ref=source, dst_ref=target, send_sem=send_sems.at[number], recv_sem=recv_sems.at[number],
            device_id=device, device_id_type=MESH,
        )
        for number, (source, target, device) in enumerate(moves)
    ]


def insert_y(ext, land_y, sided):
    for e in range(land_y.shape[1]):
        for side, y in ((0, -1 - e), (1, Y + e)):
            for q in range(Q):
                value = land_y[side, e, :, q * 128 : q * 128 + 128].astype(F32)
                value = jnp.where(sided[side], value, jnp.zeros_like(value))
                ext[pl.ds(row(q, 1, y), X, stride=SLOT), :] = value


def insert_x(ext, land_x, land_c, sided, far, corner):
    deep = land_x.shape[0]
    corner[...] = land_c[...].astype(F32)
    rows = lax.broadcasted_iota(jnp.int32, (8, 128), 0)
    for d in range(deep):
        plane = far if d == 0 else FAR
        for q in range(Q):
            start = pl.multiple_of(row(q, plane, 0), 8)
            ext[pl.ds(start, Y), :] = land_x[d, :, q * 128 : q * 128 + 128].astype(F32)
            low = jnp.zeros((8, 128), F32)
            high = jnp.zeros((8, 128), F32)
            for e in range(deep):
                cell = d * deep + e
                low = jnp.where((rows == 7 - e) & sided[0], corner[0, cell, q : q + 1, :], low)
                high = jnp.where((rows == e) & sided[1], corner[1, cell, q : q + 1, :], high)
            ext[pl.ds(start - 8, 8), :] = low
            ext[pl.ds(start + Y, 8), :] = high


def operand(values, low):
    zero = jnp.zeros_like(values[0])
    padded = [zero] + values + [zero]
    return [
        (padded[q + 1].astype(BF16), jnp.where(low, padded[q + 2], padded[q]).astype(BF16))
        for q in range(Q)
    ]


def conv_own(ext, wide, banded, shifted, flipped):
    low = low_lanes(Y)
    for x in range(X):
        for dy in range(3):
            values = [ext[pl.ds(row(q, x + 1, dy - 1), Y), :] for q in range(Q)]
            for q, (own, mixed) in enumerate(operand(values, low)):
                wide[q, x * Y : x * Y + Y, dy * 256 : dy * 256 + 128] = own
                wide[q, x * Y : x * Y + Y, dy * 256 + 128 : dy * 256 + 256] = mixed
    dims = (((1,), (1 if flipped else 0,)), ((), ()))
    result = lax.dot_general(
        wide[...].reshape(Q * X * Y, 768), banded[...], dims, preferred_element_type=F32
    )
    shifted[:, Y : Y + X * Y, :] = result.reshape(Q, X * Y, 384)


def conv_y(ext, banded, columns, flipped):
    low = low_lanes(X)
    for side, y, dy in ((0, -1, 0), (1, Y, 2)):
        values = [ext[pl.ds(row(q, 1, y), X, stride=SLOT), :] for q in range(Q)]
        padded = [jnp.zeros((X, 128), F32)] + values + [jnp.zeros((X, 128), F32)]
        own = jnp.concatenate(values, axis=0)
        mixed = jnp.concatenate([jnp.where(low, padded[q + 2], padded[q]) for q in range(Q)], axis=0)
        rows = jnp.concatenate([own, mixed], axis=1).astype(BF16)
        if flipped:
            weight = banded[:, dy * 256 : dy * 256 + 256]
        else:
            weight = banded[dy * 256 : dy * 256 + 256, :]
        dims = (((1,), (1 if flipped else 0,)), ((), ()))
        result = lax.dot_general(rows, weight, dims, preferred_element_type=F32)
        for q in range(Q):
            columns[side, q, 8:16, :] = result[q * X : q * X + X]


def conv_x(ext, thin, banded, flipped, gx, far):
    low = low_lanes(Y)
    for dy in range(3):
        values = [
            ext[pl.ds(pl.multiple_of(row(q, far, 0), 8) + dy - 1, Y), :] for q in range(Q)
        ]
        for q, (own, mixed) in enumerate(operand(values, low)):
            thin[q * Y : q * Y + Y, dy * 256 : dy * 256 + 128] = own
            thin[q * Y : q * Y + Y, dy * 256 + 128 : dy * 256 + 256] = mixed
    tap = pl.ds(pl.multiple_of((1 - gx) * 256, 128), 128)
    weight = banded[tap, :] if flipped else banded[:, tap]
    dims = (((1,), (1 if flipped else 0,)), ((), ()))
    return lax.dot_general(thin[...], weight, dims, preferred_element_type=F32)


def add_plane(sums, added, gx):
    edge = pl.ds(pl.multiple_of((X - 1) * (1 - gx) * Y, Y), Y)
    for q in range(Q):
        sums[q, edge, :] = sums[q, edge, :] + added[q * Y : q * Y + Y]


def silu(value):
    return (value * jax.nn.sigmoid(value)).astype(BF16).astype(F32)


def lanes_of(values, low):
    padded = [jnp.zeros_like(values[0])] + values + [jnp.zeros_like(values[0])]
    own = jnp.concatenate(values, axis=0)
    mixed = jnp.concatenate([jnp.where(low, padded[q + 2], padded[q]) for q in range(Q)], axis=0)
    return [own.astype(BF16), mixed.astype(BF16)]


def slot_operand(ext, plane):
    low = low_lanes(SLOT)
    parts = []
    for dy in range(3):
        starts = [pl.multiple_of(row(q, plane, -8), 8) + dy - 1 for q in range(Q)]
        parts += lanes_of([ext[pl.ds(start, SLOT), :] for start in starts], low)
    return jnp.concatenate(parts, axis=1)


def ring_near(ext, banded, near_part, gx):
    tap = pl.ds(pl.multiple_of(256 * gx, 128), 128)
    near_part[...] = jnp.dot(
        slot_operand(ext, X - (X - 1) * gx), banded[:, tap], preferred_element_type=F32
    )


def ring_far(ext, hidden_ext, banded, near_part, edge_part, sided, gx, far):
    tap = pl.ds(pl.multiple_of((1 - gx) * 256, 128), 128)
    both = jnp.concatenate([banded[:, tap], banded[:, 128:256]], axis=1)
    result = jnp.dot(slot_operand(ext, far), both, preferred_element_type=F32)
    edge_part[...] = result[:, 0:128]
    total = near_part[...] + result[:, 128:256]
    total = total + jnp.dot(slot_operand(ext, FAR), banded[:, tap], preferred_element_type=F32)
    hidden = silu(total)
    y = lax.broadcasted_iota(jnp.int32, (SLOT, 128), 0) - 8
    inside = ((y >= 0) & (y < Y)) | ((y == -1) & sided[0]) | ((y == Y) & sided[1])
    for q in range(Q):
        part = hidden[q * SLOT : q * SLOT + SLOT]
        hidden_ext[pl.ds(pl.multiple_of(row(q, far, -8), 8), SLOT), :] = jnp.where(inside, part, jnp.zeros_like(part))


def ring_y(ext, hidden_ext, banded, ring, ring_pre, sided):
    low = low_lanes(PLANES)
    for side, y in ((0, -1), (1, Y)):
        parts = []
        for dy in range(3):
            parts += lanes_of(
                [ext[pl.ds(row(q, 0, y + dy - 1), PLANES, stride=SLOT), :] for q in range(Q)], low
            )
        ring[...] = jnp.dot(jnp.concatenate(parts, axis=1), banded[...], preferred_element_type=F32)
        for q in range(Q):
            start = q * PLANES
            total = (
                ring[start : start + X, 0:128]
                + ring[start + 1 : start + 1 + X, 128:256]
                + ring[start + 2 : start + 2 + X, 256:384]
            )
            ring_pre[side, pl.ds(q, X, stride=Q), :] = total
            hidden = silu(total)
            hidden_ext[pl.ds(row(q, 1, y), X, stride=SLOT), :] = jnp.where(
                sided[side], hidden, jnp.zeros_like(hidden)
            )


def plane_sum(shifted, p):
    n = X * Y
    return (
        shifted[p, 0:n, 0:128]
        + shifted[p, Y : Y + n, 128:256]
        + shifted[p, 2 * Y : 2 * Y + n, 256:384]
    )


def conv_sum(shifted, columns, sums, p):
    sums[p] = plane_sum(shifted, p)
    if columns is None:
        return
    for side, y in ((0, 0), (1, Y - 1)):
        extra = (
            columns[side, p, 7:15, 0:128]
            + columns[side, p, 8:16, 128:256]
            + columns[side, p, 9:17, 256:384]
        )
        place = pl.ds(y, X, stride=Y)
        sums[p, place, :] = sums[p, place, :] + extra


TAPS = ((1, 0), (2, 1), (None, 2), (0, None))


def piece(weight, tap):
    return jnp.zeros((C, C), BF16) if tap is None else weight[tap]


def forward_weight(weight, banded):
    for dy in range(3):
        for slot in range(4):
            rows = slice(dy * 256 + slot * C, dy * 256 + slot * C + C)
            for dx in range(3):
                pieces = [
                    piece(weight, None if t is None else (dx * 3 + dy) * 3 + t) for t in TAPS[slot]
                ]
                banded[rows, dx * 128 : dx * 128 + 128] = jnp.concatenate(pieces, axis=1)


def backward_weight(weight, banded):
    for dx in range(3):
        for b in range(2):
            rows = slice(dx * 128 + b * C, dx * 128 + b * C + C)
            for dy in range(3):
                for half in range(2):
                    pieces = []
                    for slot in (2 * half, 2 * half + 1):
                        t = TAPS[slot][b]
                        tap = None if t is None else ((2 - dx) * 3 + 2 - dy) * 3 + 2 - t
                        pieces.append(piece(weight, tap))
                    start = dy * 256 + half * 128
                    banded[rows, start : start + 128] = jnp.concatenate(pieces, axis=1)


def kernel_grad(ext, turned, packed, g, finished):
    low = low_lanes(192)
    turned_value = turned[...]

    def moving(tap):
        dx, dy = tap // 3, tap % 3
        blocks = [
            ext[pl.ds(row(q, x + dx, dy - 1), Y), :].astype(BF16) for q in range(Q) for x in range(X)
        ]
        return jnp.concatenate(blocks, axis=0)

    for pair in range(PAIRS):
        first = 2 * pair
        if first + 1 < 9:
            rhs = jnp.concatenate([moving(first), moving(first + 1)], axis=1)
        else:
            rhs = moving(first)
        result = jnp.dot(turned_value, rhs, preferred_element_type=F32)
        one = result[:, 0:128]
        two = result[:, 128:256] if first + 1 < 9 else jnp.zeros_like(one)
        straight = jnp.where(low, one[0:192], two[64:256])
        crossed = jnp.where(low, two[0:192], one[64:256])
        total = straight + pltpu.roll(crossed, 64, 1)
        packed[g, pair * 192 : pair * 192 + 192, :] = total.astype(BF16)
        finished(pair)


def turn(turned, q, block):
    flat = block.astype(F32).T.astype(BF16)
    columns = lambda w: slice(w * 128, w * 128 + 128)
    turned[64:192, columns(q)] = flat
    if q + 1 < Q:
        turned[0:64, columns(q + 1)] = flat[64:128]
    else:
        turned[192:256, columns(q)] = jnp.zeros((64, 128), BF16)
    if q > 0:
        turned[192:256, columns(q - 1)] = flat[0:64]
    else:
        turned[0:64, columns(q)] = jnp.zeros((64, 128), BF16)


def step(
    sizes,
    field_hbm, first_hbm, second_hbm, cotangent_hbm,
    output, full,
    field, first, second, cotangent, load_sems, shifted, shifted_c,
    ext_f, ext_c, ext_h, wide, thin, columns, columns_c, pre, sums_c,
    banded_1, banded_2, banded_t, turned_c, turned_p, slope,
    send_xf, send_yf, send_cf, land_xf, land_yf, land_cf, corner_f,
    send_xc, send_yc, send_cc, land_xc, land_yc, land_cc, corner_c, ring,
    ring_pre, near_part, edge_part,
    packed, gathered_xy, gathered_z,
    halo_send, halo_recv, xy_send, xy_recv, z_send, z_recv,
    back_xy_send, back_xy_recv, share_send, share_recv,
):
    nx, ny, ng = sizes
    zl = ng // 2
    nz = nx * zl
    chunk = gathered_xy.shape[1]
    owners = PACKED // chunk
    loads = [
        pltpu.make_async_copy(source, target, load_sems.at[number])
        for number, (source, target) in enumerate(
            ((field_hbm, field), (cotangent_hbm, cotangent), (first_hbm, first), (second_hbm, second))
        )
    ]
    for load in loads:
        load.start()
    gx, gy, grp = lax.axis_index("gx"), lax.axis_index("gy"), lax.axis_index("grp")
    core = lax.rem(grp, 2)
    z = gx * zl + grp // 2
    me = (gx, gy, grp)
    sibling = (gx, gy, grp + 1 - 2 * core)

    def along_xy(k):
        return lax.rem(gy + k, ny)

    def along_z(k):
        return lax.rem(z + k, nz)

    def z_device(target):
        return (target // zl, gy, 2 * lax.rem(target, zl) + core)

    barrier = pltpu.get_barrier_semaphore()

    def greet(device):
        pl.semaphore_signal(barrier, inc=1, device_id=device, device_id_type=MESH)

    greet((1 - gx, along_xy(1), grp))
    greet((1 - gx, along_xy(ny - 1), grp))
    greet((1 - gx, gy, grp))
    greet((gx, along_xy(1), grp))
    greet((gx, along_xy(ny - 1), grp))
    greet(sibling)
    for k in range(1, nz):
        if k != zl:
            greet(z_device(along_z(k)))

    @pl.loop(2, ny - 1)
    def _(k):
        greet((gx, along_xy(k), grp))

    @pl.loop(1, ny)
    def _(k):
        greet((gx, along_xy(k), grp + 1 - 2 * core))

    place = (gx, gy, grp)
    sided = (gy > 0, gy < ny - 1)
    far = (XE - 1) * (1 - gx)
    ends = (
        (send_xf, send_yf, send_cf, land_xf, land_yf, land_cf),
        (send_xc, send_yc, send_cc, land_xc, land_yc, land_cc),
    )
    corners = (corner_f, corner_c)
    halos = [
        halo_copies(ends[number], halo_send.at[number], halo_recv.at[number], place, ny)
        for number in range(2)
    ]

    def dispatch(number, ext):
        take_edges(ext, *ends[number][:3], corners[number], gx)
        if number == 0:
            pl.semaphore_wait(barrier, nz - 1 + 2 * (ny - 1) + 3)
        for copy in halos[number]:
            copy.start()

    def arrive_y(number, ext):
        for which in (3, 4):
            halos[number][which].wait_recv()
        insert_y(ext, ends[number][4], sided)

    def arrive_x(number, ext):
        for which in (0, 1, 2):
            halos[number][which].wait_recv()
        insert_x(ext, ends[number][3], ends[number][5], sided, far, corners[number])

    def load_own(ext, source):
        for x in range(X):
            for q in range(Q):
                ext[pl.ds(row(q, x + 1, 0), Y), :] = source[0, x, :, q * 128 : q * 128 + 128].astype(F32)

    clear_halo(ext_f, shifted)
    loads[0].wait()
    load_own(ext_f, field)
    dispatch(0, ext_f)
    clear_halo(ext_c, shifted_c)
    loads[1].wait()
    load_own(ext_c, cotangent)
    dispatch(1, ext_c)

    loads[2].wait()
    forward_weight(first, banded_1)
    conv_own(ext_f, wide, banded_1, shifted, False)
    columns[...] = jnp.zeros_like(columns)
    columns_c[...] = jnp.zeros_like(columns_c)
    loads[3].wait()
    backward_weight(second, banded_t)
    for q in range(Q):
        turn(turned_c, q, cotangent[0, :, :, q * 128 : q * 128 + 128].reshape(X * Y, 128))

    conv_own(ext_c, wide, banded_t, shifted_c, True)
    forward_weight(second, banded_2)
    clear_halo(ext_h, None)

    def activate(value):
        sigma = jax.nn.sigmoid(value)
        return (value * sigma).astype(BF16).astype(F32), sigma * (1.0 + value * (1.0 - sigma))

    arrive_y(0, ext_f)
    conv_y(ext_f, banded_1, columns, False)
    for p in range(Q):
        conv_sum(shifted, columns, pre, p)
        hidden, slope[p] = activate(pre[p])
        for x in range(X):
            ext_h[pl.ds(row(p, x + 1, 0), Y), :] = hidden[x * Y : x * Y + Y]
    arrive_y(1, ext_c)
    conv_y(ext_c, banded_t, columns_c, True)
    for p in range(Q):
        conv_sum(shifted_c, columns_c, sums_c, p)
    ring_y(ext_f, ext_h, banded_1, ring, ring_pre, sided)
    ring_near(ext_f, banded_1, near_part, gx)

    arrive_x(0, ext_f)
    ring_far(ext_f, ext_h, banded_1, near_part, edge_part, sided, gx, far)
    edge = (X - 1) * (1 - gx)
    edge_rows = pl.ds(pl.multiple_of(edge * Y, Y), Y)
    for p in range(Q):
        added = edge_part[p * SLOT + 8 : p * SLOT + 8 + Y, :]
        hidden, slope[p, edge_rows, :] = activate(pre[p, edge_rows, :] + added)
        ext_h[pl.ds(pl.multiple_of(row(p, edge + 1, 0), 8), Y), :] = hidden
    for side, y in ((0, -1), (1, Y)):
        added = edge_part[pl.ds(8 + y, Q, stride=SLOT), :]
        hidden = silu(ring_pre[side, pl.ds(pl.multiple_of(edge * Q, Q), Q), :] + added)
        ext_h[pl.ds(row(0, edge + 1, y), Q, stride=PLANES * SLOT), :] = jnp.where(
            sided[side], hidden, jnp.zeros_like(hidden)
        )

    owner = gy < owners

    def scatter(g):
        def finished(pair):
            for j in range(owners):
                if not pair * 192 < (j + 1) * chunk <= (pair + 1) * 192:
                    continue

                @pl.when(jnp.logical_or(gy != j, core != g))
                def _():
                    pltpu.make_async_remote_copy(
                        src_ref=packed.at[g, pl.ds(j * chunk, chunk)], dst_ref=gathered_xy.at[core * ny + gy],
                        send_sem=xy_send, recv_sem=xy_recv,
                        device_id=(gx, j, grp + g - core), device_id_type=MESH,
                    ).start()

        return finished

    kernel_grad(ext_h, turned_c, packed, 1, scatter(1))
    arrive_x(1, ext_c)
    add_plane(sums_c, conv_x(ext_c, thin, banded_t, True, gx, far), gx)
    for p in range(Q):
        turn(turned_p, p, (sums_c[p] * slope[p]).astype(BF16))

    kernel_grad(ext_f, turned_p, packed, 0, scatter(0))

    conv_own(ext_h, wide, banded_2, shifted, False)
    for p in range(Q):
        conv_sum(shifted, None, pre, p)
    add_plane(pre, conv_x(ext_h, thin, banded_2, False, gx, far), gx)
    for p in range(Q):
        output[0, :, :, p * 128 : p * 128 + 128] = pre[p].astype(BF16).reshape(X, Y, 128)

    def rows_of(j):
        return pl.ds(pl.multiple_of(j * chunk, 16), chunk)

    def several(count):
        part = gathered_xy.at[pl.ds(0, count)]
        return pltpu.make_async_remote_copy(
            src_ref=part, dst_ref=part, send_sem=xy_send, recv_sem=xy_recv,
            device_id=me, device_id_type=MESH,
        )

    @pl.when(owner)
    def _():
        several(2 * ny - 1).wait_recv()
        gathered_xy[core * ny + gy] = packed[core, rows_of(gy), :]
        total = gathered_xy[0].astype(F32)
        for k in range(1, 2 * ny):
            total = total + gathered_xy[k].astype(F32)
        gathered_z[z] = total.astype(BF16)
        for k in sorted(range(1, nz), key=lambda k: -min(k, nz - k)):
            pltpu.make_async_remote_copy(
                src_ref=gathered_z.at[z], dst_ref=gathered_z.at[z],
                send_sem=z_send, recv_sem=z_recv,
                device_id=z_device(along_z(k)), device_id_type=MESH,
            ).start()

    def share(j):
        pltpu.make_async_remote_copy(
            src_ref=full.at[core, rows_of(j)], dst_ref=full.at[core, rows_of(j)],
            send_sem=share_send, recv_sem=share_recv,
            device_id=sibling, device_id_type=MESH,
        ).start()

    by_distance = sorted(
        range(1, ny), key=lambda k: -(min(k // 4, 4 - k // 4) + min(k % 4, 4 - k % 4))
    )
    others = gathered_z.at[pl.ds(0, nz - 1)]
    z_all = pltpu.make_async_remote_copy(
        src_ref=others, dst_ref=others, send_sem=z_send, recv_sem=z_recv,
        device_id=me, device_id_type=MESH,
    )

    @pl.when(owner)
    def _():
        z_all.wait_recv()
        grand = gathered_z[0].astype(F32)
        for k in range(1, nz):
            grand = grand + gathered_z[k].astype(F32)
        rows = lax.broadcasted_iota(jnp.int32, (128, 128), 0)
        lanes = lax.broadcasted_iota(jnp.int32, (128, 128), 1)
        unit = (rows == lanes).astype(BF16)
        turned = []
        for start in range(0, chunk, C):
            block = lax.dot_general(
                unit, grand[start : start + C].astype(BF16), (((1,), (1,)), ((), ())),
                preferred_element_type=F32,
            )
            turned.append(jnp.concatenate([block[0:C], block[C : 2 * C]], axis=1))
        full[core, rows_of(gy), :] = jnp.concatenate(turned, axis=0).astype(BF16)

        for k in by_distance:
            pltpu.make_async_remote_copy(
                src_ref=full.at[core, rows_of(gy)], dst_ref=full.at[core, rows_of(gy)],
                send_sem=back_xy_send, recv_sem=back_xy_recv.at[k],
                device_id=(gx, along_xy(k), grp), device_id_type=MESH,
            ).start()

        share(gy)

    for k in reversed(by_distance):
        j = along_xy(ny - k)

        @pl.when(j < owners)
        def _(j=j, k=k):
            pltpu.make_async_remote_copy(
                src_ref=full.at[core, rows_of(j)], dst_ref=full.at[core, rows_of(j)],
                send_sem=back_xy_send, recv_sem=back_xy_recv.at[k],
                device_id=me, device_id_type=MESH,
            ).wait_recv()
            share(j)

    whole = pltpu.make_async_remote_copy(
        src_ref=full.at[core], dst_ref=full.at[1 - core], send_sem=share_send, recv_sem=share_recv,
        device_id=sibling, device_id_type=MESH,
    )
    whole.wait_recv()

    for number in range(2):
        for copy in halos[number]:
            copy.wait_send()

    @pl.when(owner)
    def _():
        several(2 * owners - 1).wait_send()
        z_all.wait_send()
        part = gathered_xy.at[pl.ds(0, ny - 1)]
        pltpu.make_async_remote_copy(
            src_ref=part, dst_ref=part, send_sem=back_xy_send, recv_sem=share_recv,
            device_id=me, device_id_type=MESH,
        ).wait_send()

    if owners < ny:

        @pl.when(jnp.logical_not(owner))
        def _():
            several(2 * owners).wait_send()

    whole.wait_send()


def unpack(factor, output_in, full, output, first_out, second_out, one, two, sems):
    copies = [
        pltpu.make_async_copy(source, target, sems.at[number])
        for number, (source, target) in enumerate(
            ((output_in, output), (one, first_out), (two, second_out))
        )
    ]
    copies[0].start()
    for g, target in ((0, one), (1, two)):
        for pair in range(PAIRS):
            for v in range(3):
                start = (pair * 3 + v) * C
                block = full[g, start : start + C, :].astype(F32) * factor
                target[2 * pair * 3 + 2 - v] = block[:, 0:C]
                if 2 * pair + 1 < 9:
                    target[(2 * pair + 1) * 3 + 2 - v] = block[:, C : 2 * C]
        copies[g + 1].start()
    for copy in copies:
        copy.wait()


def halo_buffers(deep):
    ends = [
        pltpu.VMEM((deep, Y, 1024), BF16),
        pltpu.VMEM((2, deep, X, 1024), BF16),
        pltpu.VMEM((2, deep * deep, Q, 128), BF16),
    ]
    return ends + ends + [pltpu.VMEM((2, deep * deep, Q, 128), F32)]


def shards(sizes, field_in, first_weight, second_weight, cotangent):
    nx, ny, ng = sizes
    nz = nx * ng // 2
    chunk = C * pl.cdiv(PACKED, C * ny)
    assert PACKED % chunk == 0
    rows = PACKED
    total = ng * nx * X * ny * Y * NZ
    dma = pltpu.SemaphoreType.DMA
    vmem = pltpu.VMEM
    inside = pl.BlockSpec(memory_space=pltpu.VMEM)
    outside = pl.BlockSpec(memory_space=pltpu.HBM)
    cells = (Q * PLANES * SLOT + 2 * MARGIN, 128)
    sums = (Q, ROWS_E, 384)
    weight = (27, C, C)
    output, full = pl.pallas_call(
        functools.partial(step, sizes),
        out_shape=(
            jax.ShapeDtypeStruct(field_in.shape, BF16),
            jax.ShapeDtypeStruct((2, rows, 128), BF16),
        ),
        in_specs=[outside] * 4,
        out_specs=(inside,) * 2,
        scratch_shapes=[
            vmem(field_in.shape, BF16), vmem(weight, BF16), vmem(weight, BF16), vmem(field_in.shape, BF16),
            dma((4,)), vmem(sums, F32), vmem(sums, F32),
            vmem(cells, F32), vmem(cells, F32), vmem(cells, F32),
            vmem((Q, X * Y, 768), BF16), vmem((Q * Y, 768), BF16), vmem((2, Q, 24, 384), F32), vmem((2, Q, 24, 384), F32),
            vmem((Q, X * Y, 128), F32), vmem((Q, X * Y, 128), F32),
            vmem((768, 384), BF16), vmem((768, 384), BF16), vmem((384, 768), BF16),
            vmem((256, Q * 128), BF16), vmem((256, Q * 128), BF16),
            vmem((Q, X * Y, 128), F32),
            *halo_buffers(2), *halo_buffers(1), vmem((Q * PLANES, 384), F32),
            vmem((2, X * Q, 128), F32), vmem((Q * SLOT, 128), F32), vmem((Q * SLOT, 128), F32),
            vmem((2, rows, 128), BF16), vmem((2 * ny, chunk, 128), BF16), vmem((nz, chunk, 128), BF16),
            dma((2, 5)), dma((2, 5)), dma, dma, dma, dma,
            dma, dma((ny,)), dma, dma,
        ],
        compiler_params=pltpu.CompilerParams(
            collective_id=0, has_side_effects=True, vmem_limit_bytes=40 * 1024 * 1024
        ),
    )(
        *(
            pltpu.with_memory_space_constraint(array, pltpu.HBM)
            for array in (
                field_in,
                first_weight.reshape(weight),
                second_weight.reshape(weight),
                cotangent,
            )
        )
    )
    output, first_grad, second_grad = pl.pallas_call(
        functools.partial(unpack, 1.0 / math.sqrt(total)),
        out_shape=(
            jax.ShapeDtypeStruct(field_in.shape, BF16),
            jax.ShapeDtypeStruct(weight, F32),
            jax.ShapeDtypeStruct(weight, F32),
        ),
        in_specs=[inside] * 2,
        out_specs=(outside,) * 3,
        scratch_shapes=[vmem(weight, F32), vmem(weight, F32), dma((3,))],
        compiler_params=pltpu.CompilerParams(vmem_limit_bytes=16 * 1024 * 1024),
    )(output, full)
    shape = (3, 3, 3, C, C)
    return output, first_grad.reshape(shape), second_grad.reshape(shape)


def solution(mesh):
    sizes = (mesh.shape["gx"], mesh.shape["gy"], mesh.shape["grp"])
    return jax.shard_map(
        functools.partial(shards, sizes),
        mesh=mesh,
        in_specs=(P("grp", "gx", "gy", None), P(), P(), P("grp", "gx", "gy", None)),
        out_specs=(P("grp", "gx", "gy", None), P(), P()),
        check_vma=False,
    )
```

```python
import functools
import math

import jax
import jax.numpy as jnp
from jax import lax
from jax.experimental import pallas as pl
from jax.experimental.pallas import tpu as pltpu
from jax.sharding import PartitionSpec as P

C = 64
NZ = 16
X = 8
Y = 16
Q = 8
XE = X + 2
PLANES = 16
FAR = 10
SLOT = 32
MARGIN = 8
ROWS_E = XE * Y
PAIRS = 5
PACKED = PAIRS * 192
F32 = jnp.float32
BF16 = jnp.bfloat16
MESH = pl.DeviceIdType.MESH


def low_lanes(rows):
    return lax.broadcasted_iota(jnp.int32, (rows, 128), 1) < 64


def row(q, x, y):
    return (q * PLANES + x) * SLOT + MARGIN + 8 + y


def clear_halo(ext, shifted):
    edge = jnp.zeros((8, 128), F32)
    plane = jnp.zeros((SLOT, 128), F32)
    for q in range(Q):
        for x in range(XE):
            if x in (0, XE - 1):
                ext[pl.ds(row(q, x, -8), SLOT), :] = plane
            else:
                ext[pl.ds(row(q, x, -8), 8), :] = edge
                ext[pl.ds(row(q, x, Y), 8), :] = edge
        if shifted is not None:
            shifted[q, 0:Y, :] = jnp.zeros((Y, 384), F32)
            shifted[q, ROWS_E - Y : ROWS_E, :] = jnp.zeros((Y, 384), F32)


def take_edges(ext, send_x, send_y, send_c, corner, gx):
    deep = send_x.shape[0]
    for q in range(Q):
        columns = slice(q * 128, q * 128 + 128)
        for d in range(deep):
            near = (X - d) - (X - 1 - 2 * d) * gx
            plane = ext[pl.ds(pl.multiple_of(row(q, near, 0), 8), Y), :]
            send_x[d, :, columns] = plane.astype(BF16)
            for e in range(deep):
                corner[0, d * deep + e, q : q + 1, :] = plane[e : e + 1]
                corner[1, d * deep + e, q : q + 1, :] = plane[Y - 1 - e : Y - e]
        for e in range(deep):
            for side, y in ((0, e), (1, Y - 1 - e)):
                send_y[side, e, :, columns] = ext[pl.ds(row(q, 1, y), X, stride=SLOT), :].astype(BF16)
    send_c[...] = corner[...].astype(BF16)


def halo_copies(ends, send_sems, recv_sems, place, count):
    send_x, send_y, send_c, land_x, land_y, land_c = ends
    gx, gy, grp = place
    up = lax.rem(gy + 1, count)
    down = lax.rem(gy + count - 1, count)
    moves = (
        (send_c.at[1], land_c.at[0], (1 - gx, up, grp)),
        (send_c.at[0], land_c.at[1], (1 - gx, down, grp)),
        (send_x, land_x, (1 - gx, gy, grp)),
        (send_y.at[1], land_y.at[0], (gx, up, grp)),
        (send_y.at[0], land_y.at[1], (gx, down, grp)),
    )
    return [
        pltpu.make_async_remote_copy(
            src_ref=source, dst_ref=target, send_sem=send_sems.at[number], recv_sem=recv_sems.at[number],
            device_id=device, device_id_type=MESH,
        )
        for number, (source, target, device) in enumerate(moves)
    ]


def insert_y(ext, land_y, sided):
    for e in range(land_y.shape[1]):
        for side, y in ((0, -1 - e), (1, Y + e)):
            for q in range(Q):
                value = land_y[side, e, :, q * 128 : q * 128 + 128].astype(F32)
                value = jnp.where(sided[side], value, jnp.zeros_like(value))
                ext[pl.ds(row(q, 1, y), X, stride=SLOT), :] = value


def insert_x(ext, land_x, land_c, sided, far, corner):
    deep = land_x.shape[0]
    corner[...] = land_c[...].astype(F32)
    rows = lax.broadcasted_iota(jnp.int32, (8, 128), 0)
    for d in range(deep):
        plane = far if d == 0 else FAR
        for q in range(Q):
            start = pl.multiple_of(row(q, plane, 0), 8)
            ext[pl.ds(start, Y), :] = land_x[d, :, q * 128 : q * 128 + 128].astype(F32)
            low = jnp.zeros((8, 128), F32)
            high = jnp.zeros((8, 128), F32)
            for e in range(deep):
                cell = d * deep + e
                low = jnp.where((rows == 7 - e) & sided[0], corner[0, cell, q : q + 1, :], low)
                high = jnp.where((rows == e) & sided[1], corner[1, cell, q : q + 1, :], high)
            ext[pl.ds(start - 8, 8), :] = low
            ext[pl.ds(start + Y, 8), :] = high


def operand(values, low):
    zero = jnp.zeros_like(values[0])
    padded = [zero] + values + [zero]
    return [
        (padded[q + 1].astype(BF16), jnp.where(low, padded[q + 2], padded[q]).astype(BF16))
        for q in range(Q)
    ]


def conv_own(ext, wide, banded, shifted, flipped):
    low = low_lanes(Y)
    for x in range(X):
        for dy in range(3):
            values = [ext[pl.ds(row(q, x + 1, dy - 1), Y), :] for q in range(Q)]
            for q, (own, mixed) in enumerate(operand(values, low)):
                wide[q, x * Y : x * Y + Y, dy * 256 : dy * 256 + 128] = own
                wide[q, x * Y : x * Y + Y, dy * 256 + 128 : dy * 256 + 256] = mixed
    dims = (((1,), (1 if flipped else 0,)), ((), ()))
    result = lax.dot_general(
        wide[...].reshape(Q * X * Y, 768), banded[...], dims, preferred_element_type=F32
    )
    shifted[:, Y : Y + X * Y, :] = result.reshape(Q, X * Y, 384)


def conv_y(ext, banded, columns, flipped):
    low = low_lanes(X)
    for side, y, dy in ((0, -1, 0), (1, Y, 2)):
        values = [ext[pl.ds(row(q, 1, y), X, stride=SLOT), :] for q in range(Q)]
        padded = [jnp.zeros((X, 128), F32)] + values + [jnp.zeros((X, 128), F32)]
        own = jnp.concatenate(values, axis=0)
        mixed = jnp.concatenate([jnp.where(low, padded[q + 2], padded[q]) for q in range(Q)], axis=0)
        rows = jnp.concatenate([own, mixed], axis=1).astype(BF16)
        if flipped:
            weight = banded[:, dy * 256 : dy * 256 + 256]
        else:
            weight = banded[dy * 256 : dy * 256 + 256, :]
        dims = (((1,), (1 if flipped else 0,)), ((), ()))
        result = lax.dot_general(rows, weight, dims, preferred_element_type=F32)
        for q in range(Q):
            columns[side, q, 8:16, :] = result[q * X : q * X + X]


def conv_x(ext, thin, banded, flipped, gx, far):
    low = low_lanes(Y)
    for dy in range(3):
        values = [
            ext[pl.ds(pl.multiple_of(row(q, far, 0), 8) + dy - 1, Y), :] for q in range(Q)
        ]
        for q, (own, mixed) in enumerate(operand(values, low)):
            thin[q * Y : q * Y + Y, dy * 256 : dy * 256 + 128] = own
            thin[q * Y : q * Y + Y, dy * 256 + 128 : dy * 256 + 256] = mixed
    tap = pl.ds(pl.multiple_of((1 - gx) * 256, 128), 128)
    weight = banded[tap, :] if flipped else banded[:, tap]
    dims = (((1,), (1 if flipped else 0,)), ((), ()))
    return lax.dot_general(thin[...], weight, dims, preferred_element_type=F32)


def add_plane(sums, added, gx):
    edge = pl.ds(pl.multiple_of((X - 1) * (1 - gx) * Y, Y), Y)
    for q in range(Q):
        sums[q, edge, :] = sums[q, edge, :] + added[q * Y : q * Y + Y]


def silu(value):
    return (value * jax.nn.sigmoid(value)).astype(BF16).astype(F32)


def lanes_of(values, low):
    padded = [jnp.zeros_like(values[0])] + values + [jnp.zeros_like(values[0])]
    own = jnp.concatenate(values, axis=0)
    mixed = jnp.concatenate([jnp.where(low, padded[q + 2], padded[q]) for q in range(Q)], axis=0)
    return [own.astype(BF16), mixed.astype(BF16)]


def slot_operand(ext, plane):
    low = low_lanes(SLOT)
    parts = []
    for dy in range(3):
        starts = [pl.multiple_of(row(q, plane, -8), 8) + dy - 1 for q in range(Q)]
        parts += lanes_of([ext[pl.ds(start, SLOT), :] for start in starts], low)
    return jnp.concatenate(parts, axis=1)


def ring_near(ext, banded, near_part, gx):
    tap = pl.ds(pl.multiple_of(256 * gx, 128), 128)
    near_part[...] = jnp.dot(
        slot_operand(ext, X - (X - 1) * gx), banded[:, tap], preferred_element_type=F32
    )


def ring_far(ext, hidden_ext, banded, near_part, edge_part, sided, gx, far):
    tap = pl.ds(pl.multiple_of((1 - gx) * 256, 128), 128)
    both = jnp.concatenate([banded[:, tap], banded[:, 128:256]], axis=1)
    result = jnp.dot(slot_operand(ext, far), both, preferred_element_type=F32)
    edge_part[...] = result[:, 0:128]
    total = near_part[...] + result[:, 128:256]
    total = total + jnp.dot(slot_operand(ext, FAR), banded[:, tap], preferred_element_type=F32)
    hidden = silu(total)
    y = lax.broadcasted_iota(jnp.int32, (SLOT, 128), 0) - 8
    inside = ((y >= 0) & (y < Y)) | ((y == -1) & sided[0]) | ((y == Y) & sided[1])
    for q in range(Q):
        part = hidden[q * SLOT : q * SLOT + SLOT]
        hidden_ext[pl.ds(pl.multiple_of(row(q, far, -8), 8), SLOT), :] = jnp.where(inside, part, jnp.zeros_like(part))


def ring_y(ext, hidden_ext, banded, ring, ring_pre, sided):
    low = low_lanes(PLANES)
    for side, y in ((0, -1), (1, Y)):
        parts = []
        for dy in range(3):
            parts += lanes_of(
                [ext[pl.ds(row(q, 0, y + dy - 1), PLANES, stride=SLOT), :] for q in range(Q)], low
            )
        ring[...] = jnp.dot(jnp.concatenate(parts, axis=1), banded[...], preferred_element_type=F32)
        for q in range(Q):
            start = q * PLANES
            total = (
                ring[start : start + X, 0:128]
                + ring[start + 1 : start + 1 + X, 128:256]
                + ring[start + 2 : start + 2 + X, 256:384]
            )
            ring_pre[side, pl.ds(q, X, stride=Q), :] = total
            hidden = silu(total)
            hidden_ext[pl.ds(row(q, 1, y), X, stride=SLOT), :] = jnp.where(
                sided[side], hidden, jnp.zeros_like(hidden)
            )


def plane_sum(shifted, p):
    n = X * Y
    return (
        shifted[p, 0:n, 0:128]
        + shifted[p, Y : Y + n, 128:256]
        + shifted[p, 2 * Y : 2 * Y + n, 256:384]
    )


def conv_sum(shifted, columns, sums, p):
    sums[p] = plane_sum(shifted, p)
    if columns is None:
        return
    for side, y in ((0, 0), (1, Y - 1)):
        extra = (
            columns[side, p, 7:15, 0:128]
            + columns[side, p, 8:16, 128:256]
            + columns[side, p, 9:17, 256:384]
        )
        place = pl.ds(y, X, stride=Y)
        sums[p, place, :] = sums[p, place, :] + extra


TAPS = ((1, 0), (2, 1), (None, 2), (0, None))


def piece(weight, tap):
    return jnp.zeros((C, C), BF16) if tap is None else weight[tap]


def forward_weight(weight, banded):
    for dy in range(3):
        for slot in range(4):
            rows = slice(dy * 256 + slot * C, dy * 256 + slot * C + C)
            for dx in range(3):
                pieces = [
                    piece(weight, None if t is None else (dx * 3 + dy) * 3 + t) for t in TAPS[slot]
                ]
                banded[rows, dx * 128 : dx * 128 + 128] = jnp.concatenate(pieces, axis=1)


def backward_weight(weight, banded):
    for dx in range(3):
        for b in range(2):
            rows = slice(dx * 128 + b * C, dx * 128 + b * C + C)
            for dy in range(3):
                for half in range(2):
                    pieces = []
                    for slot in (2 * half, 2 * half + 1):
                        t = TAPS[slot][b]
                        tap = None if t is None else ((2 - dx) * 3 + 2 - dy) * 3 + 2 - t
                        pieces.append(piece(weight, tap))
                    start = dy * 256 + half * 128
                    banded[rows, start : start + 128] = jnp.concatenate(pieces, axis=1)


def kernel_grad(ext, turned, packed, g, finished):
    low = low_lanes(192)
    turned_value = turned[...]

    def moving(tap):
        dx, dy = tap // 3, tap % 3
        blocks = [
            ext[pl.ds(row(q, x + dx, dy - 1), Y), :].astype(BF16) for q in range(Q) for x in range(X)
        ]
        return jnp.concatenate(blocks, axis=0)

    for pair in range(PAIRS):
        first = 2 * pair
        if first + 1 < 9:
            rhs = jnp.concatenate([moving(first), moving(first + 1)], axis=1)
        else:
            rhs = moving(first)
        result = jnp.dot(turned_value, rhs, preferred_element_type=F32)
        one = result[:, 0:128]
        two = result[:, 128:256] if first + 1 < 9 else jnp.zeros_like(one)
        straight = jnp.where(low, one[0:192], two[64:256])
        crossed = jnp.where(low, two[0:192], one[64:256])
        total = straight + pltpu.roll(crossed, 64, 1)
        packed[g, pair * 192 : pair * 192 + 192, :] = total.astype(BF16)
        finished(pair)


def turn(turned, q, block):
    flat = block.astype(F32).T.astype(BF16)
    columns = lambda w: slice(w * 128, w * 128 + 128)
    turned[64:192, columns(q)] = flat
    if q + 1 < Q:
        turned[0:64, columns(q + 1)] = flat[64:128]
    else:
        turned[192:256, columns(q)] = jnp.zeros((64, 128), BF16)
    if q > 0:
        turned[192:256, columns(q - 1)] = flat[0:64]
    else:
        turned[0:64, columns(q)] = jnp.zeros((64, 128), BF16)


def step(
    sizes,
    field_hbm, first_hbm, second_hbm, cotangent_hbm,
    output, full,
    field, first, second, cotangent, load_sems, shifted, shifted_c,
    ext_f, ext_c, ext_h, wide, thin, columns, columns_c, pre, sums_c,
    banded_1, banded_2, banded_t, turned_c, turned_p, slope,
    send_xf, send_yf, send_cf, land_xf, land_yf, land_cf, corner_f,
    send_xc, send_yc, send_cc, land_xc, land_yc, land_cc, corner_c, ring,
    ring_pre, near_part, edge_part,
    packed, gathered_xy, gathered_z,
    halo_send, halo_recv, xy_send, xy_recv, z_send, z_recv,
    back_xy_send, back_xy_recv, share_send, share_recv,
):
    nx, ny, ng = sizes
    zl = ng // 2
    nz = nx * zl
    chunk = gathered_xy.shape[1]
    owners = PACKED // chunk
    loads = [
        pltpu.make_async_copy(source, target, load_sems.at[number])
        for number, (source, target) in enumerate(
            ((field_hbm, field), (cotangent_hbm, cotangent), (first_hbm, first), (second_hbm, second))
        )
    ]
    for load in loads:
        load.start()
    gx, gy, grp = lax.axis_index("gx"), lax.axis_index("gy"), lax.axis_index("grp")
    core = lax.rem(grp, 2)
    z = gx * zl + grp // 2
    me = (gx, gy, grp)
    sibling = (gx, gy, grp + 1 - 2 * core)

    def along_xy(k):
        return lax.rem(gy + k, ny)

    def along_z(k):
        return lax.rem(z + k, nz)

    def z_device(target):
        return (target // zl, gy, 2 * lax.rem(target, zl) + core)

    barrier = pltpu.get_barrier_semaphore()

    def greet(device):
        pl.semaphore_signal(barrier, inc=1, device_id=device, device_id_type=MESH)

    greet((1 - gx, along_xy(1), grp))
    greet((1 - gx, along_xy(ny - 1), grp))
    greet((1 - gx, gy, grp))
    greet((gx, along_xy(1), grp))
    greet((gx, along_xy(ny - 1), grp))
    greet(sibling)
    for k in range(1, nz):
        if k != zl:
            greet(z_device(along_z(k)))

    for k in range(2, ny - 1):
        greet((gx, along_xy(k), grp))
    for k in range(1, ny):
        greet((gx, along_xy(k), grp + 1 - 2 * core))

    place = (gx, gy, grp)
    sided = (gy > 0, gy < ny - 1)
    far = (XE - 1) * (1 - gx)
    ends = (
        (send_xf, send_yf, send_cf, land_xf, land_yf, land_cf),
        (send_xc, send_yc, send_cc, land_xc, land_yc, land_cc),
    )
    corners = (corner_f, corner_c)
    halos = [
        halo_copies(ends[number], halo_send.at[number], halo_recv.at[number], place, ny)
        for number in range(2)
    ]

    def dispatch(number, ext):
        take_edges(ext, *ends[number][:3], corners[number], gx)
        if number == 0:
            pl.semaphore_wait(barrier, nz - 1 + 2 * (ny - 1) + 3)
        for copy in halos[number]:
            copy.start()

    def arrive_y(number, ext):
        for which in (3, 4):
            halos[number][which].wait_recv()
        insert_y(ext, ends[number][4], sided)

    def arrive_x(number, ext):
        for which in (0, 1, 2):
            halos[number][which].wait_recv()
        insert_x(ext, ends[number][3], ends[number][5], sided, far, corners[number])

    def load_own(ext, source):
        for x in range(X):
            for q in range(Q):
                ext[pl.ds(row(q, x + 1, 0), Y), :] = source[0, x, :, q * 128 : q * 128 + 128].astype(F32)

    clear_halo(ext_f, shifted)
    loads[0].wait()
    load_own(ext_f, field)
    dispatch(0, ext_f)
    clear_halo(ext_c, shifted_c)
    loads[1].wait()
    load_own(ext_c, cotangent)
    dispatch(1, ext_c)

    loads[2].wait()
    forward_weight(first, banded_1)
    conv_own(ext_f, wide, banded_1, shifted, False)
    columns[...] = jnp.zeros_like(columns)
    columns_c[...] = jnp.zeros_like(columns_c)
    loads[3].wait()
    backward_weight(second, banded_t)
    for q in range(Q):
        turn(turned_c, q, cotangent[0, :, :, q * 128 : q * 128 + 128].reshape(X * Y, 128))

    conv_own(ext_c, wide, banded_t, shifted_c, True)
    forward_weight(second, banded_2)
    clear_halo(ext_h, None)

    def activate(value):
        sigma = jax.nn.sigmoid(value)
        return (value * sigma).astype(BF16).astype(F32), sigma * (1.0 + value * (1.0 - sigma))

    arrive_y(0, ext_f)
    conv_y(ext_f, banded_1, columns, False)
    for p in range(Q):
        conv_sum(shifted, columns, pre, p)
        hidden, slope[p] = activate(pre[p])
        for x in range(X):
            ext_h[pl.ds(row(p, x + 1, 0), Y), :] = hidden[x * Y : x * Y + Y]
    arrive_y(1, ext_c)
    conv_y(ext_c, banded_t, columns_c, True)
    for p in range(Q):
        conv_sum(shifted_c, columns_c, sums_c, p)
    ring_y(ext_f, ext_h, banded_1, ring, ring_pre, sided)
    ring_near(ext_f, banded_1, near_part, gx)

    arrive_x(0, ext_f)
    ring_far(ext_f, ext_h, banded_1, near_part, edge_part, sided, gx, far)
    edge = (X - 1) * (1 - gx)
    edge_rows = pl.ds(pl.multiple_of(edge * Y, Y), Y)
    for p in range(Q):
        added = edge_part[p * SLOT + 8 : p * SLOT + 8 + Y, :]
        hidden, slope[p, edge_rows, :] = activate(pre[p, edge_rows, :] + added)
        ext_h[pl.ds(pl.multiple_of(row(p, edge + 1, 0), 8), Y), :] = hidden
    for side, y in ((0, -1), (1, Y)):
        added = edge_part[pl.ds(8 + y, Q, stride=SLOT), :]
        hidden = silu(ring_pre[side, pl.ds(pl.multiple_of(edge * Q, Q), Q), :] + added)
        ext_h[pl.ds(row(0, edge + 1, y), Q, stride=PLANES * SLOT), :] = jnp.where(
            sided[side], hidden, jnp.zeros_like(hidden)
        )

    owner = gy < owners

    def scatter(g):
        def finished(pair):
            for j in range(owners):
                if not pair * 192 < (j + 1) * chunk <= (pair + 1) * 192:
                    continue

                @pl.when(jnp.logical_or(gy != j, core != g))
                def _():
                    pltpu.make_async_remote_copy(
                        src_ref=packed.at[g, pl.ds(j * chunk, chunk)], dst_ref=gathered_xy.at[core * ny + gy],
                        send_sem=xy_send, recv_sem=xy_recv,
                        device_id=(gx, j, grp + g - core), device_id_type=MESH,
                    ).start()

        return finished

    kernel_grad(ext_h, turned_c, packed, 1, scatter(1))
    arrive_x(1, ext_c)
    add_plane(sums_c, conv_x(ext_c, thin, banded_t, True, gx, far), gx)
    for p in range(Q):
        turn(turned_p, p, (sums_c[p] * slope[p]).astype(BF16))

    kernel_grad(ext_f, turned_p, packed, 0, scatter(0))

    conv_own(ext_h, wide, banded_2, shifted, False)
    for p in range(Q):
        conv_sum(shifted, None, pre, p)
    add_plane(pre, conv_x(ext_h, thin, banded_2, False, gx, far), gx)
    for p in range(Q):
        output[0, :, :, p * 128 : p * 128 + 128] = pre[p].astype(BF16).reshape(X, Y, 128)

    def rows_of(j):
        return pl.ds(pl.multiple_of(j * chunk, 16), chunk)

    def several(count):
        part = gathered_xy.at[pl.ds(0, count)]
        return pltpu.make_async_remote_copy(
            src_ref=part, dst_ref=part, send_sem=xy_send, recv_sem=xy_recv,
            device_id=me, device_id_type=MESH,
        )

    @pl.when(owner)
    def _():
        several(2 * ny - 1).wait_recv()
        gathered_xy[core * ny + gy] = packed[core, rows_of(gy), :]
        total = gathered_xy[0].astype(F32)
        for k in range(1, 2 * ny):
            total = total + gathered_xy[k].astype(F32)
        gathered_z[z] = total.astype(BF16)
        for k in sorted(range(1, nz), key=lambda k: -min(k, nz - k)):
            pltpu.make_async_remote_copy(
                src_ref=gathered_z.at[z], dst_ref=gathered_z.at[z],
                send_sem=z_send, recv_sem=z_recv,
                device_id=z_device(along_z(k)), device_id_type=MESH,
            ).start()

    def share(j):
        pltpu.make_async_remote_copy(
            src_ref=full.at[core, rows_of(j)], dst_ref=full.at[core, rows_of(j)],
            send_sem=share_send, recv_sem=share_recv,
            device_id=sibling, device_id_type=MESH,
        ).start()

    by_distance = sorted(
        range(1, ny), key=lambda k: -(min(k // 4, 4 - k // 4) + min(k % 4, 4 - k % 4))
    )
    others = gathered_z.at[pl.ds(0, nz - 1)]
    z_all = pltpu.make_async_remote_copy(
        src_ref=others, dst_ref=others, send_sem=z_send, recv_sem=z_recv,
        device_id=me, device_id_type=MESH,
    )

    @pl.when(owner)
    def _():
        z_all.wait_recv()
        grand = gathered_z[0].astype(F32)
        for k in range(1, nz):
            grand = grand + gathered_z[k].astype(F32)
        rows = lax.broadcasted_iota(jnp.int32, (128, 128), 0)
        lanes = lax.broadcasted_iota(jnp.int32, (128, 128), 1)
        unit = (rows == lanes).astype(BF16)
        turned = []
        for start in range(0, chunk, C):
            block = lax.dot_general(
                unit, grand[start : start + C].astype(BF16), (((1,), (1,)), ((), ())),
                preferred_element_type=F32,
            )
            turned.append(jnp.concatenate([block[0:C], block[C : 2 * C]], axis=1))
        full[core, rows_of(gy), :] = jnp.concatenate(turned, axis=0).astype(BF16)

        for k in by_distance:
            pltpu.make_async_remote_copy(
                src_ref=full.at[core, rows_of(gy)], dst_ref=full.at[core, rows_of(gy)],
                send_sem=back_xy_send, recv_sem=back_xy_recv.at[k],
                device_id=(gx, along_xy(k), grp), device_id_type=MESH,
            ).start()

        share(gy)

    for k in reversed(by_distance):
        j = along_xy(ny - k)

        @pl.when(j < owners)
        def _(j=j, k=k):
            pltpu.make_async_remote_copy(
                src_ref=full.at[core, rows_of(j)], dst_ref=full.at[core, rows_of(j)],
                send_sem=back_xy_send, recv_sem=back_xy_recv.at[k],
                device_id=me, device_id_type=MESH,
            ).wait_recv()
            share(j)

    whole = pltpu.make_async_remote_copy(
        src_ref=full.at[core], dst_ref=full.at[1 - core], send_sem=share_send, recv_sem=share_recv,
        device_id=sibling, device_id_type=MESH,
    )
    whole.wait_recv()

    for number in range(2):
        for copy in halos[number]:
            copy.wait_send()

    @pl.when(owner)
    def _():
        several(2 * owners - 1).wait_send()
        z_all.wait_send()
        part = gathered_xy.at[pl.ds(0, ny - 1)]
        pltpu.make_async_remote_copy(
            src_ref=part, dst_ref=part, send_sem=back_xy_send, recv_sem=share_recv,
            device_id=me, device_id_type=MESH,
        ).wait_send()

    if owners < ny:

        @pl.when(jnp.logical_not(owner))
        def _():
            several(2 * owners).wait_send()

    whole.wait_send()


def unpack(factor, output_in, full, output, first_out, second_out, one, two, sems):
    copies = [
        pltpu.make_async_copy(source, target, sems.at[number])
        for number, (source, target) in enumerate(
            ((output_in, output), (one, first_out), (two, second_out))
        )
    ]
    copies[0].start()
    for g, target in ((0, one), (1, two)):
        for pair in range(PAIRS):
            for v in range(3):
                start = (pair * 3 + v) * C
                block = full[g, start : start + C, :].astype(F32) * factor
                target[2 * pair * 3 + 2 - v] = block[:, 0:C]
                if 2 * pair + 1 < 9:
                    target[(2 * pair + 1) * 3 + 2 - v] = block[:, C : 2 * C]
        copies[g + 1].start()
    for copy in copies:
        copy.wait()


def halo_buffers(deep):
    ends = [
        pltpu.VMEM((deep, Y, 1024), BF16),
        pltpu.VMEM((2, deep, X, 1024), BF16),
        pltpu.VMEM((2, deep * deep, Q, 128), BF16),
    ]
    return ends + ends + [pltpu.VMEM((2, deep * deep, Q, 128), F32)]


def shards(sizes, field_in, first_weight, second_weight, cotangent):
    nx, ny, ng = sizes
    nz = nx * ng // 2
    chunk = C * pl.cdiv(PACKED, C * ny)
    assert PACKED % chunk == 0
    rows = PACKED
    total = ng * nx * X * ny * Y * NZ
    dma = pltpu.SemaphoreType.DMA
    vmem = pltpu.VMEM
    inside = pl.BlockSpec(memory_space=pltpu.VMEM)
    outside = pl.BlockSpec(memory_space=pltpu.HBM)
    cells = (Q * PLANES * SLOT + 2 * MARGIN, 128)
    sums = (Q, ROWS_E, 384)
    weight = (27, C, C)
    output, full = pl.pallas_call(
        functools.partial(step, sizes),
        out_shape=(
            jax.ShapeDtypeStruct(field_in.shape, BF16),
            jax.ShapeDtypeStruct((2, rows, 128), BF16),
        ),
        in_specs=[outside] * 4,
        out_specs=(inside,) * 2,
        scratch_shapes=[
            vmem(field_in.shape, BF16), vmem(weight, BF16), vmem(weight, BF16), vmem(field_in.shape, BF16),
            dma((4,)), vmem(sums, F32), vmem(sums, F32),
            vmem(cells, F32), vmem(cells, F32), vmem(cells, F32),
            vmem((Q, X * Y, 768), BF16), vmem((Q * Y, 768), BF16), vmem((2, Q, 24, 384), F32), vmem((2, Q, 24, 384), F32),
            vmem((Q, X * Y, 128), F32), vmem((Q, X * Y, 128), F32),
            vmem((768, 384), BF16), vmem((768, 384), BF16), vmem((384, 768), BF16),
            vmem((256, Q * 128), BF16), vmem((256, Q * 128), BF16),
            vmem((Q, X * Y, 128), F32),
            *halo_buffers(2), *halo_buffers(1), vmem((Q * PLANES, 384), F32),
            vmem((2, X * Q, 128), F32), vmem((Q * SLOT, 128), F32), vmem((Q * SLOT, 128), F32),
            vmem((2, rows, 128), BF16), vmem((2 * ny, chunk, 128), BF16), vmem((nz, chunk, 128), BF16),
            dma((2, 5)), dma((2, 5)), dma, dma, dma, dma,
            dma, dma((ny,)), dma, dma,
        ],
        compiler_params=pltpu.CompilerParams(
            collective_id=0, has_side_effects=True, vmem_limit_bytes=40 * 1024 * 1024
        ),
    )(
        *(
            pltpu.with_memory_space_constraint(array, pltpu.HBM)
            for array in (
                field_in,
                first_weight.reshape(weight),
                second_weight.reshape(weight),
                cotangent,
            )
        )
    )
    output, first_grad, second_grad = pl.pallas_call(
        functools.partial(unpack, 1.0 / math.sqrt(total)),
        out_shape=(
            jax.ShapeDtypeStruct(field_in.shape, BF16),
            jax.ShapeDtypeStruct(weight, F32),
            jax.ShapeDtypeStruct(weight, F32),
        ),
        in_specs=[inside] * 2,
        out_specs=(outside,) * 3,
        scratch_shapes=[vmem(weight, F32), vmem(weight, F32), dma((3,))],
        compiler_params=pltpu.CompilerParams(vmem_limit_bytes=16 * 1024 * 1024),
    )(output, full)
    shape = (3, 3, 3, C, C)
    return output, first_grad.reshape(shape), second_grad.reshape(shape)


def solution(mesh):
    sizes = (mesh.shape["gx"], mesh.shape["gy"], mesh.shape["grp"])
    return jax.shard_map(
        functools.partial(shards, sizes),
        mesh=mesh,
        in_specs=(P("grp", "gx", "gy", None), P(), P(), P("grp", "gx", "gy", None)),
        out_specs=(P("grp", "gx", "gy", None), P(), P()),
        check_vma=False,
    )
```
